32 devices in a mesh: dp: 4 (over x, core), tensor: 8 (over z, y).
Axes of the slice: x: 2, y: 2, z: 4, core: 2. Of those that a mesh axis runs over, the one named last changes fastest.
Arguments:
- block_input: bfloat16 [6144, 2048], P(('dp', 'tensor')), may hold values from -6 to 6
- norm_gain: bfloat16 [2048], P('dp'), may hold values from 0.5 to 1.5
- in_weight: bfloat16 [2, 2048, 4096], P(None, 'dp', 'tensor'), may hold values from -0.125 to 0.125
- conv_weight: bfloat16 [4, 32, 128], P(None, 'tensor', 'dp'), may hold values from -0.5 to 0.5
- conv_bias: bfloat16 [32, 128], P('tensor', 'dp'), may hold values from -0.5 to 0.5
- select_weight: bfloat16 [32, 128, 160], P('tensor', 'dp'), may hold values from -0.09375 to 0.09375
- delta_weight: bfloat16 [128, 4096], P('dp', 'tensor'), may hold values from -0.5 to 0.5
- delta_bias: bfloat16 [32, 128], P('tensor', 'dp'), may hold values from -6 to -1
- decay_log: bfloat16 [4096, 16], P('tensor', 'dp'), may hold values from 0 to 2.765625
- skip_weight: bfloat16 [32, 128], P('tensor', 'dp'), may hold values from 0.5 to 1.5
- out_weight: bfloat16 [4096, 2048], P('tensor', 'dp'), may hold values from -0.1875 to 0.1875
- out_cotangent: bfloat16 [6144, 2048], P(('dp', 'tensor')), may hold values from -6 to 6
- seq_lengths: int32 [4, 4], P('dp'), may hold values from 1 to 1152, 1536 in all within a row
- deal_order: int32 [6144], P(('dp', 'tensor')), may hold values from 0 to 6143, as said below
Outputs:
- block_output: bfloat16 [6144, 2048], P(('dp', 'tensor'))
- input_grad: bfloat16 [6144, 2048], P(('dp', 'tensor'))
- norm_gain_grad: float32 [2048], P('dp')
- in_weight_grad: float32 [2, 2048, 4096], P(None, 'dp', 'tensor')
- conv_weight_grad: float32 [4, 32, 128], P(None, 'tensor', 'dp')
- conv_bias_grad: float32 [32, 128], P('tensor', 'dp')
- select_weight_grad: float32 [32, 128, 160], P('tensor', 'dp')
- delta_weight_grad: float32 [128, 4096], P('dp', 'tensor')
- delta_bias_grad: float32 [32, 128], P('tensor', 'dp')
- decay_log_grad: float32 [4096, 16], P('tensor', 'dp')
- skip_weight_grad: float32 [32, 128], P('tensor', 'dp')
- out_weight_grad: float32 [4096, 2048], P('tensor', 'dp')
The draws below stay inside these ranges and needn't reach their ends.
Inputs may be any that keep to these rules, and one draw needn't show every extreme that they name: A permutation of the tokens: dealt place p holds the token of given place deal_order[p]. p and deal_order[p] lie in the same one of the 8 runs of 192 places inside their blocks of 1536 places, and each aligned run of 192 given places sends exactly 48 tokens to each block of 1536 dealt places. `seq_lengths`: each row sums to 1536; its largest entry is exactly 1152.
All inputs are finite; a program needn't handle non-finite values.
Results may differ from the reference program's by a relative error of at most 0.012.
Values may be sent and summed in bfloat16 or wider, within the bound.
No kernel may reach another device: no remote copies, remote signals or barrier semaphores. Data moves between devices by JAX's collectives and lax.ppermute only.
A program may use at most 320 MiB of HBM per device.

```python
import math
import jax
import jax.numpy as jnp
import numpy as np
from jax import lax

D_MODEL = 2048
D_INNER = 4096
STATE = 16
KERNEL = 4
DT_RANK = 128
LANE = 128
ROWS_DEV = 192
SEQS = 4
GROUP = 1536
TOKENS = 6144
LONGEST = 1152
N_DP = 4
N_TENSOR = 8


def draw_deal_order(key, part):
    per_pair = ROWS_DEV // N_DP
    first_key = jax.random.fold_in(key, 11)
    second_key = jax.random.fold_in(key, 23)
    local_rows = jnp.broadcast_to(jnp.arange(ROWS_DEV, dtype=jnp.int32), (N_TENSOR, N_DP, ROWS_DEV))
    shuffled = jax.random.permutation(first_key, local_rows, axis=2, independent=True)
    tensor_ids = jnp.arange(N_TENSOR, dtype=jnp.int32)[:, None, None]
    source_ids = jnp.arange(N_DP, dtype=jnp.int32)[None, :, None]
    given_place = source_ids * GROUP + tensor_ids * ROWS_DEV + shuffled
    given_place = given_place.reshape(N_TENSOR, N_DP, N_DP, per_pair)
    arrived = jnp.transpose(given_place, (0, 2, 1, 3)).reshape(N_TENSOR, N_DP, ROWS_DEV)
    slot_ids = jnp.broadcast_to(jnp.arange(ROWS_DEV, dtype=jnp.int32), (N_TENSOR, N_DP, ROWS_DEV))
    placing = jax.random.permutation(second_key, slot_ids, axis=2, independent=True)
    dealt_rows = jnp.take_along_axis(arrived, placing, axis=2)
    return jnp.transpose(dealt_rows, (1, 0, 2)).reshape(TOKENS).astype(jnp.int32)


def level_of(rng, extent, pieces, smallest, top_value):
    def one(dim, parts):
        steps = jax.random.uniform(jax.random.fold_in(jax.random.fold_in(rng, 6), dim), (parts,), jnp.float32, smallest / len(pieces), top_value / len(pieces))
        return jnp.repeat(jnp.exp(steps), extent[dim] // parts).reshape((-1,) + (1,) * (len(extent) - dim - 1))

    loudness = one(*pieces[0])
    for cut in pieces[1:]:
        loudness = loudness * one(*cut)
    return loudness


def length_profile(count, total, reach, lean):
    portions = [(1 << 20) // math.isqrt(grade ** lean) + 1 for grade in range(2, count + 1)]
    rest, given = total - reach - (count - 1), [1] * (count - 1)
    while rest > 0:
        candidates = [i for i in range(count - 1) if given[i] < reach]
        pool, left = sum([portions[i] for i in candidates]), rest
        for i in candidates:
            more = min(reach - given[i], max(1, left * portions[i] // pool), rest)
            given[i] = given[i] + more
            rest = rest - more
    return np.array([reach] + given)


def ragged(rng, count, total, most, slope):
    if count == 2:
        one = jax.random.randint(rng, (), max(1, total - most), min(most, total - 1) + 1)
        return jnp.stack([one, total - one])
    sizes = jnp.asarray(length_profile(count, total, most, slope), jnp.int32)
    couples = (count - 1) // 2
    donor, receiver = sizes[1:1 + 2 * couples:2], sizes[2:2 + 2 * couples:2]
    room = jnp.minimum(donor - 1, most - receiver)
    moved = jax.random.randint(jax.random.fold_in(rng, 1), (couples,), 0, 1 << 20) % (room + 1)
    sizes = sizes.at[1:1 + 2 * couples:2].set(donor - moved).at[2:2 + 2 * couples:2].set(receiver + moved)
    return sizes[jax.random.permutation(jax.random.fold_in(rng, 2), count)]


def centred(key, dims, spread, limit, split=(), held_as=jnp.bfloat16):
    gain = level_of(key, dims, split, -0.22, 0.18) if split else 1.0
    values = jax.random.normal(key, dims, jnp.float32) * spread * gain
    return jnp.minimum(jnp.maximum(values, -limit), limit).astype(held_as)


def setup_inputs(seed: int = 0) -> dict:
    streams_of = jax.random.split(jax.random.key(seed), 15)
    return {
        "block_input": centred(streams_of[0], (TOKENS, D_MODEL), 1.0, 6.0, ((0, 32),)),
        "norm_gain": jnp.clip(1.0 + 0.1 * jax.random.normal(streams_of[1], (D_MODEL,), jnp.float32), 0.5, 1.5).astype(jnp.bfloat16),
        "in_weight": centred(streams_of[2], (2, D_MODEL, D_INNER), D_MODEL ** -0.5, 0.125, ((1, 4), (2, 8))),
        "conv_weight": jnp.clip(jax.random.uniform(streams_of[3], (KERNEL, D_INNER // LANE, LANE), jnp.float32, -0.5, 0.5) * level_of(streams_of[3], (KERNEL, D_INNER // LANE, LANE), ((1, 8), (2, 4)), -0.4, 0.0), -0.5, 0.5).astype(jnp.bfloat16),
        "conv_bias": jnp.clip(jax.random.uniform(streams_of[4], (D_INNER // LANE, LANE), jnp.float32, -0.5, 0.5) * level_of(streams_of[4], (D_INNER // LANE, LANE), ((0, 8), (1, 4)), -0.4, 0.0), -0.5, 0.5).astype(jnp.bfloat16),
        "select_weight": centred(streams_of[5], (D_INNER // LANE, LANE, DT_RANK + 2 * STATE), D_INNER ** -0.5, 0.09375, ((0, 8), (1, 4))),
        "delta_weight": centred(streams_of[6], (DT_RANK, D_INNER), DT_RANK ** -0.5, 0.5, ((0, 4), (1, 8))),
        "delta_bias": jnp.clip(-6.0 + 5.0 * jax.random.uniform(streams_of[7], (D_INNER // LANE, LANE), jnp.float32) ** level_of(streams_of[7], (D_INNER // LANE, LANE), ((0, 8), (1, 4)), -0.2, 0.2), -6.0, -1.0).astype(jnp.bfloat16),
        "decay_log": jnp.clip(2.765625 * jax.random.uniform(streams_of[8], (D_INNER, STATE), jnp.float32) ** level_of(streams_of[8], (D_INNER, STATE), ((0, 8), (1, 4)), -0.2, 0.2), 0.0, 2.765625).astype(jnp.bfloat16),
        "skip_weight": jnp.clip(0.5 + 1.0 * jax.random.uniform(streams_of[9], (D_INNER // LANE, LANE), jnp.float32) ** level_of(streams_of[9], (D_INNER // LANE, LANE), ((0, 8), (1, 4)), -0.2, 0.2), 0.5, 1.5).astype(jnp.bfloat16),
        "out_weight": centred(streams_of[10], (D_INNER, D_MODEL), (D_INNER // 4) ** -0.5, 0.1875, ((0, 8), (1, 4))),
        "out_cotangent": centred(streams_of[11], (TOKENS, D_MODEL), 1.0, 6.0, ((0, 32),)),
        "seq_lengths": jax.vmap(lambda own: ragged(own, SEQS, GROUP, LONGEST, 2))(jax.random.split(streams_of[12], N_DP)).reshape((N_DP, SEQS)).astype(jnp.int32),
        "deal_order": draw_deal_order(jax.random.fold_in(streams_of[14], 71), 0),
    }


EPSILON = 1e-05
HIGH = lax.Precision.HIGHEST

@jax.custom_vjp
def low(v):
    return lax.optimization_barrier(v.astype(jnp.bfloat16)).astype(jnp.float32)

@jax.custom_vjp
def low_back(v):
    return v

def low_keep(v):
    return (low(v), None)

def low_pass(kept, grad):
    return (grad,)

def back_keep(v):
    return (v, None)

def back_low(kept, grad):
    return (low(grad),)
low.defvjp(low_keep, low_pass)
low_back.defvjp(back_keep, back_low)

def shifted(values, amount):
    head = jnp.zeros((amount,) + values.shape[1:], values.dtype)
    return jnp.concatenate([head, values[:values.shape[0] - amount]], axis=0)

def selective_scan(step_size, act_values, b_values, c_values, continues, decay_rate, skip_values):

    def position(current, inputs):
        step_row, act_row, b_row, c_row, keep_row = inputs
        decays = jnp.exp(step_row[:, None] * decay_rate) * keep_row
        current = decays * current + (step_row * act_row)[:, None] * b_row[None, :]
        return (current, lax.optimization_barrier(jnp.sum(current * c_row[None, :], axis=1)))

    def run_block(current, inputs):
        return lax.scan(position, current, inputs)
    blocked = tuple((array_item.reshape((-1, 64) + array_item.shape[1:]) for array_item in (step_size, act_values, b_values, c_values, continues)))
    unused, outputs = lax.scan(jax.checkpoint(run_block), jnp.zeros(decay_rate.shape, jnp.float32), blocked)
    return outputs.reshape(step_size.shape) + skip_values[None, :] * act_values

def group_block(weights, rows, lengths_row):
    norm_gain, in_weight, conv_weight, conv_bias, select_weight, delta_weight, delta_bias, decay_log, skip_weight, out_weight = weights
    taps = conv_weight.reshape(KERNEL, D_INNER)
    select_matrix = select_weight.reshape(D_INNER, DT_RANK + 2 * STATE)
    positions = jnp.arange(GROUP, dtype=jnp.int32)
    seq_ends = jnp.cumsum(lengths_row).astype(jnp.int32)
    begins = (seq_ends - lengths_row).astype(jnp.int32)
    inside = (positions[:, None] >= begins[None, :]) & (positions[:, None] < seq_ends[None, :])
    offset = (positions - lax.optimization_barrier(jnp.sum(jnp.where(inside, begins[None, :], 0), axis=1))).astype(jnp.int32)
    continues = (offset > 0).astype(jnp.float32)
    normed = low(rows * lax.rsqrt(lax.optimization_barrier(jnp.mean(rows * rows, axis=1, keepdims=True)) + EPSILON) * norm_gain[None, :])
    projected = low_back(low(jnp.einsum('gd,kdc->gkc', normed, in_weight, precision=HIGH)))
    inner_in = projected[:, 0]
    gate_in = projected[:, 1]
    convolved = conv_bias.reshape(D_INNER)[None, :]
    for tap_index in range(KERNEL):
        mask_row = (offset >= tap_index).astype(jnp.float32)[:, None]
        convolved = convolved + taps[tap_index][None, :] * shifted(inner_in, tap_index) * mask_row
    activated = low(jax.nn.silu(convolved))
    proj_sums = low_back(jnp.dot(activated, select_matrix, precision=HIGH))
    delta_low = low(proj_sums[:, :DT_RANK])
    b_values = proj_sums[:, DT_RANK:DT_RANK + STATE]
    c_values = proj_sums[:, DT_RANK + STATE:]
    pre_delta = low_back(jnp.dot(delta_low, delta_weight, precision=HIGH) + delta_bias.reshape(D_INNER)[None, :])
    step_size = jax.nn.softplus(pre_delta)
    decay_rate = -jnp.exp(decay_log)
    y_values = selective_scan(step_size, activated, b_values, c_values, continues, decay_rate, skip_weight.reshape(D_INNER))
    gated = low(y_values * jax.nn.silu(gate_in))
    return rows + jnp.dot(gated, out_weight, precision=HIGH)

def reference(block_input, norm_gain, in_weight, conv_weight, conv_bias, select_weight, delta_weight, delta_bias, decay_log, skip_weight, out_weight, out_cotangent, seq_lengths, deal_order):
    weights = tuple((weight_item.astype(jnp.float32) for weight_item in (norm_gain, in_weight, conv_weight, conv_bias, select_weight, delta_weight, delta_bias, decay_log, skip_weight, out_weight)))
    dealt_x = block_input[deal_order].astype(jnp.float32).reshape(N_DP, GROUP, D_MODEL)
    dealt_cot = out_cotangent[deal_order].astype(jnp.float32).reshape(N_DP, GROUP, D_MODEL)

    def one_group(totals, inputs):
        rows, cot_rows, lengths_row = inputs

        def forward(weight_args, row_args):
            return group_block(weight_args, row_args, lengths_row)
        result, pullback = jax.vjp(forward, weights, rows)
        weight_grads, row_grads = pullback(cot_rows)
        totals = jax.tree.map(lambda total_item, grad_item: total_item + grad_item, totals, weight_grads)
        return (totals, (result, row_grads))
    zero_grads = jax.tree.map(jnp.zeros_like, weights)
    weight_totals, (outputs, row_grads) = lax.scan(one_group, zero_grads, (dealt_x, dealt_cot, seq_lengths))
    inverse = jnp.zeros((TOKENS,), jnp.int32).at[deal_order].set(jnp.arange(TOKENS, dtype=jnp.int32))
    block_output = outputs.reshape(TOKENS, D_MODEL)[inverse].astype(jnp.bfloat16)
    input_grad = row_grads.reshape(TOKENS, D_MODEL)[inverse].astype(jnp.bfloat16)
    return (block_output, input_grad, weight_totals[0], weight_totals[1], weight_totals[2], weight_totals[3], weight_totals[4], weight_totals[5], weight_totals[6], weight_totals[7], weight_totals[8], weight_totals[9])
```

```python
import functools
import jax
import jax.numpy as jnp
from jax import lax
from jax.experimental import pallas as pl
from jax.experimental.pallas import tpu as pltpu

from jax.sharding import PartitionSpec as P

LOG2E = 1.4426950408889634
FAR = 1e30
GROUP_STEP = 16


def softplus(v):
    return jnp.maximum(v, 0.0) + jnp.log1p(jnp.exp(-jnp.abs(v)))


def sigmoid(v):
    return 1.0 / (1.0 + jnp.exp(-v))


def spread_mask(rows, states):
    row = lax.broadcasted_iota(jnp.int32, (rows, GROUP_STEP * states), 0) % GROUP_STEP
    lane = lax.broadcasted_iota(jnp.int32, (rows, GROUP_STEP * states), 1) // states
    return row == lane


def tile_matrix(states, dtype):
    row = lax.broadcasted_iota(jnp.int32, (states, GROUP_STEP * states), 0)
    lane = lax.broadcasted_iota(jnp.int32, (states, GROUP_STEP * states), 1) % states
    return (row == lane).astype(dtype)


def untile_matrix(states, dtype):
    row = lax.broadcasted_iota(jnp.int32, (GROUP_STEP * states, states), 0) % states
    lane = lax.broadcasted_iota(jnp.int32, (GROUP_STEP * states, states), 1)
    return (row == lane).astype(dtype)


NT = (((1,), (1,)), ((), ()))
TN = (((0,), (0,)), ((), ()))


def forward_kernel(low_ref, act_ref, gate_ref, begin_ref, bt_ref, c_ref, dw_ref, bias_ref, rate_ref, skip_ref,
                   pre_ref, y_ref, gated_ref, hist_ref,
                   dtm_s, u_s, h_s):
    states = rate_ref.shape[0]
    chunk = act_ref.shape[0]

    @pl.when(pl.program_id(0) == 0)
    def _():
        h_s[...] = jnp.zeros_like(h_s)

    pre = jnp.dot(low_ref[...], dw_ref[...], preferred_element_type=jnp.float32) + bias_ref[...]
    pre_ref[...] = pre
    dt = softplus(pre)
    act = act_ref[...].astype(jnp.float32)
    u_s[...] = dt * act
    dtm_s[...] = jnp.where(begin_ref[...] > 0.0, FAR, dt)
    rate = rate_ref[...]
    bt = bt_ref[...]
    spread = jnp.where(
        spread_mask(chunk, states),
        jnp.dot(c_ref[...], tile_matrix(states, jnp.bfloat16), preferred_element_type=jnp.float32),
        0.0,
    ).astype(jnp.bfloat16)

    def group(g, h):
        base = pl.multiple_of(g * GROUP_STEP, GROUP_STEP)
        bg = pltpu.roll(bt, (chunk - base) % chunk, 1)
        dtm = dtm_s[pl.ds(base, GROUP_STEP), :]
        u = u_s[pl.ds(base, GROUP_STEP), :]
        for j in range(GROUP_STEP):
            a = jnp.exp2(dtm[j:j + 1, :] * rate)
            h = a * h + u[j:j + 1, :] * bg[:, j:j + 1]
            at = pl.multiple_of((base + j) * states, states)
            hist_ref[pl.ds(at, states), :] = h.astype(jnp.bfloat16)
        return h

    h_s[...] = lax.fori_loop(0, chunk // GROUP_STEP, group, h_s[...])
    width = GROUP_STEP * states
    for g in range(chunk // GROUP_STEP):
        y_ref[g * GROUP_STEP:(g + 1) * GROUP_STEP, :] = jnp.dot(
            spread[g * GROUP_STEP:(g + 1) * GROUP_STEP, :], hist_ref[g * width:(g + 1) * width, :],
            preferred_element_type=jnp.float32)
    y = y_ref[...] + skip_ref[...] * act
    y_ref[...] = y
    gate = gate_ref[...].astype(jnp.float32)
    gated_ref[...] = (y * gate * sigmoid(gate)).astype(jnp.bfloat16)


def scan_forward(low, act, gate, begin, bt, c_values, delta_w, bias, rate, skip, chunk=128):
    tokens, channels = act.shape
    states = rate.shape[0]
    rank = low.shape[1]
    row = lambda i: (i, 0)
    fixed = lambda i: (0, 0)
    return pl.pallas_call(
        forward_kernel,
        name="scan_forward",
        grid=(tokens // chunk,),
        in_specs=[
            pl.BlockSpec((chunk, rank), row),
            pl.BlockSpec((chunk, channels), row),
            pl.BlockSpec((chunk, channels), row),
            pl.BlockSpec((chunk, 1), row),
            pl.BlockSpec((states, chunk), lambda i: (0, i)),
            pl.BlockSpec((chunk, states), row),
            pl.BlockSpec((rank, channels), fixed),
            pl.BlockSpec((1, channels), fixed),
            pl.BlockSpec((states, channels), fixed),
            pl.BlockSpec((1, channels), fixed),
        ],
        out_specs=[
            pl.BlockSpec((chunk, channels), row),
            pl.BlockSpec((chunk, channels), row),
            pl.BlockSpec((chunk, channels), row),
            pl.BlockSpec((chunk * states, channels), row),
        ],
        out_shape=[
            jax.ShapeDtypeStruct((tokens, channels), jnp.float32),
            jax.ShapeDtypeStruct((tokens, channels), jnp.float32),
            jax.ShapeDtypeStruct((tokens, channels), jnp.bfloat16),
            jax.ShapeDtypeStruct((tokens * states, channels), jnp.bfloat16),
        ],
        scratch_shapes=[
            pltpu.VMEM((chunk, channels), jnp.float32),
            pltpu.VMEM((chunk, channels), jnp.float32),
            pltpu.VMEM((states, channels), jnp.float32),
        ],
        compiler_params=pltpu.CompilerParams(dimension_semantics=("arbitrary",), vmem_limit_bytes=48 << 20),
        cost_estimate=pl.CostEstimate(flops=tokens * channels * states * 20, transcendentals=tokens * channels * states, bytes_accessed=tokens * channels * (states * 2 + 20)),
    )(low, act, gate, begin, bt, c_values, delta_w, bias, rate, skip)


def backward_kernel(low_ref, pre_ref, act_ref, gate_ref, gg_ref, y_ref, begin_ref, b_ref, ct_ref,
                    hist_ref, prior_ref, dw_ref, rate_ref, skip_ref,
                    ggate_ref, gact_ref, gpre_ref, glow_ref, gbc_ref, rgrad_ref, dwgrad_ref, rows_ref,
                    dtm_s, u_s, dt_s, gy_s, drive_s, decay_s, carry_s, adj_s, thr_s):
    states = rate_ref.shape[0]
    chunk = act_ref.shape[0]
    step = pl.program_id(0)

    @pl.when(step == 0)
    def _():
        carry_s[...] = jnp.zeros_like(carry_s)
        rgrad_ref[...] = jnp.zeros_like(rgrad_ref)
        dwgrad_ref[...] = jnp.zeros_like(dwgrad_ref)
        rows_ref[...] = jnp.zeros_like(rows_ref)

    pre = pre_ref[...]
    dt = softplus(pre)
    act = act_ref[...].astype(jnp.float32)
    dt_s[...] = dt
    u_s[...] = dt * act
    dtm_s[...] = jnp.where(begin_ref[...] > 0.0, FAR, dt)
    gate = gate_ref[...].astype(jnp.float32)
    sig = sigmoid(gate)
    gg = gg_ref[...].astype(jnp.float32) * sig
    gy = gg * gate
    gy_s[...] = gy
    ggate_ref[...] = (gg * y_ref[...] * (1.0 + gate * (1.0 - sig))).astype(jnp.bfloat16)
    rate = rate_ref[...]
    scale = 1.0 / LOG2E
    ct = ct_ref[...]
    groups = chunk // GROUP_STEP
    width = GROUP_STEP * states

    def one(base, j, carry, rgrad, cg, dtm, dts, gys, prior):
        a = jnp.exp2(dtm[j:j + 1, :] * rate)
        adj = cg[:, j:j + 1] * gys[j:j + 1, :] + carry
        carry = a * adj
        through = carry * prior
        rgrad = rgrad + through * dts[j:j + 1, :]
        at = pl.multiple_of((base + j) * states, states)
        adj_s[pl.ds(at, states), :] = adj.astype(jnp.bfloat16)
        thr_s[pl.ds(at, states), :] = (through * rate).astype(jnp.bfloat16)
        return carry, rgrad

    def group(k, held):
        carry, rgrad = held
        g = groups - 1 - k
        base = pl.multiple_of(g * GROUP_STEP, GROUP_STEP)
        cg = pltpu.roll(ct, (chunk - base) % chunk, 1)
        dtm = dtm_s[pl.ds(base, GROUP_STEP), :]
        dts = dt_s[pl.ds(base, GROUP_STEP), :]
        gys = gy_s[pl.ds(base, GROUP_STEP), :]
        for j in reversed(range(GROUP_STEP)):
            if j > 0:
                at = pl.multiple_of((base + j - 1) * states, states)
                prior = hist_ref[pl.ds(at, states), :].astype(jnp.float32)
            else:
                at = pl.multiple_of(jnp.maximum(base - 1, 0) * states, states)
                prior = jnp.where(base == 0, prior_ref[...].astype(jnp.float32), hist_ref[pl.ds(at, states), :].astype(jnp.float32))
            carry, rgrad = one(base, j, carry, rgrad, cg, dtm, dts, gys, prior)
        return carry, rgrad

    carry, rgrad = lax.fori_loop(0, groups, group, (carry_s[...], rgrad_ref[...]))
    carry_s[...] = carry
    rgrad_ref[...] = rgrad

    mask = spread_mask(GROUP_STEP, states)
    untile = untile_matrix(states, jnp.bfloat16)
    spread_b = jnp.where(
        spread_mask(chunk, states),
        jnp.dot(b_ref[...], tile_matrix(states, jnp.bfloat16), preferred_element_type=jnp.float32),
        0.0,
    ).astype(jnp.bfloat16)
    ones = jnp.where(mask, 1.0, 0.0).astype(jnp.bfloat16)
    ub = u_s[...].astype(jnp.bfloat16)
    gyb = gy.astype(jnp.bfloat16)
    for g in range(groups):
        rows = slice(g * GROUP_STEP, (g + 1) * GROUP_STEP)
        wide = slice(g * width, (g + 1) * width)
        adj = adj_s[wide, :]
        drive_s[rows, :] = jnp.dot(spread_b[rows, :], adj, preferred_element_type=jnp.float32)
        decay_s[rows, :] = jnp.dot(ones, thr_s[wide, :], preferred_element_type=jnp.float32)
        gb = lax.dot_general(ub[rows, :], adj, NT, preferred_element_type=jnp.float32)
        gc = lax.dot_general(gyb[rows, :], hist_ref[wide, :], NT, preferred_element_type=jnp.float32)
        gb = jnp.where(mask, gb, 0.0).astype(jnp.bfloat16)
        gc = jnp.where(mask, gc, 0.0).astype(jnp.bfloat16)
        gbc_ref[rows, :states] = jnp.dot(gb, untile, preferred_element_type=jnp.float32)
        gbc_ref[rows, states:] = jnp.dot(gc, untile, preferred_element_type=jnp.float32)
    drive = drive_s[...]
    gact_ref[...] = drive * dt + gy * skip_ref[...]
    gpre = ((drive * act + decay_s[...] * scale) * sigmoid(pre)).astype(jnp.bfloat16)
    gpre_ref[...] = gpre
    rows_ref[0:1, :] += jnp.sum(gy * act, axis=0, keepdims=True)
    rows_ref[1:2, :] += jnp.sum(gpre.astype(jnp.float32), axis=0, keepdims=True)
    dwgrad_ref[...] += lax.dot_general(low_ref[...], gpre, TN, preferred_element_type=jnp.float32)
    glow_ref[...] = lax.dot_general(gpre, dw_ref[...], NT, preferred_element_type=jnp.float32)


def scan_backward(low, pre, act, gate, gg, y, begin, b_values, ct, hist, delta_w, rate, skip, chunk=128):
    tokens, channels = act.shape
    states = rate.shape[0]
    rank = low.shape[1]
    steps = tokens // chunk
    row = lambda i: (steps - 1 - i, 0)
    fixed = lambda i: (0, 0)
    return pl.pallas_call(
        backward_kernel,
        name="scan_backward",
        grid=(steps,),
        in_specs=[
            pl.BlockSpec((chunk, rank), row),
            pl.BlockSpec((chunk, channels), row),
            pl.BlockSpec((chunk, channels), row),
            pl.BlockSpec((chunk, channels), row),
            pl.BlockSpec((chunk, channels), row),
            pl.BlockSpec((chunk, channels), row),
            pl.BlockSpec((chunk, 1), row),
            pl.BlockSpec((chunk, states), row),
            pl.BlockSpec((states, chunk), lambda i: (0, steps - 1 - i)),
            pl.BlockSpec((chunk * states, channels), row),
            pl.BlockSpec((states, channels), lambda i: (jnp.maximum((steps - 1 - i) * chunk - 1, 0), 0)),
            pl.BlockSpec((rank, channels), fixed),
            pl.BlockSpec((states, channels), fixed),
            pl.BlockSpec((1, channels), fixed),
        ],
        out_specs=[
            pl.BlockSpec((chunk, channels), row),
            pl.BlockSpec((chunk, channels), row),
            pl.BlockSpec((chunk, channels), row),
            pl.BlockSpec((chunk, rank), row),
            pl.BlockSpec((chunk, 2 * states), row),
            pl.BlockSpec((states, channels), fixed),
            pl.BlockSpec((rank, channels), fixed),
            pl.BlockSpec((8, channels), fixed),
        ],
        out_shape=[
            jax.ShapeDtypeStruct((tokens, channels), jnp.bfloat16),
            jax.ShapeDtypeStruct((tokens, channels), jnp.float32),
            jax.ShapeDtypeStruct((tokens, channels), jnp.bfloat16),
            jax.ShapeDtypeStruct((tokens, rank), jnp.float32),
            jax.ShapeDtypeStruct((tokens, 2 * states), jnp.float32),
            jax.ShapeDtypeStruct((states, channels), jnp.float32),
            jax.ShapeDtypeStruct((rank, channels), jnp.float32),
            jax.ShapeDtypeStruct((8, channels), jnp.float32),
        ],
        scratch_shapes=[pltpu.VMEM((chunk, channels), jnp.float32)] * 6
        + [pltpu.VMEM((states, channels), jnp.float32)]
        + [pltpu.VMEM((chunk * states, channels), jnp.bfloat16)] * 2,
        compiler_params=pltpu.CompilerParams(dimension_semantics=("arbitrary",), vmem_limit_bytes=56 << 20),
        cost_estimate=pl.CostEstimate(flops=tokens * channels * states * 40, transcendentals=tokens * channels * states, bytes_accessed=tokens * channels * (states * 2 + 28)),
    )(low, pre, act, gate, gg, y, begin, b_values, ct, hist, hist, delta_w, rate, skip)


EPSILON = 1e-05


def deal_kernel(x_ref, cot_ref, order_ref, gain_ref, me_ref, sendx_ref, sendc_ref, pick_ref, place_ref):
    rows = x_ref.shape[0]
    dp_size = order_ref.shape[0]
    group_tokens = me_ref[1]
    me = me_ref[0]
    pair = rows // dp_size
    order = order_ref[...]
    source = order // group_tokens
    local = order % rows
    before = (
        lax.broadcasted_iota(jnp.int32, (rows, rows), 0) < lax.broadcasted_iota(jnp.int32, (rows, rows), 1)
    ).astype(jnp.bfloat16)
    slots = lax.broadcasted_iota(jnp.int32, (rows, rows), 0)
    chosen = source == me
    rank = jnp.dot(chosen.astype(jnp.bfloat16), before, preferred_element_type=jnp.float32).astype(jnp.int32)
    dest = lax.broadcasted_iota(jnp.int32, (dp_size, rows), 0)
    slot = jnp.where(chosen, dest * pair + rank, -1)
    pick = jnp.zeros((rows, rows), jnp.float32)
    for d in range(dp_size):
        pick += lax.dot_general(
            (slots == slot[d:d + 1, :]).astype(jnp.bfloat16),
            (slots == local[d:d + 1, :]).astype(jnp.bfloat16),
            NT, preferred_element_type=jnp.float32)
    pick = pick.astype(jnp.bfloat16)
    pick_ref[...] = pick
    mine = jnp.sum(jnp.where(dest == me, source, 0), axis=0, keepdims=True)
    held = (mine == dest).astype(jnp.bfloat16)
    ranks = jnp.dot(held, before, preferred_element_type=jnp.float32).astype(jnp.int32)
    arrived = jnp.sum(jnp.where(mine == dest, dest * pair + ranks, 0), axis=0, keepdims=True)
    place_ref[...] = (slots == arrived).astype(jnp.bfloat16)
    x = x_ref[...].astype(jnp.float32)
    rinv = lax.rsqrt(jnp.mean(x * x, axis=1, keepdims=True) + EPSILON)
    normed = (x * rinv * gain_ref[...]).astype(jnp.bfloat16)
    sendx_ref[...] = jnp.dot(pick, normed, preferred_element_type=jnp.float32).astype(jnp.bfloat16)
    sendc_ref[...] = jnp.dot(pick, cot_ref[...], preferred_element_type=jnp.float32).astype(jnp.bfloat16)


def deal(x, cot, order, gain, me):
    rows, width = x.shape
    vm = pl.BlockSpec(memory_space=pltpu.VMEM)
    return pl.pallas_call(
        deal_kernel,
        name="deal",
        in_specs=[vm, vm, vm, vm, pl.BlockSpec(memory_space=pltpu.SMEM)],
        out_specs=[vm] * 4,
        out_shape=[
            jax.ShapeDtypeStruct((rows, width), jnp.bfloat16),
            jax.ShapeDtypeStruct((rows, width), jnp.bfloat16),
            jax.ShapeDtypeStruct((rows, rows), jnp.bfloat16),
            jax.ShapeDtypeStruct((rows, rows), jnp.bfloat16),
        ],
        compiler_params=pltpu.CompilerParams(vmem_limit_bytes=32 << 20),
        cost_estimate=pl.CostEstimate(flops=rows * rows * width * 6, transcendentals=rows, bytes_accessed=rows * width * 8),
    )(x, cot, order, gain, me)


def exact_dot(a, b, dims=(((1,), (0,)), ((), ()))):
    return lax.dot_general(a, b, dims, preferred_element_type=jnp.float32).astype(jnp.bfloat16)


def swap(values, axis):
    return lax.all_to_all(values, axis, split_axis=0, concat_axis=0, tiled=True)


def sum_all(part, axis):
    size = lax.axis_size(axis)
    pieces = part.astype(jnp.bfloat16).reshape((size, -1) + part.shape[1:])
    total = jnp.sum(swap(pieces, axis).astype(jnp.float32), axis=0).astype(jnp.bfloat16)
    everyone = jnp.broadcast_to(total[None], (size,) + total.shape)
    return swap(everyone, axis).reshape(part.shape)


def shifted(values, amount):
    if amount == 0:
        return values
    head = jnp.zeros((amount,) + values.shape[1:], values.dtype)
    return jnp.concatenate([head, values[: values.shape[0] - amount]], axis=0)


def unshifted(values, amount):
    if amount == 0:
        return values
    tail = jnp.zeros((amount,) + values.shape[1:], values.dtype)
    return jnp.concatenate([values[amount:], tail], axis=0)


def shards(
    block_input, norm_gain, in_weight, conv_weight, conv_bias, select_weight, delta_weight, delta_bias,
    decay_log, skip_weight, out_weight, out_cotangent, seq_lengths, deal_order,
):
    rows_dev = block_input.shape[0]
    dp_size = lax.axis_size("dp")
    tensor_size = lax.axis_size("tensor")
    pair = rows_dev // dp_size
    group_tokens = rows_dev * tensor_size
    me = jnp.stack([lax.axis_index("dp"), jnp.int32(group_tokens)]).astype(jnp.int32)
    orders = lax.all_gather(deal_order.reshape(1, rows_dev), "dp", axis=0, tiled=True)
    gain_full = lax.all_gather(norm_gain.reshape(1, -1), "dp", axis=1, tiled=True)
    gain_values = gain_full.astype(jnp.float32)
    send_rows, send_cot, pick, place = deal(block_input, out_cotangent, orders, gain_values, me)
    recv_rows = swap(send_rows.reshape(dp_size, pair, -1), "dp").reshape(rows_dev, -1)
    recv_cot = swap(send_cot.reshape(dp_size, pair, -1), "dp").reshape(rows_dev, -1)
    normed = exact_dot(place, recv_rows, TN)
    dealt_cot = exact_dot(place, recv_cot, TN)
    group_normed = lax.all_gather(normed, "tensor", axis=0, tiled=True)
    group_cot = lax.all_gather(dealt_cot, "tensor", axis=0, tiled=True)
    in_full = lax.all_gather(in_weight, "dp", axis=1, tiled=True)
    out_full = lax.all_gather(out_weight, "dp", axis=1, tiled=True)
    conv_full = lax.all_gather(conv_weight, "dp", axis=2, tiled=True)
    rows_full = lax.all_gather(jnp.stack([conv_bias, delta_bias, skip_weight]), "dp", axis=2, tiled=True)
    select_full = lax.all_gather(select_weight, "dp", axis=1, tiled=True)
    delta_full = lax.all_gather(delta_weight, "dp", axis=0, tiled=True)
    decay_full = lax.all_gather(decay_log.T, "dp", axis=0, tiled=True)
    channels = in_full.shape[2]
    taps = conv_full.shape[0]
    lane_width = rows_full.shape[2]
    states, low_rank = decay_full.shape[0], delta_full.shape[0]
    select_matrix = select_full.reshape(channels, -1)
    conv_taps = conv_full.astype(jnp.float32).reshape(taps, channels)
    conv_shift, delta_shift, skip_values = (
        rows_full[i].astype(jnp.float32).reshape(1, channels) for i in range(3)
    )
    decay_rate = -jnp.exp(decay_full.astype(jnp.float32))
    rate_two = decay_rate * LOG2E
    lengths_row = seq_lengths[0]
    seq_ends = jnp.cumsum(lengths_row)
    begins = seq_ends - lengths_row
    positions = jnp.arange(group_tokens, dtype=jnp.int32)
    inside = (positions[:, None] >= begins[None, :]) & (positions[:, None] < seq_ends[None, :])
    offset = positions - jnp.sum(jnp.where(inside, begins[None, :], 0), axis=1)
    begin = (offset == 0).astype(jnp.float32)[:, None]
    masks = [(offset >= k).astype(jnp.float32)[:, None] for k in range(taps)]
    projected = jnp.einsum("gd,kdc->kgc", group_normed, in_full, preferred_element_type=jnp.float32).astype(jnp.bfloat16)
    inner_in = projected[0].astype(jnp.float32)
    gate = projected[1]
    convolved = conv_shift
    for k in range(taps):
        convolved = convolved + conv_taps[k][None, :] * shifted(inner_in, k) * masks[k]
    activated = jax.nn.silu(convolved).astype(jnp.bfloat16)
    proj = sum_all(jnp.dot(activated, select_matrix, preferred_element_type=jnp.float32), "tensor")
    low = proj[:, :low_rank]
    b_values = proj[:, low_rank:low_rank + states]
    c_values = proj[:, low_rank + states:]
    pre, y, gated, hist = scan_forward(
        low, activated, gate, begin, b_values.T.astype(jnp.float32), c_values, delta_full, delta_shift, rate_two, skip_values)
    mixed = lax.psum_scatter(exact_dot(gated, out_full), "tensor", scatter_dimension=0, tiled=True)
    out_weight_grad = exact_dot(gated, group_cot, TN)
    grad_gated = lax.dot_general(group_cot, out_full, NT, preferred_element_type=jnp.float32)
    grad_gate, grad_act, grad_pre, grad_low, grad_bc, rate_grad, delta_weight_grad, row_grads = scan_backward(
        low, pre, activated, gate, grad_gated, y, begin, b_values, c_values.T.astype(jnp.float32), hist,
        delta_full, rate_two, skip_values)
    decay_grad = rate_grad * decay_rate
    grad_proj = sum_all(jnp.concatenate([grad_low, grad_bc], axis=1), "tensor")
    select_grad = lax.dot_general(activated, grad_proj, TN, preferred_element_type=jnp.float32)
    grad_act = grad_act + lax.dot_general(grad_proj, select_matrix, NT, preferred_element_type=jnp.float32)
    conv_sig = jax.nn.sigmoid(convolved)
    grad_conv = grad_act * conv_sig * (1.0 + convolved * (1.0 - conv_sig))
    conv_bias_grad = jnp.sum(grad_conv, axis=0)
    tap_grads = []
    grad_inner = jnp.zeros_like(grad_conv)
    for k in range(taps):
        masked = grad_conv * masks[k]
        tap_grads.append(jnp.sum(masked * shifted(inner_in, k), axis=0))
        grad_inner = grad_inner + unshifted(masked * conv_taps[k][None, :], k)
    grad_inner = grad_inner.astype(jnp.bfloat16)
    in_grad = jnp.stack([exact_dot(group_normed, grad_inner, TN), exact_dot(group_normed, grad_gate, TN)])
    grad_normed = (
        lax.dot_general(grad_inner, in_full[0], NT, preferred_element_type=jnp.float32)
        + lax.dot_general(grad_gate, in_full[1], NT, preferred_element_type=jnp.float32)
    ).astype(jnp.bfloat16)
    grad_rows = lax.psum_scatter(grad_normed, "tensor", scatter_dimension=0, tiled=True)
    in_weight_grad = lax.psum_scatter(in_grad, "dp", scatter_dimension=1, tiled=True).astype(jnp.float32)
    out_grad = lax.psum_scatter(out_weight_grad, "dp", scatter_dimension=1, tiled=True).astype(jnp.float32)

    def by_lane(values):
        lanes = values.reshape(-1, channels // lane_width, dp_size, lane_width // dp_size)
        return jnp.moveaxis(lanes, 2, 0).reshape(dp_size, -1)

    parts = [
        by_lane(jnp.stack(tap_grads)),
        by_lane(conv_bias_grad),
        by_lane(row_grads[1]),
        by_lane(row_grads[0]),
        decay_grad.reshape(dp_size, -1),
        delta_weight_grad.reshape(dp_size, -1),
        jnp.moveaxis(select_grad.reshape(channels // lane_width, dp_size, -1), 1, 0).reshape(dp_size, -1),
    ]
    sizes = [part.shape[1] for part in parts]
    flat = jnp.concatenate(parts, axis=1)
    fill = -flat.shape[1] % 1024
    flat = jnp.pad(flat, ((0, 0), (0, fill))).astype(jnp.bfloat16).reshape(dp_size, -1, 128)
    flat = jnp.sum(swap(flat, "dp").astype(jnp.float32), axis=0).reshape(-1)
    small, start = [], 0
    for size in sizes:
        small.append(flat[start:start + size])
        start += size
    gain_part = jnp.sum(in_weight.astype(jnp.float32) * in_weight_grad, axis=(0, 2))
    gain_grad = lax.psum(gain_part, "tensor") / norm_gain.astype(jnp.float32)
    home_out = swap(exact_dot(place, mixed).reshape(dp_size, pair, -1), "dp").reshape(rows_dev, -1)
    home_grad = swap(exact_dot(place, grad_rows).reshape(dp_size, pair, -1), "dp").reshape(rows_dev, -1)
    rows_float = block_input.astype(jnp.float32)
    block_output = (rows_float + lax.dot_general(pick, home_out, TN, preferred_element_type=jnp.float32)).astype(jnp.bfloat16)
    inverse_rms = lax.rsqrt(jnp.mean(rows_float * rows_float, axis=1, keepdims=True) + EPSILON)
    unit_rows = rows_float * inverse_rms
    scaled = lax.dot_general(pick, home_grad, TN, preferred_element_type=jnp.float32) * gain_values
    input_grad = (
        out_cotangent.astype(jnp.float32)
        + inverse_rms * (scaled - unit_rows * jnp.mean(scaled * unit_rows, axis=1, keepdims=True))
    ).astype(jnp.bfloat16)
    return (
        block_output,
        input_grad,
        gain_grad,
        in_weight_grad,
        small[0].reshape(conv_weight.shape),
        small[1].reshape(conv_bias.shape),
        small[6].reshape(select_weight.shape),
        small[5].reshape(delta_weight.shape),
        small[2].reshape(delta_bias.shape),
        small[4].reshape(decay_log.shape[1], decay_log.shape[0]).T,
        small[3].reshape(skip_weight.shape),
        out_grad,
    )


def solution(mesh):
    return jax.shard_map(
        shards,
        mesh=mesh,
        in_specs=(
            P(("dp", "tensor"), None),
            P("dp"),
            P(None, "dp", "tensor"),
            P(None, "tensor", "dp"),
            P("tensor", "dp"),
            P("tensor", "dp", None),
            P("dp", "tensor"),
            P("tensor", "dp"),
            P("tensor", "dp"),
            P("tensor", "dp"),
            P("tensor", "dp"),
            P(("dp", "tensor"), None),
            P("dp", None),
            P(("dp", "tensor")),
        ),
        out_specs=(
            P(("dp", "tensor"), None),
            P(("dp", "tensor"), None),
            P("dp"),
            P(None, "dp", "tensor"),
            P(None, "tensor", "dp"),
            P("tensor", "dp"),
            P("tensor", "dp", None),
            P("dp", "tensor"),
            P("tensor", "dp"),
            P("tensor", "dp"),
            P("tensor", "dp"),
            P("tensor", "dp"),
        ),
        check_vma=False,
    )
```

```python
import functools

import jax
import jax.numpy as jnp
from jax import lax
from jax.experimental import pallas as pl
from jax.experimental.pallas import tpu as pltpu
from jax.sharding import PartitionSpec as P

EPSILON = 1e-05
FAR = 1e30
LANES = 128
STEP = 48
SPAN = 16
SMALL = pl.CostEstimate(flops=1, transcendentals=0, bytes_accessed=1)
NT = (((1,), (1,)), ((), ()))
TN = (((0,), (0,)), ((), ()))
F32 = jnp.float32
BF16 = jnp.bfloat16


def softplus(v):
    return jnp.maximum(v, 0.0) + jnp.log1p(jnp.exp(-jnp.abs(v)))


def sigmoid(v):
    return 1.0 / (1.0 + jnp.exp(-v))


def mm(a, b, dims=(((1,), (0,)), ((), ()))):
    return lax.dot_general(a, b, dims, preferred_element_type=F32)


def column_at(states, tokens):
    return lax.broadcasted_iota(jnp.int32, (states, tokens), 1)


def write_packed(out_ref, low, wide_ref):
    rows, rank = low.shape
    states = wide_ref.shape[0] // 2
    rest = rows - LANES
    out_ref[0, 0:rows, :] = low.astype(out_ref.dtype)
    out_ref[0, rows:rows + 2 * states, :] = wide_ref[:, 0:LANES].astype(out_ref.dtype)
    tail = wide_ref[:, LANES:2 * LANES]
    lane = lax.broadcasted_iota(jnp.int32, (states, LANES), 1)
    both = jnp.where(lane < rest, tail[:states], pltpu.roll(tail[states:], rest, 1))
    out_ref[0, rows + 2 * states:rows + 3 * states, :] = both.astype(out_ref.dtype)


def read_packed(in_ref, states):
    rows = in_ref.shape[1] - 3 * states
    rest = rows - LANES
    low = in_ref[0, 0:rows, :]
    head = in_ref[0, rows:rows + 2 * states, :].astype(F32)
    both = in_ref[0, rows + 2 * states:rows + 3 * states, :].astype(F32)
    first = jnp.concatenate([head[:states], both], axis=1)
    second = jnp.concatenate([head[states:], pltpu.roll(both, LANES - rest, 1)], axis=1)
    return low, first, second


def front_kernel(me_ref, inner_ref, offset_ref, taps_ref, shift_ref, low_ref, bc_ref, act_ref, part_ref, ext_s, wide_s):
    rows = inner_ref.shape[0]
    taps = taps_ref.shape[0]

    @pl.when(pl.program_id(0) == 0)
    def _():
        ext_s[0:8, :] = jnp.zeros((8, ext_s.shape[1]), F32)

    ext_s[8:8 + rows, :] = inner_ref[...].astype(F32)
    offset = offset_ref[...]
    conv = shift_ref[...] + taps_ref[0:1, :] * ext_s[8:8 + rows, :]
    for k in range(1, taps):
        conv += jnp.where(offset >= k, taps_ref[k:k + 1, :], 0.0) * ext_s[pl.ds(8 - k, rows), :]
    act = (conv * sigmoid(conv)).astype(BF16)
    act_ref[...] = act
    ext_s[0:8, :] = ext_s[rows:rows + 8, :]
    wide_s[:, 0:rows] = mm(bc_ref[...], act, NT)
    write_packed(part_ref, mm(act, low_ref[...]), wide_s)


def front(me, projected, offset, taps, shift, low_w, bc_w):
    tokens, channels = projected.shape[0], taps.shape[1]
    runs, rows = tokens // ROWS[0], ROWS[0]
    packed = rows + 3 * bc_w.shape[0] // 2
    row = lambda i, me: (i, 0)
    fixed = lambda i, me: (0, 0)
    return pl.pallas_call(
        front_kernel,
        name="front",
        grid_spec=pltpu.PrefetchScalarGridSpec(
            num_scalar_prefetch=1,
            grid=(runs,),
            in_specs=[
                pl.BlockSpec((rows, channels), row),
                pl.BlockSpec((rows, 1), row),
                pl.BlockSpec(taps.shape, fixed),
                pl.BlockSpec(shift.shape, fixed),
                pl.BlockSpec(low_w.shape, fixed),
                pl.BlockSpec(bc_w.shape, fixed),
            ],
            out_specs=[pl.BlockSpec((rows, channels), row), pl.BlockSpec((1, packed, LANES), lambda i, me: (i ^ me[0], 0, 0))],
            scratch_shapes=[pltpu.VMEM((rows + 8, channels), F32), pltpu.VMEM((bc_w.shape[0], 2 * LANES), F32)],
        ),
        out_shape=[
            pltpu.HBM((tokens, channels), BF16),
            jax.ShapeDtypeStruct((runs, packed, LANES), BF16),
        ],
        compiler_params=pltpu.CompilerParams(dimension_semantics=("arbitrary",), vmem_limit_bytes=8 << 20),
        cost_estimate=SMALL,
    )(me, projected, offset, taps, shift, low_w, bc_w)


ROWS = [192]


def spread_mask(rows, states):
    width = SPAN * states
    row = lax.broadcasted_iota(jnp.int32, (rows, width), 0) % SPAN
    return row == lax.broadcasted_iota(jnp.int32, (rows, width), 1) // states


def tile_matrix(states):
    width = SPAN * states
    row = lax.broadcasted_iota(jnp.int32, (states, width), 0)
    return (row == lax.broadcasted_iota(jnp.int32, (states, width), 1) % states).astype(BF16)


def spread_columns(columns, rows, states):
    tiled = mm(columns[:, 0:rows].astype(BF16), tile_matrix(states), TN)
    return jnp.where(spread_mask(rows, states), tiled, 0.0).astype(BF16)


def forward_kernel(kept, me_ref, pack_ref, act_ref, gate_ref, offset_ref, dw_ref, bias_ref, rate_ref, skip_ref, h_in, *rest):
    pre_ref, y_ref, gated_ref, hist_ref, h_s, dtm_s, u_s = rest[kept:]
    states, channels = rate_ref.shape
    chunk = act_ref.shape[0]

    @pl.when(pl.program_id(0) == 0)
    def _():
        h_s[...] = h_in[...]

    low, bt, ct = read_packed(pack_ref, states)
    wide = bt.shape[1]
    pre = mm(low, dw_ref[...]) + bias_ref[...]
    pre_ref[...] = pre
    dt = softplus(pre)
    act = act_ref[...].astype(F32)
    u_s[...] = dt * act
    dtm_s[...] = jnp.where(offset_ref[...] == 0, FAR, dt)
    rate = rate_ref[...]

    def group(g, h):
        base = pl.multiple_of(g * STEP, STEP)
        bg = pltpu.roll(bt, wide - base, 1)
        dtm = dtm_s[pl.ds(base, STEP), :]
        u = u_s[pl.ds(base, STEP), :]
        for j in range(STEP):
            a = jnp.exp(dtm[j:j + 1, :] * rate)
            h = a * h + u[j:j + 1, :] * bg[:, j:j + 1]
            at = pl.multiple_of((base + j) * states, states)
            hist_ref[pl.ds(at, states), :] = h.astype(BF16)
        return h

    h_s[...] = lax.fori_loop(0, chunk // STEP, group, h_s[...])
    spread = spread_columns(ct, chunk, states)
    width = SPAN * states
    for g in range(chunk // SPAN):
        rows = slice(g * SPAN, (g + 1) * SPAN)
        y_ref[rows, :] = mm(spread[rows, :], hist_ref[g * width:(g + 1) * width, :])
    y = y_ref[...] + skip_ref[...] * act
    y_ref[...] = y
    gate = gate_ref[...].astype(F32)
    gated_ref[...] = (y * gate * sigmoid(gate)).astype(BF16)


def scan_forward(me, pack, act, projected, offset, delta_w, bias, rate, skip, held, whole, first, steps):
    tokens, channels = act.shape
    states = rate.shape[0]
    chunk = ROWS[0]
    row = lambda i, me: (first + i, 0)
    fixed = lambda i, me: (0, 0)
    done = steps * chunk
    return pl.pallas_call(
        functools.partial(forward_kernel, len(whole)),
        name="scan_forward",
        grid_spec=pltpu.PrefetchScalarGridSpec(
            num_scalar_prefetch=1,
            grid=(steps,),
            in_specs=[
                pl.BlockSpec((1,) + pack.shape[1:], lambda i, me: ((first + i) ^ me[0], 0, 0)),
                pl.BlockSpec((chunk, channels), row),
                pl.BlockSpec((chunk, channels), lambda i, me: (first + i, 1)),
                pl.BlockSpec((chunk, 1), row),
                pl.BlockSpec(delta_w.shape, fixed),
                pl.BlockSpec(bias.shape, fixed),
                pl.BlockSpec(rate.shape, fixed),
                pl.BlockSpec(skip.shape, fixed),
                pl.BlockSpec(rate.shape, fixed),
            ] + [pl.BlockSpec(memory_space=pl.ANY)] * len(whole),
            out_specs=[
                pl.BlockSpec((chunk, channels), row),
                pl.BlockSpec((chunk, channels), row),
                pl.BlockSpec((chunk, channels), row),
                pl.BlockSpec((chunk * states, channels), row),
                pl.BlockSpec(rate.shape, fixed),
            ],
            scratch_shapes=[
                pltpu.VMEM((chunk, channels), F32),
                pltpu.VMEM((chunk, channels), F32),
            ],
        ),
        out_shape=[
            pltpu.HBM((tokens, channels), F32),
            pltpu.HBM((tokens, channels), F32),
            jax.ShapeDtypeStruct((tokens, channels), BF16),
            pltpu.HBM((tokens * states, channels), BF16),
            jax.ShapeDtypeStruct(rate.shape, F32),
        ],
        input_output_aliases={10 + i: i for i in range(len(whole))},
        compiler_params=pltpu.CompilerParams(dimension_semantics=("arbitrary",), vmem_limit_bytes=16 << 20),
        cost_estimate=SMALL,
    )(me, pack, in_hbm(act), projected, offset, delta_w, bias, rate, skip, held, *(v if k == 2 else in_hbm(v) for k, v in enumerate(whole)))


def backward_kernel(kept, me_ref, pack_ref, pre_ref, act_ref, gate_ref, gg_ref, y_ref, offset_ref,
                    hist_ref, prior_ref, dw_ref, rate_ref, skip_ref, carry_in, rgrad_in, dwgrad_in, rows_in, *rest):
    (ggate_ref, gact_ref, part_ref, carry_s, rgrad_ref, dwgrad_ref, rows_ref,
     dtm_s, u_s, dt_s, gy_s, drive_s, decay_s, wide_s, adj_s, thr_s) = rest[kept:]
    states, channels = rate_ref.shape
    chunk = act_ref.shape[0]

    @pl.when(pl.program_id(0) == 0)
    def _():
        carry_s[...] = carry_in[...]
        rgrad_ref[...] = rgrad_in[...]
        dwgrad_ref[...] = dwgrad_in[...]
        rows_ref[...] = rows_in[...]

    low, bt, ct = read_packed(pack_ref, states)
    wide = bt.shape[1]
    pre = pre_ref[...]
    dt = softplus(pre)
    act = act_ref[...].astype(F32)
    dt_s[...] = dt
    u_s[...] = dt * act
    dtm_s[...] = jnp.where(offset_ref[...] == 0, FAR, dt)
    gate = gate_ref[...].astype(F32)
    sig = sigmoid(gate)
    gg = gg_ref[...].astype(F32) * sig
    gy = gg * gate
    gy_s[...] = gy
    ggate_ref[...] = (gg * y_ref[...] * (1.0 + gate * (1.0 - sig))).astype(BF16)
    rate = rate_ref[...]
    groups = chunk // STEP

    def group(k, held):
        carry, rgrad = held
        g = groups - 1 - k
        base = pl.multiple_of(g * STEP, STEP)
        cg = pltpu.roll(ct, wide - base, 1)
        dtm = dtm_s[pl.ds(base, STEP), :]
        dts = dt_s[pl.ds(base, STEP), :]
        gys = gy_s[pl.ds(base, STEP), :]
        for j in reversed(range(STEP)):
            if j > 0:
                at = pl.multiple_of((base + j - 1) * states, states)
                prior = hist_ref[pl.ds(at, states), :].astype(F32)
            else:
                at = pl.multiple_of(jnp.maximum(base - 1, 0) * states, states)
                prior = jnp.where(base == 0, prior_ref[...], hist_ref[pl.ds(at, states), :]).astype(F32)
            a = jnp.exp(dtm[j:j + 1, :] * rate)
            adj = cg[:, j:j + 1] * gys[j:j + 1, :] + carry
            carry = a * adj
            through = carry * prior
            rgrad = rgrad + through * dts[j:j + 1, :]
            at = pl.multiple_of((base + j) * states, states)
            adj_s[pl.ds(at, states), :] = adj.astype(BF16)
            thr_s[pl.ds(at, states), :] = (through * rate).astype(BF16)
        return carry, rgrad

    carry, rgrad = lax.fori_loop(0, groups, group, (carry_s[...], rgrad_ref[...]))
    carry_s[...] = carry
    rgrad_ref[...] = rgrad
    spread = spread_columns(bt, chunk, states)
    ones = jnp.where(spread_mask(SPAN, states), 1.0, 0.0).astype(BF16)
    width = SPAN * states
    ub = u_s[...].astype(BF16)
    gyb = gy.astype(BF16)
    ahead = (lax.broadcasted_iota(jnp.int32, (width, chunk), 1)
             - lax.broadcasted_iota(jnp.int32, (width, chunk), 0) // states)
    gb_all = jnp.zeros((width, chunk), F32)
    gc_all = jnp.zeros((width, chunk), F32)
    for g in range(chunk // SPAN):
        rows = slice(g * SPAN, (g + 1) * SPAN)
        adj = adj_s[g * width:(g + 1) * width, :]
        drive_s[rows, :] = mm(spread[rows, :], adj)
        decay_s[rows, :] = mm(ones, thr_s[g * width:(g + 1) * width, :])
        gb_all = jnp.where(ahead == g * SPAN, mm(adj, ub, NT), gb_all)
        gc_all = jnp.where(ahead == g * SPAN, mm(hist_ref[g * width:(g + 1) * width, :], gyb, NT), gc_all)
    tiles = tile_matrix(states)
    wide_s[0:states, 0:chunk] = mm(tiles, gb_all.astype(BF16))
    wide_s[states:2 * states, 0:chunk] = mm(tiles, gc_all.astype(BF16))
    drive = drive_s[...]
    gact_ref[...] = drive * dt + gy * skip_ref[...]
    gpre = ((drive * act + decay_s[...]) * sigmoid(pre)).astype(BF16)
    rows_ref[0:1, :] += jnp.sum(gy * act, axis=0, keepdims=True)
    rows_ref[1:2, :] += jnp.sum(gpre.astype(F32), axis=0, keepdims=True)
    dwgrad_ref[...] += mm(low, gpre, TN)
    write_packed(part_ref, mm(gpre, dw_ref[...], NT), wide_s)


def scan_backward(me, pack, pre, act, projected, gg, y, offset, hist, delta_w, rate, skip, held, whole, last, steps):
    tokens, channels = act.shape
    states = rate.shape[0]
    chunk = ROWS[0]
    row = lambda i, me: (last - i, 0)
    second = lambda i, me: (last - i, 1)
    run = lambda i, me: ((last - i) ^ me[0], 0, 0)
    fixed = lambda i, me: (0, 0)
    blocks = [pl.BlockSpec((chunk, channels), second), pl.BlockSpec((chunk, channels), row), pl.BlockSpec((1,) + pack.shape[1:], run)]
    shapes = [
        jax.ShapeDtypeStruct((tokens, 2 * channels), BF16),
        pltpu.HBM((tokens, channels), F32),
        jax.ShapeDtypeStruct(pack.shape, BF16),
    ]
    sums = [pl.BlockSpec(v.shape, fixed) for v in held]
    done = steps * chunk
    return pl.pallas_call(
        functools.partial(backward_kernel, len(whole)),
        name="scan_backward",
        grid_spec=pltpu.PrefetchScalarGridSpec(
            num_scalar_prefetch=1,
            grid=(steps,),
            in_specs=[
                pl.BlockSpec((1,) + pack.shape[1:], run),
                pl.BlockSpec((chunk, channels), row),
                pl.BlockSpec((chunk, channels), row),
                pl.BlockSpec((chunk, channels), second),
                pl.BlockSpec((chunk, channels), row),
                pl.BlockSpec((chunk, channels), row),
                pl.BlockSpec((chunk, 1), row),
                pl.BlockSpec((chunk * states, channels), row),
                pl.BlockSpec((states, channels), lambda i, me: (jnp.maximum((last - i) * chunk - 1, 0), 0)),
                pl.BlockSpec(delta_w.shape, fixed),
                pl.BlockSpec(rate.shape, fixed),
                pl.BlockSpec(skip.shape, fixed),
            ] + sums + [pl.BlockSpec(memory_space=pl.ANY)] * len(whole),
            out_specs=blocks + sums,
            scratch_shapes=[pltpu.VMEM((chunk, channels), F32)] * 6
            + [pltpu.VMEM((2 * states, 2 * LANES), F32)]
            + [pltpu.VMEM((chunk * states, channels), BF16)] * 2,
        ),
        out_shape=shapes + [jax.ShapeDtypeStruct(v.shape, F32) for v in held],
        input_output_aliases={17 + i: i for i in range(len(whole))},
        compiler_params=pltpu.CompilerParams(dimension_semantics=("arbitrary",), vmem_limit_bytes=24 << 20),
        cost_estimate=SMALL,
    )(me, pack, in_hbm(pre), in_hbm(act), projected, gg, in_hbm(y), offset, in_hbm(hist), in_hbm(hist), delta_w, rate, skip, *held, *(in_hbm(v) if k == 1 else v for k, v in enumerate(whole)))


def end_kernel(me_ref, pack_ref, gact_ref, act_ref, inner_ref, prior_ref, offset_ref, taps_ref, shift_ref, low_ref, bc_ref, grad_ref,
               ginner_ref, tapg_ref, selow_ref, selbc_ref, ext_s, after_s, wide_s):
    rows, channels = inner_ref.shape
    taps = taps_ref.shape[0]
    states = bc_ref.shape[0] // 2

    @pl.when(pl.program_id(0) == 0)
    def _():
        after_s[...] = jnp.zeros_like(after_s)
        tapg_ref[...] = jnp.zeros_like(tapg_ref)
        selow_ref[...] = jnp.zeros_like(selow_ref)
        selbc_ref[...] = jnp.zeros_like(selbc_ref)

    low, gbt, gct = read_packed(pack_ref, states)
    wide_s[0:states, :] = gbt
    wide_s[states:2 * states, :] = gct
    gbc = wide_s[:, 0:rows].astype(BF16)
    act = act_ref[...]
    selow_ref[...] += mm(act, low, TN)
    selbc_ref[...] += mm(gbc, act)
    gact = gact_ref[...] + mm(low, low_ref[...], NT) + mm(gbc, bc_ref[...], TN)
    before = prior_ref.shape[0]
    ext_s[0:before, :] = prior_ref[...].astype(F32)
    ext_s[before:before + rows, :] = inner_ref[...].astype(F32)
    offset = offset_ref[...]
    conv = shift_ref[...] + taps_ref[0:1, :] * ext_s[before:before + rows, :]
    for k in range(1, taps):
        conv += jnp.where(offset >= k, taps_ref[k:k + 1, :], 0.0) * ext_s[pl.ds(before - k, rows), :]
    q = sigmoid(conv)
    gconv = gact * q * (1.0 + conv * (1.0 - q))
    tapg_ref[taps:taps + 1, :] += jnp.sum(gconv, axis=0, keepdims=True)
    tapg_ref[0:1, :] += jnp.sum(gconv * ext_s[before:before + rows, :], axis=0, keepdims=True)
    ginner = gconv * taps_ref[0:1, :]
    for k in range(1, taps):
        masked = jnp.where(offset >= k, gconv, 0.0)
        tapg_ref[k:k + 1, :] += jnp.sum(masked * ext_s[pl.ds(before - k, rows), :], axis=0, keepdims=True)
        after_s[k - 1, rows:rows + 8, :] = after_s[k - 1, 0:8, :]
        after_s[k - 1, 0:rows, :] = masked * taps_ref[k:k + 1, :]
        ginner += after_s[k - 1, pl.ds(k, rows), :]
    ginner_ref[...] = ginner.astype(BF16)


def end(me, pack, gact, act, projected, offset, taps, shift, low_w, bc_w, grad_projected):
    tokens, channels = act.shape
    rows = ROWS[0]
    steps = tokens // rows
    row = lambda i, me: (steps - 1 - i, 0)
    fixed = lambda i, me: (0, 0)
    return pl.pallas_call(
        end_kernel,
        name="end",
        grid_spec=pltpu.PrefetchScalarGridSpec(
            num_scalar_prefetch=1,
            grid=(steps,),
            in_specs=[
                pl.BlockSpec((1,) + pack.shape[1:], lambda i, me: ((steps - 1 - i) ^ me[0], 0, 0)),
                pl.BlockSpec((rows, channels), row),
                pl.BlockSpec((rows, channels), row),
                pl.BlockSpec((rows, channels), row),
                pl.BlockSpec((16, channels), lambda i, me: (jnp.maximum((steps - 1 - i) * (rows // 16) - 1, 0), 0)),
                pl.BlockSpec((rows, 1), row),
                pl.BlockSpec(taps.shape, fixed),
                pl.BlockSpec(shift.shape, fixed),
                pl.BlockSpec(low_w.shape, fixed),
                pl.BlockSpec(bc_w.shape, fixed),
                pl.BlockSpec(memory_space=pl.ANY),
            ],
            out_specs=[
                pl.BlockSpec((rows, channels), row),
                pl.BlockSpec((8, channels), fixed),
                pl.BlockSpec(low_w.shape, fixed),
                pl.BlockSpec(bc_w.shape, fixed),
            ],
            scratch_shapes=[
                pltpu.VMEM((rows + 16, channels), F32),
                pltpu.VMEM((3, rows + 8, channels), F32),
                pltpu.VMEM((bc_w.shape[0], 2 * LANES), F32),
            ],
        ),
        out_shape=[
            jax.ShapeDtypeStruct(grad_projected.shape, BF16),
            jax.ShapeDtypeStruct((8, channels), F32),
            jax.ShapeDtypeStruct(low_w.shape, F32),
            jax.ShapeDtypeStruct(bc_w.shape, F32),
        ],
        input_output_aliases={11: 0},
        compiler_params=pltpu.CompilerParams(dimension_semantics=("arbitrary",), vmem_limit_bytes=14 << 20),
        cost_estimate=SMALL,
    )(me, pack, in_hbm(gact), in_hbm(act), projected, projected, offset, taps, shift, low_w, bc_w, grad_projected)


def weight_grad_kernel(count, turned, table_ref, *refs):
    a_refs, b_refs = refs[:count], refs[count:2 * count]
    out_ref, a_s, b_s = refs[2 * count:]
    rows = a_refs[0].shape[0]
    for s in range(count):
        a_s[s * rows:(s + 1) * rows, :] = a_refs[s][...]

    @pl.when(pl.program_id(0) == 0)
    def _():
        for s in range(count):
            b_s[s * rows:(s + 1) * rows, :] = b_refs[s][...]

    first, second = (b_s, a_s) if turned else (a_s, b_s)
    out_ref[0] = mm(first[...], second[...], TN).astype(BF16)


def weight_grad(table, distances, shards, b, column, channels, size, turned):
    rows, width = shards[0].shape
    block = width // size
    count = len(shards)
    shape = (1, channels, block) if turned else (1, block, channels)
    return pl.pallas_call(
        functools.partial(weight_grad_kernel, count, turned),
        name="weight_grad",
        grid_spec=pltpu.PrefetchScalarGridSpec(
            num_scalar_prefetch=1,
            grid=(size,),
            in_specs=[pl.BlockSpec((rows, block), lambda i, table: (0, i))] * count
            + [pl.BlockSpec((rows, channels), lambda i, table, d=d: (table[d], column)) for d in distances],
            out_specs=pl.BlockSpec(shape, lambda i, table: (i, 0, 0)),
            scratch_shapes=[pltpu.VMEM((rows * count, block), BF16), pltpu.VMEM((rows * count, channels), BF16)],
        ),
        out_shape=jax.ShapeDtypeStruct((size,) + shape[1:], BF16),
        compiler_params=pltpu.CompilerParams(dimension_semantics=("arbitrary",), vmem_limit_bytes=16 << 20),
        cost_estimate=SMALL,
    )(table, *shards, *([b] * count))


def weight_block(weight, dims, blocks):
    if dims[0][1] == (0,):
        columns = weight.shape[1] // blocks
        return pl.BlockSpec((weight.shape[0], columns), lambda i, *rest: (0, i)), columns
    columns = weight.shape[0] // blocks
    return pl.BlockSpec((columns, weight.shape[1]), lambda i, *rest: (i, 0)), columns


def placed_kernel(dims, count, table_ref, *refs):
    w_ref, out_ref = refs[count], refs[-1]
    for s in range(count):
        @pl.when(pl.program_id(1) == s)
        def _(s=s):
            out_ref[...] = mm(refs[s][...], w_ref[...], dims).astype(out_ref.dtype)


def pick_entry(values, i):
    chosen = values[0]
    for k in range(1, len(values)):
        chosen = jnp.where(i == k, values[k], chosen)
    return chosen


def placed_product(table, distances, shards, weight, dims, out):
    rows, width = shards[0].shape
    count, blocks = len(shards), 2
    spec, columns = weight_block(weight, dims, blocks)
    return pl.pallas_call(
        functools.partial(placed_kernel, dims, count),
        name="placed_product",
        grid_spec=pltpu.PrefetchScalarGridSpec(
            num_scalar_prefetch=1,
            grid=(blocks, count),
            in_specs=[pl.BlockSpec((rows, width), lambda i, k, table: (0, 0))] * count
            + [spec, pl.BlockSpec(memory_space=pl.ANY)],
            out_specs=pl.BlockSpec((rows, columns), lambda i, k, table: (pick_entry([table[d] for d in distances], k), i)),
        ),
        out_shape=jax.ShapeDtypeStruct(out.shape, out.dtype),
        input_output_aliases={count + 2: 0},
        compiler_params=pltpu.CompilerParams(dimension_semantics=("arbitrary", "arbitrary"), vmem_limit_bytes=16 << 20),
        cost_estimate=SMALL,
    )(table, *shards, weight, out)


def far_kernel(dims, distances, table_ref, g_ref, w_ref, ahead_ref, behind_ref):
    total = mm(rows_at(g_ref, table_ref, distances[0]), w_ref[...], dims).astype(BF16)
    half = total.shape[1] // 2
    ahead_ref[...] = total[:, :half]
    behind_ref[...] = total[:, half:]


def pair_kernel(dims, distances, table_ref, g_ref, w_ref, ra_ref, rb_ref, ahead_ref, behind_ref):
    width, part = ahead_ref.shape[1], ra_ref.shape[1]
    ahead = mm(rows_at(g_ref, table_ref, distances[0]), w_ref[...], dims)
    behind = mm(rows_at(g_ref, table_ref, distances[1]), w_ref[...], dims)
    ahead_ref[:, :part] = (ahead[:, :part] + ra_ref[...].astype(F32)).astype(BF16)
    behind_ref[:, width - part:] = (behind[:, width - part:] + rb_ref[...].astype(F32)).astype(BF16)
    if part < width:
        ahead_ref[:, part:] = ahead[:, part:].astype(BF16)
        behind_ref[:, :width - part] = behind[:, :width - part].astype(BF16)


def own_kernel(dims, distances, table_ref, g_ref, w_ref, ra_ref, rb_ref, place_ref, out_ref):
    total = mm(rows_at(g_ref, table_ref, distances[0]), w_ref[...], dims)
    total = total + ra_ref[...].astype(F32) + rb_ref[...].astype(F32)
    out_ref[...] = mm(place_ref[...], total.astype(BF16)).astype(BF16)


def rows_at(g_ref, table_ref, distance):
    rows = ROWS[0]
    return g_ref[pl.ds(pl.multiple_of(table_ref[distance] * rows, rows), rows), :]


def ring_step(kernel, dims, table, distances, g, weight, extra, widths):
    rows = ROWS[0]
    vm = pl.BlockSpec(memory_space=pltpu.VMEM)
    return pl.pallas_call(
        functools.partial(kernel, dims, distances),
        name=kernel.__name__,
        in_specs=[pl.BlockSpec(memory_space=pltpu.SMEM)] + [vm] * (2 + len(extra)),
        out_specs=[vm] * len(widths),
        out_shape=[jax.ShapeDtypeStruct((rows, w), BF16) for w in widths],
        compiler_params=pltpu.CompilerParams(vmem_limit_bytes=16 << 20),
        cost_estimate=SMALL,
    )(table, g, weight, *extra)


def in_hbm(value):
    return pltpu.with_memory_space_constraint(value, pltpu.HBM)


def add_kernel(ra_rows, rb_rows, ta_ref, tb_ref, ahead_ref, behind_ref):
    width, part = ahead_ref.shape[1], ra_rows.shape[1]
    ahead_ref[:, :part] = (ta_ref[:, :part].astype(F32) + ra_rows[...].astype(F32)).astype(BF16)
    behind_ref[:, width - part:] = (tb_ref[:, width - part:].astype(F32) + rb_rows[...].astype(F32)).astype(BF16)
    if part < width:
        ahead_ref[:, part:] = ta_ref[:, part:]
        behind_ref[:, :width - part] = tb_ref[:, :width - part]


def add_pair(arrived, terms):
    vm = pl.BlockSpec(memory_space=pltpu.VMEM)
    return pl.pallas_call(
        add_kernel, name="add_pair", in_specs=[vm] * 4, out_specs=[vm] * 2,
        out_shape=[jax.ShapeDtypeStruct(v.shape, v.dtype) for v in terms],
        compiler_params=pltpu.CompilerParams(vmem_limit_bytes=8 << 20),
        cost_estimate=SMALL,
    )(*arrived, *terms)


def blank(*shapes):
    hbm = pl.BlockSpec(memory_space=pl.ANY)
    return pl.pallas_call(
        lambda *refs: None, name="blank", out_specs=[hbm] * len(shapes),
        out_shape=[jax.ShapeDtypeStruct(*v) for v in shapes],
        cost_estimate=SMALL)()


def deal_kernel(x_ref, cot_ref, order_ref, gain_ref, me_ref, sendx_ref, sendc_ref, pick_ref, place_ref):
    rows = x_ref.shape[0]
    dp_size = order_ref.shape[0]
    me = me_ref[0]
    group_tokens = me_ref[1]
    pair = rows // dp_size
    order = order_ref[...].astype(jnp.int32)
    near = lax.broadcasted_iota(jnp.int32, (dp_size, rows), 0)
    other = near ^ me
    source = order // group_tokens
    local = order % rows
    before = (
        lax.broadcasted_iota(jnp.int32, (rows, rows), 0) < lax.broadcasted_iota(jnp.int32, (rows, rows), 1)
    ).astype(BF16)
    slots = lax.broadcasted_iota(jnp.int32, (rows, rows), 0)
    chosen = source == me
    rank = mm(chosen.astype(BF16), before).astype(jnp.int32)
    slot = jnp.where(chosen, near * pair + rank, -1)
    pick = jnp.zeros((rows, rows), F32)
    for d in range(dp_size):
        pick += mm((slots == slot[d:d + 1, :]).astype(BF16), (slots == local[d:d + 1, :]).astype(BF16), NT)
    pick = pick.astype(BF16)
    pick_ref[...] = pick
    mine = source[0:1, :]
    held = (mine == other).astype(BF16)
    ranks = mm(held, before).astype(jnp.int32)
    arrived = jnp.sum(jnp.where(mine == other, near * pair + ranks, 0), axis=0, keepdims=True)
    place_ref[...] = (slots == arrived).astype(BF16)
    x = x_ref[...].astype(F32)
    rinv = lax.rsqrt(jnp.mean(x * x, axis=1, keepdims=True) + EPSILON)
    normed = (x * rinv * gain_ref[...]).astype(BF16)
    sendx_ref[...] = mm(pick, normed).astype(BF16)
    sendc_ref[...] = mm(pick, cot_ref[...]).astype(BF16)


def deal(x, cot, order, gain, me):
    rows, width = x.shape
    vm = pl.BlockSpec(memory_space=pltpu.VMEM)
    return pl.pallas_call(
        deal_kernel,
        name="deal",
        in_specs=[vm, vm, vm, vm, pl.BlockSpec(memory_space=pltpu.SMEM)],
        out_specs=[vm] * 4,
        out_shape=[
            jax.ShapeDtypeStruct((rows, width), BF16),
            jax.ShapeDtypeStruct((rows, width), BF16),
            jax.ShapeDtypeStruct((rows, rows), BF16),
            jax.ShapeDtypeStruct((rows, rows), BF16),
        ],
        compiler_params=pltpu.CompilerParams(vmem_limit_bytes=32 << 20),
        cost_estimate=SMALL,
    )(x, cot, order, gain, me)


def round_dot(a, b, dims=(((1,), (0,)), ((), ()))):
    return mm(a, b, dims).astype(BF16)


def after(value, *earlier):
    return lax.optimization_barrier((value,) + earlier)[0]


def flip(value, axis, bit):
    return lax.ppermute(value, axis, [(i, i ^ bit) for i in range(lax.axis_size(axis))])


def exchange(pieces, axis, stack=True):
    pieces = [pieces[0]] + [flip(pieces[d], axis, d) for d in range(1, lax.axis_size(axis))]
    return jnp.stack(pieces) if stack else pieces


def swap(values, axis):
    return lax.all_to_all(values, axis, split_axis=0, concat_axis=0, tiled=True)


def share(value, axis):
    return exchange([value] * lax.axis_size(axis), axis)


def in_order(pieces, axis):
    size, me, bit = lax.axis_size(axis), lax.axis_index(axis), 1
    while bit < size:
        split = pieces.reshape((size // (2 * bit), 2, bit) + pieces.shape[1:])
        turned = jnp.concatenate([split[:, 1:], split[:, :1]], axis=1)
        pieces = jnp.where((me // bit) % 2 == 1, turned, split).reshape(pieces.shape)
        bit *= 2
    return pieces


def cube_sum(value, axis, bit, end_bit):
    while bit < end_bit:
        value = value + flip(value, axis, bit)
        bit *= 2
    return value


class Bag(dict):
    def meet(self, values, *names):
        values, held = lax.optimization_barrier((values, {n: self[n] for n in names}))
        self.update(held)
        return values


def add_up(pieces):
    return jnp.sum(pieces.astype(F32), axis=0)


class Ring:
    def __init__(self, axis):
        self.axis = axis
        self.size = size = lax.axis_size(axis)
        columns = max(c for c in range(1, size) if size % c == 0 and c * c <= size)
        rows = size // columns
        cycle = [(0, c) for c in range(columns)]
        for r in range(1, rows):
            snake = range(1, columns)
            cycle += [(r, c) for c in (snake if r % 2 == 0 else reversed(snake))]
        cycle += [(r, 0) for r in reversed(range(1, rows))]
        order = [r * columns + c for r, c in cycle]
        place = {t: i for i, t in enumerate(order)}
        table = jnp.array([[order[(place[t] + d) % size] for d in range(size)] for t in range(size)], jnp.int32)
        self.at = lax.dynamic_index_in_dim(table, lax.axis_index(axis), 0, keepdims=False)
        self.forward = [(order[i], order[(i + 1) % size]) for i in range(size)]
        self.backward = [(b, a) for a, b in self.forward]

    def hop(self, value, ahead):
        return lax.ppermute(value, self.axis, self.forward if ahead else self.backward)


def ring_gather(ring, own, between):
    half, size = ring.size // 2, ring.size
    middle = own.shape[1] // 2
    distances, shards = [0], [own]
    ahead = behind = own
    for d in range(1, half):
        ahead, behind = between(d, ring.hop(ahead, True), ring.hop(behind, False))
        distances += [size - d, d]
        shards += [ahead, behind]
    first, second = between(half, ring.hop(ahead[:, :middle], True), ring.hop(behind[:, middle:], False))
    return distances + [half], shards + [jnp.concatenate([first, second], axis=1)]


def ring_scatter(ring, dims, g, weight, width, between):
    half, size = ring.size // 2, ring.size
    ahead, behind = ring_step(far_kernel, dims, ring.at, [half], g, weight, [], [width // 2] * 2)
    for d in range(half, 0, -1):
        ahead, behind = between(half - d, ring.hop(ahead, True), ring.hop(behind, False))
        if d > 1:
            ahead, behind = ring_step(
                pair_kernel, dims, ring.at, [d - 1, size + 1 - d], g, weight, [ahead, behind], [width] * 2)
    return ahead, behind


def ring_finish(ring, dims, g, weight, width, ahead, behind, place):
    return ring_step(own_kernel, dims, ring.at, [0], g, weight, [ahead, behind, place], [width])[0]


def ring_reduce(ring, partial, between):
    half, size = ring.size // 2, ring.size
    far = partial(half)
    middle = far.shape[1] // 2
    ahead, behind = far[:, :middle], far[:, middle:]
    for d in range(half, 0, -1):
        terms = [partial(d - 1, ahead), partial(size + 1 - d, ahead)] if d > 1 else [partial(0, ahead)]
        arrived = (ring.hop(ahead, True), ring.hop(behind, False))
        ahead, behind, *terms = between(half - d, far, arrived, terms)
        if d > 1:
            ahead, behind = add_pair((ahead, behind), terms)
    return (ahead.astype(F32) + behind.astype(F32) + terms[0].astype(F32)).astype(BF16)


def shards(
    block_input, norm_gain, in_weight, conv_weight, conv_bias, select_weight, delta_weight, delta_bias,
    decay_log, skip_weight, out_weight, out_cotangent, seq_lengths, deal_order,
):
    rows_dev, width = block_input.shape
    dp_size = lax.axis_size("dp")
    tensor_size = lax.axis_size("tensor")
    pair = rows_dev // dp_size
    group_tokens = rows_dev * tensor_size
    ring = Ring("tensor")
    here = jnp.zeros((1,), jnp.int32)
    me = jnp.stack([lax.axis_index("dp"), jnp.int32(group_tokens)]).astype(jnp.int32)
    head = share(jnp.concatenate([deal_order.astype(F32), norm_gain.astype(F32)]), "dp")
    gain_values = in_order(head[:, rows_dev:], "dp").reshape(1, -1)
    send_rows, send_cot, pick, place = deal(block_input, out_cotangent, head[:, :rows_dev], gain_values, me)
    in_cat = jnp.swapaxes(after(in_weight, send_rows), 0, 1).reshape(in_weight.shape[1], -1)
    recv_rows = exchange(send_rows.reshape(dp_size, pair, -1), "dp")
    recv_rows, in_cat = lax.optimization_barrier((recv_rows, in_cat))
    in_full = lax.all_gather(in_cat, "dp", axis=0, tiled=True)
    out_own = after(out_weight, in_full)
    out_full = lax.all_gather(out_own, "dp", axis=1, tiled=True)
    normed = round_dot(place, recv_rows.reshape(rows_dev, -1), TN)
    channels = in_full.shape[1] // 2
    taps = conv_weight.shape[0]
    lane_width = conv_bias.shape[1] * dp_size
    own_states = decay_log.shape[1]
    states, low_rank = own_states * dp_size, delta_weight.shape[0] * dp_size
    lengths_row = seq_lengths[0]
    seq_ends = jnp.cumsum(lengths_row)
    begins = seq_ends - lengths_row
    positions = jnp.arange(group_tokens, dtype=jnp.int32)
    inside = (positions[:, None] >= begins[None, :]) & (positions[:, None] < seq_ends[None, :])
    offset = (positions - jnp.sum(jnp.where(inside, begins[None, :], 0), axis=1))[:, None]
    projected, gg = blank(((group_tokens, 2 * channels), BF16), ((group_tokens, channels), F32))
    half = tensor_size // 2
    NN = (((1,), (0,)), ((), ()))
    lanes_own = jnp.concatenate([conv_weight, jnp.stack([conv_bias, delta_bias, skip_weight])])
    bag = Bag(
        cot=send_cot, select=jnp.concatenate([select_weight, jnp.moveaxis(lanes_own, 0, 2)], axis=2),
        thin=jnp.concatenate([decay_log.T, delta_weight]), projected=projected)
    waiting = {"shards": [normed], "distances": [0]}

    def during_normed(d, ahead, behind):
        if d == 1:
            ahead, behind = bag.meet((ahead, behind), "cot")
            bag["cot"] = exchange(bag["cot"].reshape(dp_size, pair, -1), "dp")
        elif d >= half - 1:
            if d == half - 1:
                bag["select"] = lax.all_gather(after(bag["select"], bag["projected"]), "dp", axis=1, tiled=True)
            bag["projected"] = placed_product(
                ring.at, waiting["distances"], waiting["shards"], in_full, NN, bag["projected"])
            waiting["shards"], waiting["distances"] = [], []
            ahead, behind = bag.meet((ahead, behind), "projected", "select", *(["cot"] if d == half else []))
        if d < half:
            waiting["distances"] += [tensor_size - d, d]
            waiting["shards"] += [ahead, behind]
        return ahead, behind

    distances, normed_shards = ring_gather(ring, normed, during_normed)

    def rows_of(values, distance):
        return lax.dynamic_slice(values, (ring.at[distance] * rows_dev, 0), (rows_dev, values.shape[1]))

    def put_rows(values, distance, rows):
        return lax.dynamic_update_slice(values, rows, (ring.at[distance] * rows_dev, 0))

    projected = put_rows(bag["projected"], distances[-1], round_dot(normed_shards[-1], in_full))
    dealt_cot = round_dot(place, bag["cot"].reshape(rows_dev, -1), TN)
    select_matrix = bag["select"].reshape(channels, -1)
    low_w, bc_w = select_matrix[:, :low_rank], select_matrix[:, low_rank:low_rank + 2 * states].T
    lanes_float = select_matrix[:, low_rank + 2 * states:].astype(F32).T
    conv_taps = lanes_float[:taps]
    conv_shift, delta_shift, skip_values = (lanes_float[taps + i:taps + i + 1] for i in range(3))
    activated, part = front(here, projected, offset, conv_taps, conv_shift, low_w, bc_w)
    scan = {"held": jnp.zeros((states, channels), F32), "whole": []}
    cots = {"shards": [dealt_cot], "distances": [0], "gg": gg}

    def forward_part(first, steps):
        result = scan_forward(
            here, scan["pack"], activated, projected, offset, delta_full, delta_shift, decay_rate, skip_values,
            scan["held"], scan["whole"], first, steps)
        scan["whole"], scan["held"] = list(result[:4]), result[4]

    def flush():
        for distance, shard in zip(cots["distances"], cots["shards"]):
            cots["gg"] = put_rows(cots["gg"], distance, mm(shard, out_full, NT))
        cots["shards"], cots["distances"] = [], []

    bag["thin"] = lax.all_gather(after(bag["thin"], part)[None], "dp", axis=0, tiled=True)
    arrived = bag.meet(swap(part, "tensor"), "thin")
    decay_full = bag["thin"][:, :own_states].reshape(states, channels)
    delta_full = bag["thin"][:, own_states:].reshape(low_rank, channels)
    decay_rate = -jnp.exp(decay_full.astype(F32))
    total = jnp.sum(arrived.astype(F32), axis=0).astype(BF16)
    scan["pack"] = swap(jnp.broadcast_to(total[None], part.shape), "tensor")

    def during_cot(d, ahead, behind):
        if d == 1:
            flush()
            scan["pack"], cots["gg"] = lax.optimization_barrier((scan["pack"], cots["gg"]))
        if d in (half - 2, half - 1):
            flush()
            forward_part((d - half + 2) * half, half)
            (ahead, behind), (scan["held"], scan["whole"][2], cots["gg"]) = lax.optimization_barrier(
                ((ahead, behind), (scan["held"], scan["whole"][2], cots["gg"])))
        if d == half:
            flush()
            ahead, behind, cots["gg"] = lax.optimization_barrier((ahead, behind, cots["gg"]))
        if d < half:
            cots["distances"] += [tensor_size - d, d]
            cots["shards"] += [ahead, behind]
        return ahead, behind

    cot_distances, cot_shards = ring_gather(ring, dealt_cot, during_cot)
    gg = put_rows(cots["gg"], cot_distances[-1], mm(cot_shards[-1], out_full, NT))
    pre, y, gated, hist = scan["whole"]
    held = [
        jnp.zeros((states, channels), F32),
        jnp.zeros((states, channels), F32),
        jnp.zeros((low_rank, channels), F32),
        jnp.zeros((8, channels), F32),
    ]
    state = {"held": held, "whole": []}
    steps = tensor_size // half

    def back_part(k, ahead, behind):
        result = scan_backward(
            here, pack_all, pre, activated, projected, gg, y, offset, hist, delta_full, decay_rate, skip_values,
            state["held"], state["whole"], tensor_size - 1 - k * steps, steps)
        (ahead, behind), result = lax.optimization_barrier(((ahead, behind), list(result)))
        state["whole"], state["held"] = result[:3], result[3:]
        return ahead, behind

    pack_all = scan["pack"]
    mixed = ring_scatter(ring, NN, gated, out_full, width, back_part)
    grad_projected, grad_act, grad_part = state["whole"]
    unused_carry, rate_grad, delta_weight_grad, row_grads = state["held"]
    decay_grad = rate_grad * decay_rate
    def by_lane(values):
        lanes = values.reshape(-1, channels // lane_width, dp_size, lane_width // dp_size)
        return jnp.moveaxis(lanes, 2, 0).reshape(dp_size, -1)

    def pack_small(taps_sum, low_sum, bc_sum):
        select_grad = jnp.concatenate([low_sum, bc_sum.T], axis=1)
        parts = [
            by_lane(jnp.concatenate([taps_sum[:taps + 1], row_grads[:2]])),
            decay_grad.reshape(dp_size, -1),
            delta_weight_grad.reshape(dp_size, -1),
            jnp.moveaxis(select_grad.reshape(channels // lane_width, dp_size, -1), 1, 0).reshape(dp_size, -1),
        ]
        flat = jnp.concatenate(parts, axis=1)
        fill = -flat.shape[1] % 2048
        flat = jnp.pad(flat, ((0, 0), (0, fill))).astype(BF16).reshape(dp_size, -1, LANES)
        return flat, [part.shape[1] for part in parts]

    bag["out"] = weight_grad(
        ring.at, cot_distances, cot_shards, after(gated, grad_part), 0, channels, dp_size, True)
    arrived = bag.meet(swap(grad_part, "tensor"), "out")
    grad_total = jnp.sum(arrived.astype(F32), axis=0).astype(BF16)
    bag["gate"] = weight_grad(
        ring.at, distances, normed_shards, after(grad_projected, grad_total), 1, channels, dp_size, False)
    bag["out"] = lax.psum_scatter(after(bag["out"], grad_total), "dp", scatter_dimension=0, tiled=True)
    bag["mixed"] = ring_finish(
        ring, NN, gated, out_full, width, after(mixed[0], grad_total), mixed[1], place)
    grad_pack = bag.meet(swap(jnp.broadcast_to(grad_total[None], grad_part.shape), "tensor"), "gate", "mixed")
    bag["gate"] = lax.psum_scatter(bag["gate"], "dp", scatter_dimension=0, tiled=True)
    grad_projected, *bag["sums"] = end(
        here, grad_pack, grad_act, activated, projected, offset, conv_taps, conv_shift, low_w, bc_w, grad_projected)

    def during_grad(k, sent, arrived, terms):
        if k == 0:
            names = ["mixed", "sums"]
        elif k == half - 2:
            names = ["mixed", "flat", "gate", "out"]
        elif k == half - 1:
            bag["in"] = jnp.concatenate([bag["inner"], bag["gate"]]).astype(F32)
            bag["gain"] = cube_sum(jnp.sum(in_weight.astype(F32) * bag["in"], axis=(0, 2)), "tensor", 1, 2)
            names = ["gain", "inner"]
        else:
            names = ["mixed", "sums"]
        bag["arrived"], bag["terms"] = arrived, terms
        bag.meet((), "arrived", "terms", *names)
        if k == 0:
            bag["mixed"] = exchange(bag["mixed"].reshape(dp_size, pair, -1), "dp")
        if k == 1:
            flat, waiting["sizes"] = pack_small(*bag["sums"])
            bag["flat"] = swap(flat, "dp")
        return (*bag["arrived"], *bag["terms"])

    def grad_term(distance, earlier=None):
        rows = grad_projected if earlier is None else after(grad_projected, earlier)
        if distance == half - 1:
            bag["inner"] = weight_grad(ring.at, distances, normed_shards, rows, 0, channels, dp_size, False)
            rows = after(rows, bag["inner"])
            bag["inner"] = lax.psum_scatter(bag["inner"], "dp", scatter_dimension=0, tiled=True)
        return round_dot(rows_of(rows, distance), in_full, NT)

    grad_rows = ring_reduce(ring, grad_term, during_grad)
    send_grad = round_dot(place, grad_rows)
    home_grad = exchange(send_grad.reshape(dp_size, pair, -1), "dp").reshape(rows_dev, -1)
    home_out = bag["mixed"].reshape(rows_dev, -1)
    out_grad = bag["out"][0].astype(F32)
    in_weight_grad = bag["in"]
    gain_grad = cube_sum(after(bag["gain"], send_grad), "tensor", 2, tensor_size) / norm_gain.astype(F32)
    flat = jnp.sum(bag["flat"].astype(F32), axis=0).reshape(-1)
    small, start = [], 0
    for size in waiting["sizes"]:
        small.append(flat[start:start + size])
        start += size
    lane_grads = small[0].reshape((taps + 3,) + conv_bias.shape)
    rows_float = block_input.astype(F32)
    block_output = (rows_float + mm(pick, home_out, TN)).astype(BF16)
    inverse_rms = lax.rsqrt(jnp.mean(rows_float * rows_float, axis=1, keepdims=True) + EPSILON)
    unit_rows = rows_float * inverse_rms
    scaled = mm(pick, home_grad, TN) * gain_values
    input_grad = (
        out_cotangent.astype(F32)
        + inverse_rms * (scaled - unit_rows * jnp.mean(scaled * unit_rows, axis=1, keepdims=True))
    ).astype(BF16)
    return (
        block_output,
        input_grad,
        gain_grad,
        in_weight_grad,
        lane_grads[:taps],
        lane_grads[taps],
        small[3].reshape(select_weight.shape),
        small[2].reshape(delta_weight.shape),
        lane_grads[taps + 2],
        small[1].reshape(decay_log.shape[1], decay_log.shape[0]).T,
        lane_grads[taps + 1],
        out_grad,
    )


def solution(mesh):
    return jax.shard_map(
        shards,
        mesh=mesh,
        in_specs=(
            P(("dp", "tensor"), None),
            P("dp"),
            P(None, "dp", "tensor"),
            P(None, "tensor", "dp"),
            P("tensor", "dp"),
            P("tensor", "dp", None),
            P("dp", "tensor"),
            P("tensor", "dp"),
            P("tensor", "dp"),
            P("tensor", "dp"),
            P("tensor", "dp"),
            P(("dp", "tensor"), None),
            P("dp", None),
            P(("dp", "tensor")),
        ),
        out_specs=(
            P(("dp", "tensor"), None),
            P(("dp", "tensor"), None),
            P("dp"),
            P(None, "dp", "tensor"),
            P(None, "tensor", "dp"),
            P("tensor", "dp"),
            P("tensor", "dp", None),
            P("dp", "tensor"),
            P("tensor", "dp"),
            P("tensor", "dp"),
            P("tensor", "dp"),
            P("tensor", "dp"),
        ),
        check_vma=False,
    )
```

```python
import functools

import jax
import jax.numpy as jnp
from jax import lax
from jax.experimental import pallas as pl
from jax.experimental.pallas import tpu as pltpu
from jax.sharding import PartitionSpec as P

EPSILON = 1e-05
FAR = 1e30
LANES = 128
STEP = 48
SPAN = 16
SMALL = pl.CostEstimate(flops=1, transcendentals=0, bytes_accessed=1)
NT = (((1,), (1,)), ((), ()))
TN = (((0,), (0,)), ((), ()))
F32 = jnp.float32
BF16 = jnp.bfloat16


def softplus(v):
    return jnp.maximum(v, 0.0) + jnp.log1p(jnp.exp(-jnp.abs(v)))


def sigmoid(v):
    return 1.0 / (1.0 + jnp.exp(-v))


def mm(a, b, dims=(((1,), (0,)), ((), ()))):
    return lax.dot_general(a, b, dims, preferred_element_type=F32)


def column_at(states, tokens):
    return lax.broadcasted_iota(jnp.int32, (states, tokens), 1)


def write_packed(out_ref, low, wide_ref):
    rows, rank = low.shape
    states = wide_ref.shape[0] // 2
    rest = rows - LANES
    out_ref[0, 0:rows, :] = low.astype(out_ref.dtype)
    out_ref[0, rows:rows + 2 * states, :] = wide_ref[:, 0:LANES].astype(out_ref.dtype)
    tail = wide_ref[:, LANES:2 * LANES]
    lane = lax.broadcasted_iota(jnp.int32, (states, LANES), 1)
    both = jnp.where(lane < rest, tail[:states], pltpu.roll(tail[states:], rest, 1))
    out_ref[0, rows + 2 * states:rows + 3 * states, :] = both.astype(out_ref.dtype)


def read_packed(in_ref, states):
    rows = in_ref.shape[1] - 3 * states
    rest = rows - LANES
    low = in_ref[0, 0:rows, :]
    head = in_ref[0, rows:rows + 2 * states, :].astype(F32)
    both = in_ref[0, rows + 2 * states:rows + 3 * states, :].astype(F32)
    first = jnp.concatenate([head[:states], both], axis=1)
    second = jnp.concatenate([head[states:], pltpu.roll(both, LANES - rest, 1)], axis=1)
    return low, first, second


def front_kernel(me_ref, inner_ref, offset_ref, taps_ref, shift_ref, low_ref, bc_ref, act_ref, part_ref, ext_s, wide_s):
    rows = inner_ref.shape[0]
    taps = taps_ref.shape[0]

    @pl.when(pl.program_id(0) == 0)
    def _():
        ext_s[0:8, :] = jnp.zeros((8, ext_s.shape[1]), F32)

    ext_s[8:8 + rows, :] = inner_ref[...].astype(F32)
    offset = offset_ref[...]
    conv = shift_ref[...] + taps_ref[0:1, :] * ext_s[8:8 + rows, :]
    for k in range(1, taps):
        conv += jnp.where(offset >= k, taps_ref[k:k + 1, :], 0.0) * ext_s[pl.ds(8 - k, rows), :]
    act = (conv * sigmoid(conv)).astype(BF16)
    act_ref[...] = act
    ext_s[0:8, :] = ext_s[rows:rows + 8, :]
    wide_s[:, 0:rows] = mm(bc_ref[...], act, NT)
    write_packed(part_ref, mm(act, low_ref[...]), wide_s)


def front(me, projected, offset, taps, shift, low_w, bc_w):
    tokens, channels = projected.shape[0], taps.shape[1]
    runs, rows = tokens // ROWS[0], ROWS[0]
    packed = rows + 3 * bc_w.shape[0] // 2
    row = lambda i, me: (i, 0)
    fixed = lambda i, me: (0, 0)
    return pl.pallas_call(
        front_kernel,
        name="front",
        grid_spec=pltpu.PrefetchScalarGridSpec(
            num_scalar_prefetch=1,
            grid=(runs,),
            in_specs=[
                pl.BlockSpec((rows, channels), row),
                pl.BlockSpec((rows, 1), row),
                pl.BlockSpec(taps.shape, fixed),
                pl.BlockSpec(shift.shape, fixed),
                pl.BlockSpec(low_w.shape, fixed),
                pl.BlockSpec(bc_w.shape, fixed),
            ],
            out_specs=[pl.BlockSpec((rows, channels), row), pl.BlockSpec((1, packed, LANES), lambda i, me: (i ^ me[0], 0, 0))],
            scratch_shapes=[pltpu.VMEM((rows + 8, channels), F32), pltpu.VMEM((bc_w.shape[0], 2 * LANES), F32)],
        ),
        out_shape=[
            pltpu.HBM((tokens, channels), BF16),
            jax.ShapeDtypeStruct((runs, packed, LANES), BF16),
        ],
        compiler_params=pltpu.CompilerParams(dimension_semantics=("arbitrary",), vmem_limit_bytes=8 << 20),
        cost_estimate=SMALL,
    )(me, in_hbm(projected), offset, taps, shift, low_w, bc_w)


ROWS = [192]


def spread_mask(rows, states):
    width = SPAN * states
    row = lax.broadcasted_iota(jnp.int32, (rows, width), 0) % SPAN
    return row == lax.broadcasted_iota(jnp.int32, (rows, width), 1) // states


def tile_matrix(states):
    width = SPAN * states
    row = lax.broadcasted_iota(jnp.int32, (states, width), 0)
    return (row == lax.broadcasted_iota(jnp.int32, (states, width), 1) % states).astype(BF16)


def spread_columns(columns, rows, states):
    tiled = mm(columns[:, 0:rows].astype(BF16), tile_matrix(states), TN)
    return jnp.where(spread_mask(rows, states), tiled, 0.0).astype(BF16)


def forward_kernel(kept, me_ref, pack_ref, act_ref, gate_ref, offset_ref, dw_ref, bias_ref, rate_ref, skip_ref, h_in, *rest):
    pre_ref, y_ref, gated_ref, hist_ref, h_s, dtm_s, u_s = rest[kept:]
    states, channels = rate_ref.shape
    chunk = act_ref.shape[0]

    @pl.when(pl.program_id(0) == 0)
    def _():
        h_s[...] = h_in[...]

    low, bt, ct = read_packed(pack_ref, states)
    wide = bt.shape[1]
    pre = mm(low, dw_ref[...]) + bias_ref[...]
    pre_ref[...] = pre
    dt = softplus(pre)
    act = act_ref[...].astype(F32)
    u_s[...] = dt * act
    dtm_s[...] = jnp.where(offset_ref[...] == 0, FAR, dt)
    rate = rate_ref[...]

    def group(g, h):
        base = pl.multiple_of(g * STEP, STEP)
        bg = pltpu.roll(bt, wide - base, 1)
        dtm = dtm_s[pl.ds(base, STEP), :]
        u = u_s[pl.ds(base, STEP), :]
        for j in range(STEP):
            a = jnp.exp(dtm[j:j + 1, :] * rate)
            h = a * h + u[j:j + 1, :] * bg[:, j:j + 1]
            at = pl.multiple_of((base + j) * states, states)
            hist_ref[pl.ds(at, states), :] = h.astype(BF16)
        return h

    h_s[...] = lax.fori_loop(0, chunk // STEP, group, h_s[...])
    spread = spread_columns(ct, chunk, states)
    width = SPAN * states
    for g in range(chunk // SPAN):
        rows = slice(g * SPAN, (g + 1) * SPAN)
        y_ref[rows, :] = mm(spread[rows, :], hist_ref[g * width:(g + 1) * width, :])
    y = y_ref[...] + skip_ref[...] * act
    y_ref[...] = y
    gate = gate_ref[...].astype(F32)
    gated_ref[...] = (y * gate * sigmoid(gate)).astype(BF16)


def scan_forward(me, pack, act, projected, offset, delta_w, bias, rate, skip, held, whole, first, steps):
    tokens, channels = act.shape
    states = rate.shape[0]
    chunk = ROWS[0]
    row = lambda i, me: (first + i, 0)
    fixed = lambda i, me: (0, 0)
    done = steps * chunk
    return pl.pallas_call(
        functools.partial(forward_kernel, len(whole)),
        name="scan_forward",
        grid_spec=pltpu.PrefetchScalarGridSpec(
            num_scalar_prefetch=1,
            grid=(steps,),
            in_specs=[
                pl.BlockSpec((1,) + pack.shape[1:], lambda i, me: ((first + i) ^ me[0], 0, 0)),
                pl.BlockSpec((chunk, channels), row),
                pl.BlockSpec((chunk, channels), lambda i, me: (first + i, 1)),
                pl.BlockSpec((chunk, 1), row),
                pl.BlockSpec(delta_w.shape, fixed),
                pl.BlockSpec(bias.shape, fixed),
                pl.BlockSpec(rate.shape, fixed),
                pl.BlockSpec(skip.shape, fixed),
                pl.BlockSpec(rate.shape, fixed),
            ] + [pl.BlockSpec(memory_space=pl.ANY)] * len(whole),
            out_specs=[
                pl.BlockSpec((chunk, channels), row),
                pl.BlockSpec((chunk, channels), row),
                pl.BlockSpec((chunk, channels), row),
                pl.BlockSpec((chunk * states, channels), row),
                pl.BlockSpec(rate.shape, fixed),
            ],
            scratch_shapes=[
                pltpu.VMEM((chunk, channels), F32),
                pltpu.VMEM((chunk, channels), F32),
            ],
        ),
        out_shape=[
            pltpu.HBM((tokens, channels), F32),
            pltpu.HBM((tokens, channels), F32),
            pltpu.HBM((tokens, channels), BF16),
            pltpu.HBM((tokens * states, channels), BF16),
            jax.ShapeDtypeStruct(rate.shape, F32),
        ],
        input_output_aliases={10 + i: i for i in range(len(whole))},
        compiler_params=pltpu.CompilerParams(dimension_semantics=("arbitrary",), vmem_limit_bytes=16 << 20),
        cost_estimate=SMALL,
    )(me, pack, in_hbm(act), in_hbm(projected), offset, delta_w, bias, rate, skip, held, *(in_hbm(v) for v in whole))


def backward_kernel(kept, me_ref, pack_ref, pre_ref, act_ref, gate_ref, gg_ref, y_ref, offset_ref,
                    hist_ref, prior_ref, dw_ref, rate_ref, skip_ref, carry_in, rgrad_in, dwgrad_in, rows_in, *rest):
    (ggate_ref, gact_ref, part_ref, carry_s, rgrad_ref, dwgrad_ref, rows_ref,
     dtm_s, u_s, dt_s, gy_s, drive_s, decay_s, wide_s, adj_s, thr_s) = rest[kept:]
    states, channels = rate_ref.shape
    chunk = act_ref.shape[0]

    @pl.when(pl.program_id(0) == 0)
    def _():
        carry_s[...] = carry_in[...]
        rgrad_ref[...] = rgrad_in[...]
        dwgrad_ref[...] = dwgrad_in[...]
        rows_ref[...] = rows_in[...]

    low, bt, ct = read_packed(pack_ref, states)
    wide = bt.shape[1]
    pre = pre_ref[...]
    dt = softplus(pre)
    act = act_ref[...].astype(F32)
    dt_s[...] = dt
    u_s[...] = dt * act
    dtm_s[...] = jnp.where(offset_ref[...] == 0, FAR, dt)
    gate = gate_ref[...].astype(F32)
    sig = sigmoid(gate)
    gg = gg_ref[...].astype(F32) * sig
    gy = gg * gate
    gy_s[...] = gy
    ggate_ref[...] = (gg * y_ref[...] * (1.0 + gate * (1.0 - sig))).astype(BF16)
    rate = rate_ref[...]
    groups = chunk // STEP

    def group(k, held):
        carry, rgrad = held
        g = groups - 1 - k
        base = pl.multiple_of(g * STEP, STEP)
        cg = pltpu.roll(ct, wide - base, 1)
        dtm = dtm_s[pl.ds(base, STEP), :]
        dts = dt_s[pl.ds(base, STEP), :]
        gys = gy_s[pl.ds(base, STEP), :]
        for j in reversed(range(STEP)):
            if j > 0:
                at = pl.multiple_of((base + j - 1) * states, states)
                prior = hist_ref[pl.ds(at, states), :].astype(F32)
            else:
                at = pl.multiple_of(jnp.maximum(base - 1, 0) * states, states)
                prior = jnp.where(base == 0, prior_ref[...], hist_ref[pl.ds(at, states), :]).astype(F32)
            a = jnp.exp(dtm[j:j + 1, :] * rate)
            adj = cg[:, j:j + 1] * gys[j:j + 1, :] + carry
            carry = a * adj
            through = carry * prior
            rgrad = rgrad + through * dts[j:j + 1, :]
            at = pl.multiple_of((base + j) * states, states)
            adj_s[pl.ds(at, states), :] = adj.astype(BF16)
            thr_s[pl.ds(at, states), :] = (through * rate).astype(BF16)
        return carry, rgrad

    carry, rgrad = lax.fori_loop(0, groups, group, (carry_s[...], rgrad_ref[...]))
    carry_s[...] = carry
    rgrad_ref[...] = rgrad
    spread = spread_columns(bt, chunk, states)
    ones = jnp.where(spread_mask(SPAN, states), 1.0, 0.0).astype(BF16)
    width = SPAN * states
    ub = u_s[...].astype(BF16)
    gyb = gy.astype(BF16)
    ahead = (lax.broadcasted_iota(jnp.int32, (width, chunk), 1)
             - lax.broadcasted_iota(jnp.int32, (width, chunk), 0) // states)
    gb_all = jnp.zeros((width, chunk), F32)
    gc_all = jnp.zeros((width, chunk), F32)
    for g in range(chunk // SPAN):
        rows = slice(g * SPAN, (g + 1) * SPAN)
        adj = adj_s[g * width:(g + 1) * width, :]
        drive_s[rows, :] = mm(spread[rows, :], adj)
        decay_s[rows, :] = mm(ones, thr_s[g * width:(g + 1) * width, :])
        gb_all = jnp.where(ahead == g * SPAN, mm(adj, ub, NT), gb_all)
        gc_all = jnp.where(ahead == g * SPAN, mm(hist_ref[g * width:(g + 1) * width, :], gyb, NT), gc_all)
    tiles = tile_matrix(states)
    wide_s[0:states, 0:chunk] = mm(tiles, gb_all.astype(BF16))
    wide_s[states:2 * states, 0:chunk] = mm(tiles, gc_all.astype(BF16))
    drive = drive_s[...]
    gact_ref[...] = drive * dt + gy * skip_ref[...]
    gpre = ((drive * act + decay_s[...]) * sigmoid(pre)).astype(BF16)
    rows_ref[0:1, :] += jnp.sum(gy * act, axis=0, keepdims=True)
    rows_ref[1:2, :] += jnp.sum(gpre.astype(F32), axis=0, keepdims=True)
    dwgrad_ref[...] += mm(low, gpre, TN)
    write_packed(part_ref, mm(gpre, dw_ref[...], NT), wide_s)


def scan_backward(me, pack, pre, act, projected, gg, y, offset, hist, delta_w, rate, skip, held, whole, last, steps):
    tokens, channels = act.shape
    states = rate.shape[0]
    chunk = ROWS[0]
    row = lambda i, me: (last - i, 0)
    second = lambda i, me: (last - i, 1)
    run = lambda i, me: ((last - i) ^ me[0], 0, 0)
    fixed = lambda i, me: (0, 0)
    blocks = [pl.BlockSpec((chunk, channels), second), pl.BlockSpec((chunk, channels), row), pl.BlockSpec((1,) + pack.shape[1:], run)]
    shapes = [
        pltpu.HBM((tokens, 2 * channels), BF16),
        pltpu.HBM((tokens, channels), F32),
        jax.ShapeDtypeStruct(pack.shape, BF16),
    ]
    sums = [pl.BlockSpec(v.shape, fixed) for v in held]
    done = steps * chunk
    return pl.pallas_call(
        functools.partial(backward_kernel, len(whole)),
        name="scan_backward",
        grid_spec=pltpu.PrefetchScalarGridSpec(
            num_scalar_prefetch=1,
            grid=(steps,),
            in_specs=[
                pl.BlockSpec((1,) + pack.shape[1:], run),
                pl.BlockSpec((chunk, channels), row),
                pl.BlockSpec((chunk, channels), row),
                pl.BlockSpec((chunk, channels), second),
                pl.BlockSpec((chunk, channels), row),
                pl.BlockSpec((chunk, channels), row),
                pl.BlockSpec((chunk, 1), row),
                pl.BlockSpec((chunk * states, channels), row),
                pl.BlockSpec((states, channels), lambda i, me: (jnp.maximum((last - i) * chunk - 1, 0), 0)),
                pl.BlockSpec(delta_w.shape, fixed),
                pl.BlockSpec(rate.shape, fixed),
                pl.BlockSpec(skip.shape, fixed),
            ] + sums + [pl.BlockSpec(memory_space=pl.ANY)] * len(whole),
            out_specs=blocks + sums,
            scratch_shapes=[pltpu.VMEM((chunk, channels), F32)] * 6
            + [pltpu.VMEM((2 * states, 2 * LANES), F32)]
            + [pltpu.VMEM((chunk * states, channels), BF16)] * 2,
        ),
        out_shape=shapes + [jax.ShapeDtypeStruct(v.shape, F32) for v in held],
        input_output_aliases={17 + i: i for i in range(len(whole))},
        compiler_params=pltpu.CompilerParams(dimension_semantics=("arbitrary",), vmem_limit_bytes=24 << 20),
        cost_estimate=SMALL,
    )(me, pack, in_hbm(pre), in_hbm(act), in_hbm(projected), in_hbm(gg), in_hbm(y), offset, in_hbm(hist), in_hbm(hist), delta_w, rate, skip, *held, *(in_hbm(v) if k == 1 else v for k, v in enumerate(whole)))


def end_kernel(me_ref, pack_ref, gact_ref, act_ref, inner_ref, prior_ref, offset_ref, taps_ref, shift_ref, low_ref, bc_ref, grad_ref,
               ginner_ref, tapg_ref, selow_ref, selbc_ref, ext_s, after_s, wide_s):
    rows, channels = inner_ref.shape
    taps = taps_ref.shape[0]
    states = bc_ref.shape[0] // 2

    @pl.when(pl.program_id(0) == 0)
    def _():
        after_s[...] = jnp.zeros_like(after_s)
        tapg_ref[...] = jnp.zeros_like(tapg_ref)
        selow_ref[...] = jnp.zeros_like(selow_ref)
        selbc_ref[...] = jnp.zeros_like(selbc_ref)

    low, gbt, gct = read_packed(pack_ref, states)
    wide_s[0:states, :] = gbt
    wide_s[states:2 * states, :] = gct
    gbc = wide_s[:, 0:rows].astype(BF16)
    act = act_ref[...]
    selow_ref[...] += mm(act, low, TN)
    selbc_ref[...] += mm(gbc, act)
    gact = gact_ref[...] + mm(low, low_ref[...], NT) + mm(gbc, bc_ref[...], TN)
    before = prior_ref.shape[0]
    ext_s[0:before, :] = prior_ref[...].astype(F32)
    ext_s[before:before + rows, :] = inner_ref[...].astype(F32)
    offset = offset_ref[...]
    conv = shift_ref[...] + taps_ref[0:1, :] * ext_s[before:before + rows, :]
    for k in range(1, taps):
        conv += jnp.where(offset >= k, taps_ref[k:k + 1, :], 0.0) * ext_s[pl.ds(before - k, rows), :]
    q = sigmoid(conv)
    gconv = gact * q * (1.0 + conv * (1.0 - q))
    tapg_ref[taps:taps + 1, :] += jnp.sum(gconv, axis=0, keepdims=True)
    tapg_ref[0:1, :] += jnp.sum(gconv * ext_s[before:before + rows, :], axis=0, keepdims=True)
    ginner = gconv * taps_ref[0:1, :]
    for k in range(1, taps):
        masked = jnp.where(offset >= k, gconv, 0.0)
        tapg_ref[k:k + 1, :] += jnp.sum(masked * ext_s[pl.ds(before - k, rows), :], axis=0, keepdims=True)
        after_s[k - 1, rows:rows + 8, :] = after_s[k - 1, 0:8, :]
        after_s[k - 1, 0:rows, :] = masked * taps_ref[k:k + 1, :]
        ginner += after_s[k - 1, pl.ds(k, rows), :]
    ginner_ref[...] = ginner.astype(BF16)


def end(me, pack, gact, act, projected, offset, taps, shift, low_w, bc_w, grad_projected):
    tokens, channels = act.shape
    rows = ROWS[0]
    steps = tokens // rows
    row = lambda i, me: (steps - 1 - i, 0)
    fixed = lambda i, me: (0, 0)
    return pl.pallas_call(
        end_kernel,
        name="end",
        grid_spec=pltpu.PrefetchScalarGridSpec(
            num_scalar_prefetch=1,
            grid=(steps,),
            in_specs=[
                pl.BlockSpec((1,) + pack.shape[1:], lambda i, me: ((steps - 1 - i) ^ me[0], 0, 0)),
                pl.BlockSpec((rows, channels), row),
                pl.BlockSpec((rows, channels), row),
                pl.BlockSpec((rows, channels), row),
                pl.BlockSpec((16, channels), lambda i, me: (jnp.maximum((steps - 1 - i) * (rows // 16) - 1, 0), 0)),
                pl.BlockSpec((rows, 1), row),
                pl.BlockSpec(taps.shape, fixed),
                pl.BlockSpec(shift.shape, fixed),
                pl.BlockSpec(low_w.shape, fixed),
                pl.BlockSpec(bc_w.shape, fixed),
                pl.BlockSpec(memory_space=pl.ANY),
            ],
            out_specs=[
                pl.BlockSpec((rows, channels), row),
                pl.BlockSpec((8, channels), fixed),
                pl.BlockSpec(low_w.shape, fixed),
                pl.BlockSpec(bc_w.shape, fixed),
            ],
            scratch_shapes=[
                pltpu.VMEM((rows + 16, channels), F32),
                pltpu.VMEM((3, rows + 8, channels), F32),
                pltpu.VMEM((bc_w.shape[0], 2 * LANES), F32),
            ],
        ),
        out_shape=[
            pltpu.HBM(grad_projected.shape, BF16),
            jax.ShapeDtypeStruct((8, channels), F32),
            jax.ShapeDtypeStruct(low_w.shape, F32),
            jax.ShapeDtypeStruct(bc_w.shape, F32),
        ],
        input_output_aliases={11: 0},
        compiler_params=pltpu.CompilerParams(dimension_semantics=("arbitrary",), vmem_limit_bytes=14 << 20),
        cost_estimate=SMALL,
    )(me, pack, in_hbm(gact), in_hbm(act), in_hbm(projected), in_hbm(projected), offset, taps, shift, low_w, bc_w, in_hbm(grad_projected))


def weight_grad_kernel(count, turned, table_ref, *refs):
    a_refs, b_refs = refs[:count], refs[count:2 * count]
    out_ref, a_s, b_s = refs[-3:]
    rows = a_refs[0].shape[0]
    for s in range(count):
        a_s[s * rows:(s + 1) * rows, :] = a_refs[s][...]

    @pl.when(pl.program_id(0) == 0)
    def _():
        for s in range(count):
            b_s[s * rows:(s + 1) * rows, :] = b_refs[s][...]

    first, second = (b_s, a_s) if turned else (a_s, b_s)
    out_ref[0] = mm(first[...], second[...], TN).astype(BF16)


def weight_grad(table, distances, shards, b, column, channels, size, turned, slots=1, slot=0, into=()):
    rows, width = shards[0].shape
    block = width // size
    count = len(shards)
    shape = (1, channels, block) if turned else (1, block, channels)
    if distances is None:
        b_specs = [pl.BlockSpec((rows, channels), lambda i, table: (0, column))]
    else:
        b_specs = [pl.BlockSpec((rows, channels), lambda i, table, d=d: (table[d], column)) for d in distances]
    return pl.pallas_call(
        functools.partial(weight_grad_kernel, count, turned),
        name="weight_grad",
        grid_spec=pltpu.PrefetchScalarGridSpec(
            num_scalar_prefetch=1,
            grid=(size,),
            in_specs=[pl.BlockSpec((rows, block), lambda i, table: (0, i))] * count
            + b_specs + [pl.BlockSpec(memory_space=pl.ANY)] * len(into),
            out_specs=pl.BlockSpec(shape, lambda i, table: (i, slot, 0)),
            scratch_shapes=[pltpu.VMEM((rows * count, block), BF16), pltpu.VMEM((rows * count, channels), BF16)],
        ),
        out_shape=pltpu.HBM((size, slots * shape[1], shape[2]), BF16),
        input_output_aliases={1 + 2 * count + k: k for k in range(len(into))},
        compiler_params=pltpu.CompilerParams(dimension_semantics=("arbitrary",), vmem_limit_bytes=16 << 20),
        cost_estimate=SMALL,
    )(table, *(in_hbm(v) for v in shards), *([in_hbm(b)] * count), *(in_hbm(v) for v in into))


def weight_block(weight, dims, blocks):
    if dims[0][1] == (0,):
        columns = weight.shape[1] // blocks
        return pl.BlockSpec((weight.shape[0], columns), lambda i, *rest: (0, i)), columns
    columns = weight.shape[0] // blocks
    return pl.BlockSpec((columns, weight.shape[1]), lambda i, *rest: (i, 0)), columns


def placed_kernel(dims, count, table_ref, *refs):
    w_ref, out_ref = refs[count], refs[-1]
    for s in range(count):
        @pl.when(pl.program_id(1) == s)
        def _(s=s):
            out_ref[...] = mm(refs[s][...], w_ref[...], dims).astype(out_ref.dtype)


def pick_entry(values, i):
    chosen = values[0]
    for k in range(1, len(values)):
        chosen = jnp.where(i == k, values[k], chosen)
    return chosen


def placed_product(table, distances, shards, weight, dims, out):
    rows, width = shards[0].shape
    count, blocks = len(shards), 2
    spec, columns = weight_block(weight, dims, blocks)
    return pl.pallas_call(
        functools.partial(placed_kernel, dims, count),
        name="placed_product",
        grid_spec=pltpu.PrefetchScalarGridSpec(
            num_scalar_prefetch=1,
            grid=(blocks, count),
            in_specs=[pl.BlockSpec((rows, width), lambda i, k, table: (0, 0))] * count
            + [spec, pl.BlockSpec(memory_space=pl.ANY)],
            out_specs=pl.BlockSpec((rows, columns), lambda i, k, table: (pick_entry([table[d] for d in distances], k), i)),
        ),
        out_shape=pltpu.HBM(out.shape, out.dtype),
        input_output_aliases={count + 2: 0},
        compiler_params=pltpu.CompilerParams(dimension_semantics=("arbitrary", "arbitrary"), vmem_limit_bytes=16 << 20),
        cost_estimate=SMALL,
    )(table, *(in_hbm(v) for v in shards), in_hbm(weight), in_hbm(out))


def placed_halves_kernel(cuts, table_ref, first_ref, second_ref, *refs):
    w_refs, out_ref = refs[:cuts], refs[-1]
    depth = w_refs[0].shape[0]
    each = first_ref.shape[1] // depth
    total = None
    for c in range(cuts):
        ref, at = (first_ref, c) if c < each else (second_ref, c - each)
        term = mm(ref[:, at * depth:(at + 1) * depth], w_refs[c][...])
        total = term if total is None else total + term
    out_ref[...] = total.astype(out_ref.dtype)


def placed_halves(table, distance, first, second, weight, out):
    rows, middle = first.shape
    cuts = 8
    depth, width = weight.shape[0] // cuts, weight.shape[1]
    return pl.pallas_call(
        functools.partial(placed_halves_kernel, cuts),
        name="placed_halves",
        grid_spec=pltpu.PrefetchScalarGridSpec(
            num_scalar_prefetch=1,
            grid=(1,),
            in_specs=[pl.BlockSpec((rows, middle), lambda i, table: (0, 0))] * 2
            + [pl.BlockSpec((depth, width), lambda i, table, c=c: (c, 0)) for c in range(cuts)]
            + [pl.BlockSpec(memory_space=pl.ANY)],
            out_specs=pl.BlockSpec((rows, width), lambda i, table: (table[distance], 0)),
        ),
        out_shape=pltpu.HBM(out.shape, out.dtype),
        input_output_aliases={3 + cuts: 0},
        compiler_params=pltpu.CompilerParams(dimension_semantics=("arbitrary",), vmem_limit_bytes=16 << 20),
        cost_estimate=SMALL,
    )(table, in_hbm(first), in_hbm(second), *([in_hbm(weight)] * cuts), in_hbm(out))


def in_hbm(value):
    return pltpu.with_memory_space_constraint(value, pltpu.HBM)


def far_kernel(cuts, table_ref, g_ref, t_ref, *refs):
    w_refs, (ahead_ref, behind_ref) = refs[:cuts], refs[cuts:]
    columns = w_refs[0].shape[0]
    for ref, first in ((ahead_ref, True), (behind_ref, False)):
        @pl.when((pl.program_id(0) == 0) == first)
        def _(ref=ref):
            for c in range(cuts):
                at = slice(c * columns, (c + 1) * columns)
                ref[:, at] = (mm(g_ref[...], w_refs[c][...], NT) + t_ref[:, at].astype(F32)).astype(BF16)


def pair_kernel(cuts, table_ref, ga_ref, gb_ref, ta_ref, tb_ref, *refs, halves=False):
    w_refs, (ra_ref, rb_ref, ahead_ref, behind_ref) = refs[:cuts], refs[cuts:]
    rows, columns = ga_ref.shape[0], w_refs[0].shape[0]
    both = jnp.concatenate([ga_ref[...], gb_ref[...]], axis=0)
    low = pl.program_id(0) == 0
    for c in range(cuts):
        at = slice(c * columns, (c + 1) * columns)
        total = mm(both, w_refs[c][...], NT)
        ra, rb = ra_ref[:, at].astype(F32), rb_ref[:, at].astype(F32)
        if halves:
            ra, rb = jnp.where(low, ra, 0.0), jnp.where(low, 0.0, rb)
        ahead_ref[:, at] = (total[:rows] + ta_ref[:, at].astype(F32) + ra).astype(BF16)
        behind_ref[:, at] = (total[rows:] + tb_ref[:, at].astype(F32) + rb).astype(BF16)


def own_kernel(cuts, table_ref, g_ref, t_ref, *refs):
    w_refs, (ra_ref, rb_ref, place_ref, out_ref) = refs[:cuts], refs[cuts:]
    columns = w_refs[0].shape[0]
    for c in range(cuts):
        at = slice(c * columns, (c + 1) * columns)
        total = mm(g_ref[...], w_refs[c][...], NT) + t_ref[:, at].astype(F32)
        total = total + ra_ref[:, at].astype(F32) + rb_ref[:, at].astype(F32)
        out_ref[:, at] = mm(place_ref[...], total.astype(BF16)).astype(BF16)


def ring_step(kernel, table, distances, grads, terms, weight, arrived=(), place=None):
    rows, cuts = ROWS[0], 4
    width, channels = weight.shape[0], weight.shape[1] // 2
    half, columns = width // 2, width // (2 * cuts)
    fixed = lambda i, table: (0, 0)
    side = lambda i, table: (0, i)
    far = not arrived
    if far:
        outs, shape = [fixed, fixed], (rows, half)
    else:
        outs, shape = [side, side] if place is None else [side], (rows, width)
    small = not far and arrived[0].shape[1] == half
    extra = [] if place is None else [place]
    return pl.pallas_call(
        functools.partial(kernel, cuts, halves=True) if small else functools.partial(kernel, cuts),
        name=kernel.__name__,
        grid_spec=pltpu.PrefetchScalarGridSpec(
            num_scalar_prefetch=1,
            grid=(2,),
            in_specs=[pl.BlockSpec((rows, channels), lambda i, table, d=d: (table[d], 0)) for d in distances]
            + [pl.BlockSpec((rows, half), lambda i, table, d=d: (table[d], i)) for d in distances]
            + [pl.BlockSpec((columns, channels), lambda i, table, c=c: (i * cuts + c, 0)) for c in range(cuts)]
            + [pl.BlockSpec((rows, half), fixed if small else side) for v in arrived]
            + [pl.BlockSpec(v.shape, fixed) for v in extra],
            out_specs=[pl.BlockSpec((rows, half), m) for m in outs],
        ),
        out_shape=[pltpu.HBM(shape, BF16) for m in outs],
        compiler_params=pltpu.CompilerParams(dimension_semantics=("arbitrary",), vmem_limit_bytes=24 << 20),
        cost_estimate=SMALL,
    )(table, *([in_hbm(grads)] * len(distances)), *([in_hbm(terms)] * len(distances)), *([in_hbm(weight)] * cuts),
      *(in_hbm(v) for v in arrived), *extra)


def blank(*shapes):
    hbm = pl.BlockSpec(memory_space=pl.ANY)
    return pl.pallas_call(
        lambda *refs: None, name="blank", out_specs=[hbm] * len(shapes),
        out_shape=[pltpu.HBM(*v) for v in shapes],
        cost_estimate=SMALL)()


def deal_kernel(x_ref, cot_ref, order_ref, gain_ref, me_ref, sendx_ref, sendc_ref, pick_ref, place_ref):
    rows = x_ref.shape[0]
    dp_size = order_ref.shape[0]
    me = me_ref[0]
    group_tokens = me_ref[1]
    pair = rows // dp_size
    order = order_ref[...].astype(jnp.int32)
    near = lax.broadcasted_iota(jnp.int32, (dp_size, rows), 0)
    other = near ^ me
    source = order // group_tokens
    local = order % rows
    before = (
        lax.broadcasted_iota(jnp.int32, (rows, rows), 0) < lax.broadcasted_iota(jnp.int32, (rows, rows), 1)
    ).astype(BF16)
    slots = lax.broadcasted_iota(jnp.int32, (rows, rows), 0)
    chosen = source == me
    rank = mm(chosen.astype(BF16), before).astype(jnp.int32)
    slot = jnp.where(chosen, near * pair + rank, -1)
    pick = jnp.zeros((rows, rows), F32)
    for d in range(dp_size):
        pick += mm((slots == slot[d:d + 1, :]).astype(BF16), (slots == local[d:d + 1, :]).astype(BF16), NT)
    pick = pick.astype(BF16)
    pick_ref[...] = pick
    mine = source[0:1, :]
    held = (mine == other).astype(BF16)
    ranks = mm(held, before).astype(jnp.int32)
    arrived = jnp.sum(jnp.where(mine == other, near * pair + ranks, 0), axis=0, keepdims=True)
    place_ref[...] = (slots == arrived).astype(BF16)
    x = x_ref[...].astype(F32)
    rinv = lax.rsqrt(jnp.mean(x * x, axis=1, keepdims=True) + EPSILON)
    normed = (x * rinv * gain_ref[...]).astype(BF16)
    sendx_ref[...] = mm(pick, normed).astype(BF16)
    sendc_ref[...] = mm(pick, cot_ref[...]).astype(BF16)


def deal(x, cot, order, gain, me):
    rows, width = x.shape
    vm = pl.BlockSpec(memory_space=pltpu.VMEM)
    return pl.pallas_call(
        deal_kernel,
        name="deal",
        in_specs=[vm, vm, vm, vm, pl.BlockSpec(memory_space=pltpu.SMEM)],
        out_specs=[vm] * 4,
        out_shape=[
            jax.ShapeDtypeStruct((rows, width), BF16),
            jax.ShapeDtypeStruct((rows, width), BF16),
            jax.ShapeDtypeStruct((rows, rows), BF16),
            jax.ShapeDtypeStruct((rows, rows), BF16),
        ],
        compiler_params=pltpu.CompilerParams(vmem_limit_bytes=32 << 20),
        cost_estimate=SMALL,
    )(x, cot, order, gain, me)


def round_dot(a, b, dims=(((1,), (0,)), ((), ()))):
    return mm(a, b, dims).astype(BF16)


def after(value, *earlier):
    return lax.optimization_barrier((value,) + earlier)[0]


def flip(value, axis, bit):
    return lax.ppermute(value, axis, [(i, i ^ bit) for i in range(lax.axis_size(axis))])


def exchange(pieces, axis, stack=True):
    pieces = [pieces[0]] + [flip(pieces[d], axis, d) for d in range(1, lax.axis_size(axis))]
    return jnp.stack(pieces) if stack else pieces


def swap(values, axis):
    return lax.all_to_all(values, axis, split_axis=0, concat_axis=0, tiled=True)


def share(value, axis):
    return exchange([value] * lax.axis_size(axis), axis)


def in_order(pieces, axis):
    size, me, bit = lax.axis_size(axis), lax.axis_index(axis), 1
    while bit < size:
        split = pieces.reshape((size // (2 * bit), 2, bit) + pieces.shape[1:])
        turned = jnp.concatenate([split[:, 1:], split[:, :1]], axis=1)
        pieces = jnp.where((me // bit) % 2 == 1, turned, split).reshape(pieces.shape)
        bit *= 2
    return pieces


def cube_sum(value, axis, bit, end_bit):
    while bit < end_bit:
        value = value + flip(value, axis, bit)
        bit *= 2
    return value


class Bag(dict):
    def meet(self, values, *names):
        values, held = lax.optimization_barrier((values, {n: self[n] for n in names}))
        self.update(held)
        return values


def add_up(pieces):
    return jnp.sum(pieces.astype(F32), axis=0)


class Ring:
    def __init__(self, axis):
        self.axis = axis
        self.size = size = lax.axis_size(axis)
        columns = max(c for c in range(1, size) if size % c == 0 and c * c <= size)
        rows = size // columns
        cycle = [(0, c) for c in range(columns)]
        for r in range(1, rows):
            snake = range(1, columns)
            cycle += [(r, c) for c in (snake if r % 2 == 0 else reversed(snake))]
        cycle += [(r, 0) for r in reversed(range(1, rows))]
        order = [r * columns + c for r, c in cycle]
        place = {t: i for i, t in enumerate(order)}
        table = jnp.array([[order[(place[t] + d) % size] for d in range(size)] for t in range(size)], jnp.int32)
        self.at = lax.dynamic_index_in_dim(table, lax.axis_index(axis), 0, keepdims=False)
        self.forward = [(order[i], order[(i + 1) % size]) for i in range(size)]
        self.backward = [(b, a) for a, b in self.forward]

    def hop(self, value, ahead):
        return lax.ppermute(value, self.axis, self.forward if ahead else self.backward)


def ring_gather(ring, own, between):
    half, size = ring.size // 2, ring.size
    middle = own.shape[1] // 2
    distances, shards = [0], [own]
    ahead = behind = own
    for d in range(1, half):
        ahead, behind = between(d, ring.hop(ahead, True), ring.hop(behind, False))
        distances += [size - d, d]
        shards += [ahead, behind]
    halves = between(half, ring.hop(ahead[:, :middle], True), ring.hop(behind[:, middle:], False))
    return distances + [half], shards, halves


def ring_reduce(ring, grads, terms, weight, place, between):
    half, size = ring.size // 2, ring.size
    step = functools.partial(ring_step, table=ring.at, grads=grads, terms=terms, weight=weight)
    ahead, behind = step(far_kernel, distances=[half])
    for d in range(half, 0, -1):
        ahead, behind = between(half - d, ahead, ring.hop(ahead, True), ring.hop(behind, False))
        if d > 1:
            ahead, behind = step(pair_kernel, distances=[d - 1, size + 1 - d], arrived=[ahead, behind])
    return step(own_kernel, distances=[0], arrived=[ahead, behind], place=place)[0]


def shards(
    block_input, norm_gain, in_weight, conv_weight, conv_bias, select_weight, delta_weight, delta_bias,
    decay_log, skip_weight, out_weight, out_cotangent, seq_lengths, deal_order,
):
    rows_dev, width = block_input.shape
    dp_size = lax.axis_size("dp")
    tensor_size = lax.axis_size("tensor")
    pair = rows_dev // dp_size
    group_tokens = rows_dev * tensor_size
    ring = Ring("tensor")
    here = jnp.zeros((1,), jnp.int32)
    me = jnp.stack([lax.axis_index("dp"), jnp.int32(group_tokens)]).astype(jnp.int32)
    head = share(jnp.concatenate([deal_order.astype(F32), norm_gain.astype(F32)]), "dp")
    gain_values = in_order(head[:, rows_dev:], "dp").reshape(1, -1)
    send_rows, send_cot, pick, place = deal(block_input, out_cotangent, head[:, :rows_dev], gain_values, me)
    in_cat = jnp.swapaxes(after(in_weight, send_rows), 0, 1).reshape(in_weight.shape[1], -1)
    recv_rows = exchange(send_rows.reshape(dp_size, pair, -1), "dp")
    recv_rows, in_cat = lax.optimization_barrier((recv_rows, in_cat))
    in_full = lax.all_gather(in_cat, "dp", axis=0, tiled=True)
    normed = round_dot(place, recv_rows.reshape(rows_dev, -1), TN)
    channels = in_full.shape[1] // 2
    taps = conv_weight.shape[0]
    lane_width = conv_bias.shape[1] * dp_size
    own_states = decay_log.shape[1]
    states, low_rank = own_states * dp_size, delta_weight.shape[0] * dp_size
    lengths_row = seq_lengths[0]
    seq_ends = jnp.cumsum(lengths_row)
    begins = seq_ends - lengths_row
    positions = jnp.arange(group_tokens, dtype=jnp.int32)
    inside = (positions[:, None] >= begins[None, :]) & (positions[:, None] < seq_ends[None, :])
    offset = (positions - jnp.sum(jnp.where(inside, begins[None, :], 0), axis=1))[:, None]
    (projected,) = blank(((group_tokens, 2 * channels), BF16))
    half = tensor_size // 2
    NN = (((1,), (0,)), ((), ()))
    lanes_own = jnp.concatenate([conv_weight, jnp.stack([conv_bias, delta_bias, skip_weight])])
    bag = Bag(
        cot=send_cot, select=jnp.concatenate([select_weight, jnp.moveaxis(lanes_own, 0, 2)], axis=2),
        thin=jnp.concatenate([decay_log.T, delta_weight]), projected=projected)
    waiting = {"shards": [normed], "distances": [0]}

    def during_normed(d, ahead, behind):
        if d == 1:
            ahead, behind = bag.meet((ahead, behind), "select")
            bag["select"] = share(bag["select"], "dp")
            bag["own"] = out_weight
        elif d < half - 1:
            ahead, behind = bag.meet((ahead, behind), "own", "select", "cot")
            if d == 2:
                bag["cot"] = exchange(bag["cot"].reshape(dp_size, pair, -1), "dp")
        elif d >= half - 1:
            bag["projected"] = placed_product(
                ring.at, waiting["distances"], waiting["shards"], in_full, NN, bag["projected"])
            waiting["shards"], waiting["distances"] = [], []
            ahead, behind = bag.meet((ahead, behind), "projected", *(["cot"] if d == half else []))
        if d < half:
            waiting["distances"] += [tensor_size - d, d]
            waiting["shards"] += [ahead, behind]
        return ahead, behind

    distances, normed_shards, halves = ring_gather(ring, normed, during_normed)

    def rows_of(values, distance):
        return lax.dynamic_slice(values, (ring.at[distance] * rows_dev, 0), (rows_dev, values.shape[1]))

    projected = placed_halves(ring.at, distances[-1], *halves, in_full, bag["projected"])
    dealt_cot = round_dot(place, bag["cot"].reshape(rows_dev, -1), TN)
    select_matrix = jnp.moveaxis(in_order(bag["select"], "dp"), 0, 1).reshape(channels, -1)
    low_w, bc_w = select_matrix[:, :low_rank], select_matrix[:, low_rank:low_rank + 2 * states].T
    lanes_float = select_matrix[:, low_rank + 2 * states:].astype(F32).T
    conv_taps = lanes_float[:taps]
    conv_shift, delta_shift, skip_values = (lanes_float[taps + i:taps + i + 1] for i in range(3))
    activated, part = front(here, projected, offset, conv_taps, conv_shift, low_w, bc_w)
    out_full = lax.all_gather(bag["own"], "dp", axis=1, tiled=True)
    group_cot = lax.all_gather(after(dealt_cot, halves[0]), "tensor", axis=0, tiled=True)
    bag["thin"] = lax.all_gather(after(bag["thin"], part)[None], "dp", axis=0, tiled=True)
    bag["last"] = jnp.concatenate([after(v, part) for v in halves], axis=1)
    arrived = bag.meet(swap(part, "tensor"), "thin", "last")
    normed_shards = normed_shards + [bag["last"]]
    decay_full = bag["thin"][:, :own_states].reshape(states, channels)
    delta_full = bag["thin"][:, own_states:].reshape(low_rank, channels)
    decay_rate = -jnp.exp(decay_full.astype(F32))
    total = jnp.sum(arrived.astype(F32), axis=0).astype(BF16)
    pack_all = swap(jnp.broadcast_to(total[None], part.shape), "tensor")
    pre, y, gated, hist, unused_state = scan_forward(
        here, pack_all, activated, projected, offset, delta_full, delta_shift, decay_rate, skip_values,
        jnp.zeros((states, channels), F32), [], 0, tensor_size)
    gg = mm(group_cot, out_full, NT)
    held = [
        jnp.zeros((states, channels), F32),
        jnp.zeros((states, channels), F32),
        jnp.zeros((low_rank, channels), F32),
        jnp.zeros((8, channels), F32),
    ]
    mixed = lax.psum_scatter(round_dot(gated, out_full), "tensor", scatter_dimension=0, tiled=True)
    grad_projected, grad_act, grad_part, unused_carry, rate_grad, delta_weight_grad, row_grads = scan_backward(
        here, pack_all, pre, activated, projected, gg, y, offset, hist, delta_full, decay_rate, skip_values,
        held, [], tensor_size - 1, tensor_size)
    decay_grad = rate_grad * decay_rate
    def by_lane(values):
        lanes = values.reshape(-1, channels // lane_width, dp_size, lane_width // dp_size)
        return jnp.moveaxis(lanes, 2, 0).reshape(dp_size, -1)

    def pack_small(taps_sum, low_sum, bc_sum, row_grads, decay_grad, delta_weight_grad):
        select_grad = jnp.concatenate([low_sum, bc_sum.T], axis=1)
        parts = [
            by_lane(jnp.concatenate([taps_sum[:taps + 1], row_grads[:2]])),
            decay_grad.reshape(dp_size, -1),
            delta_weight_grad.reshape(dp_size, -1),
            jnp.moveaxis(select_grad.reshape(channels // lane_width, dp_size, -1), 1, 0).reshape(dp_size, -1),
        ]
        flat = jnp.concatenate(parts, axis=1)
        fill = -flat.shape[1] % 2048
        flat = jnp.pad(flat, ((0, 0), (0, fill))).astype(BF16).reshape(dp_size, -1, LANES)
        return flat, [part.shape[1] for part in parts]

    merged = channels == width // dp_size
    bag["out"] = weight_grad(
        ring.at, None, [group_cot], after(gated, grad_part), 0, channels, dp_size, True, 2 if merged else 1)
    arrived = bag.meet(swap(grad_part, "tensor"), "out")
    grad_total = jnp.sum(arrived.astype(F32), axis=0).astype(BF16)
    bag["gate"] = weight_grad(
        ring.at, distances, normed_shards, after(grad_projected, grad_total), 1, channels, dp_size, False,
        *((2, 1, [bag["out"]]) if merged else ()))
    bag["terms"] = round_dot(after(grad_projected, grad_total)[:, channels:], in_full[:, channels:], NT)
    grad_pack = bag.meet(swap(jnp.broadcast_to(grad_total[None], grad_part.shape), "tensor"), "gate", "terms")
    gate_terms = bag["terms"]
    bag["gate"] = lax.psum_scatter(bag["gate"], "dp", scatter_dimension=0, tiled=True)
    if not merged:
        bag["out"] = lax.psum_scatter(bag["out"], "dp", scatter_dimension=0, tiled=True)
    grad_projected, *sums = end(
        here, grad_pack, grad_act, activated, projected, offset, conv_taps, conv_shift, low_w, bc_w, grad_projected)
    bag["sums"] = [*sums, row_grads, decay_grad, delta_weight_grad]
    bag["mixed"] = mixed

    def during_grad(k, sent, ahead, behind):
        names = []
        if k == 0:
            bag["grads"] = grad_projected
            names = ["mixed", "sums", "grads"]
        if k == 1:
            bag["inner"] = weight_grad(ring.at, distances, normed_shards, bag["grads"], 0, channels, dp_size, False)
            bag["mixed"] = round_dot(place, bag["mixed"])
            names = ["mixed", "sums", "inner"]
        if k == half - 2:
            names = ["mixed", "flat", "gate"] + ([] if merged else ["out"])
        if k == half - 1:
            gate_grad = bag["gate"][:, channels:] if merged else bag["gate"]
            bag["in"] = jnp.concatenate([bag["inner"], gate_grad]).astype(F32)
            bag["gain"] = cube_sum(jnp.sum(in_weight.astype(F32) * bag["in"], axis=(0, 2)), "tensor", 1, 2)
            names = ["gain", "in"]
        ahead, behind = bag.meet((ahead, behind), *names)
        if k == 1:
            bag["inner"] = lax.psum_scatter(bag["inner"], "dp", scatter_dimension=0, tiled=True)
            bag["mixed"] = exchange(bag["mixed"].reshape(dp_size, pair, -1), "dp")
            flat, waiting["sizes"] = pack_small(*bag["sums"])
            bag["flat"] = swap(flat, "dp")
        return ahead, behind

    send_grad = ring_reduce(ring, grad_projected, gate_terms, in_full, place, during_grad)
    home_grad = exchange(send_grad.reshape(dp_size, pair, -1), "dp").reshape(rows_dev, -1)
    home_out = bag["mixed"].reshape(rows_dev, -1)
    out_grad = (bag["gate"][0, :channels] if merged else bag["out"][0]).astype(F32)
    in_weight_grad = bag["in"]
    gain_grad = cube_sum(after(bag["gain"], send_grad), "tensor", 2, tensor_size) / norm_gain.astype(F32)
    flat = jnp.sum(bag["flat"].astype(F32), axis=0).reshape(-1)
    small, start = [], 0
    for size in waiting["sizes"]:
        small.append(flat[start:start + size])
        start += size
    lane_grads = small[0].reshape((taps + 3,) + conv_bias.shape)
    rows_float = block_input.astype(F32)
    block_output = (rows_float + mm(pick, home_out, TN)).astype(BF16)
    inverse_rms = lax.rsqrt(jnp.mean(rows_float * rows_float, axis=1, keepdims=True) + EPSILON)
    unit_rows = rows_float * inverse_rms
    scaled = mm(pick, home_grad, TN) * gain_values
    input_grad = (
        out_cotangent.astype(F32)
        + inverse_rms * (scaled - unit_rows * jnp.mean(scaled * unit_rows, axis=1, keepdims=True))
    ).astype(BF16)
    return (
        block_output,
        input_grad,
        gain_grad,
        in_weight_grad,
        lane_grads[:taps],
        lane_grads[taps],
        small[3].reshape(select_weight.shape),
        small[2].reshape(delta_weight.shape),
        lane_grads[taps + 2],
        small[1].reshape(decay_log.shape[1], decay_log.shape[0]).T,
        lane_grads[taps + 1],
        out_grad,
    )


def solution(mesh):
    return jax.shard_map(
        shards,
        mesh=mesh,
        in_specs=(
            P(("dp", "tensor"), None),
            P("dp"),
            P(None, "dp", "tensor"),
            P(None, "tensor", "dp"),
            P("tensor", "dp"),
            P("tensor", "dp", None),
            P("dp", "tensor"),
            P("tensor", "dp"),
            P("tensor", "dp"),
            P("tensor", "dp"),
            P("tensor", "dp"),
            P(("dp", "tensor"), None),
            P("dp", None),
            P(("dp", "tensor")),
        ),
        out_specs=(
            P(("dp", "tensor"), None),
            P(("dp", "tensor"), None),
            P("dp"),
            P(None, "dp", "tensor"),
            P(None, "tensor", "dp"),
            P("tensor", "dp"),
            P("tensor", "dp", None),
            P("dp", "tensor"),
            P("tensor", "dp"),
            P("tensor", "dp"),
            P("tensor", "dp"),
            P("tensor", "dp"),
        ),
        check_vma=False,
    )
```

```python
import functools

import jax
import jax.numpy as jnp
from jax import lax
from jax.experimental import pallas as pl
from jax.experimental.pallas import tpu as pltpu
from jax.sharding import PartitionSpec as P

EPSILON = 1e-05
FAR = 1e30
LANES = 128
STEP = 48
SPAN = 16
SMALL = pl.CostEstimate(flops=1, transcendentals=0, bytes_accessed=1)
NT = (((1,), (1,)), ((), ()))
TN = (((0,), (0,)), ((), ()))
F32 = jnp.float32
BF16 = jnp.bfloat16


def softplus(v):
    return jnp.maximum(v, 0.0) + jnp.log1p(jnp.exp(-jnp.abs(v)))


def sigmoid(v):
    return 1.0 / (1.0 + jnp.exp(-v))


def mm(a, b, dims=(((1,), (0,)), ((), ()))):
    return lax.dot_general(a, b, dims, preferred_element_type=F32)


def column_at(states, tokens):
    return lax.broadcasted_iota(jnp.int32, (states, tokens), 1)


def write_packed(out_ref, low, wide_ref):
    rows, rank = low.shape
    states = wide_ref.shape[0] // 2
    rest = rows - LANES
    out_ref[0, 0:rows, :] = low.astype(out_ref.dtype)
    out_ref[0, rows:rows + 2 * states, :] = wide_ref[:, 0:LANES].astype(out_ref.dtype)
    tail = wide_ref[:, LANES:2 * LANES]
    lane = lax.broadcasted_iota(jnp.int32, (states, LANES), 1)
    both = jnp.where(lane < rest, tail[:states], pltpu.roll(tail[states:], rest, 1))
    out_ref[0, rows + 2 * states:rows + 3 * states, :] = both.astype(out_ref.dtype)


def read_packed(in_ref, states):
    rows = in_ref.shape[1] - 3 * states
    rest = rows - LANES
    low = in_ref[0, 0:rows, :]
    head = in_ref[0, rows:rows + 2 * states, :].astype(F32)
    both = in_ref[0, rows + 2 * states:rows + 3 * states, :].astype(F32)
    first = jnp.concatenate([head[:states], both], axis=1)
    second = jnp.concatenate([head[states:], pltpu.roll(both, LANES - rest, 1)], axis=1)
    return low, first, second


def front_kernel(me_ref, inner_ref, offset_ref, taps_ref, shift_ref, low_ref, bc_ref, act_ref, part_ref, ext_s, wide_s):
    rows = inner_ref.shape[0]
    taps = taps_ref.shape[0]

    @pl.when(pl.program_id(0) == 0)
    def _():
        ext_s[0:8, :] = jnp.zeros((8, ext_s.shape[1]), F32)

    ext_s[8:8 + rows, :] = inner_ref[...].astype(F32)
    offset = offset_ref[...]
    conv = shift_ref[...] + taps_ref[0:1, :] * ext_s[8:8 + rows, :]
    for k in range(1, taps):
        conv += jnp.where(offset >= k, taps_ref[k:k + 1, :], 0.0) * ext_s[pl.ds(8 - k, rows), :]
    act = (conv * sigmoid(conv)).astype(BF16)
    act_ref[...] = act
    ext_s[0:8, :] = ext_s[rows:rows + 8, :]
    wide_s[:, 0:rows] = mm(bc_ref[...], act, NT)
    write_packed(part_ref, mm(act, low_ref[...]), wide_s)


def front(me, projected, offset, taps, shift, low_w, bc_w):
    tokens, channels = projected.shape[0], taps.shape[1]
    runs, rows = tokens // ROWS[0], ROWS[0]
    packed = rows + 3 * bc_w.shape[0] // 2
    row = lambda i, me: (i, 0)
    fixed = lambda i, me: (0, 0)
    return pl.pallas_call(
        front_kernel,
        name="front",
        grid_spec=pltpu.PrefetchScalarGridSpec(
            num_scalar_prefetch=1,
            grid=(runs,),
            in_specs=[
                pl.BlockSpec((rows, channels), row),
                pl.BlockSpec((rows, 1), row),
                pl.BlockSpec(taps.shape, fixed),
                pl.BlockSpec(shift.shape, fixed),
                pl.BlockSpec(low_w.shape, fixed),
                pl.BlockSpec(bc_w.shape, fixed),
            ],
            out_specs=[pl.BlockSpec((rows, channels), row), pl.BlockSpec((1, packed, LANES), lambda i, me: (i ^ me[0], 0, 0))],
            scratch_shapes=[pltpu.VMEM((rows + 8, channels), F32), pltpu.VMEM((bc_w.shape[0], 2 * LANES), F32)],
        ),
        out_shape=[
            pltpu.HBM((tokens, channels), BF16),
            jax.ShapeDtypeStruct((runs, packed, LANES), BF16),
        ],
        compiler_params=pltpu.CompilerParams(dimension_semantics=("arbitrary",), vmem_limit_bytes=8 << 20),
        cost_estimate=SMALL,
    )(me, in_hbm(projected), offset, taps, shift, low_w, bc_w)


ROWS = [192]


def spread_mask(rows, states):
    width = SPAN * states
    row = lax.broadcasted_iota(jnp.int32, (rows, width), 0) % SPAN
    return row == lax.broadcasted_iota(jnp.int32, (rows, width), 1) // states


def tile_matrix(states):
    width = SPAN * states
    row = lax.broadcasted_iota(jnp.int32, (states, width), 0)
    return (row == lax.broadcasted_iota(jnp.int32, (states, width), 1) % states).astype(BF16)


def spread_columns(columns, rows, states):
    tiled = mm(columns[:, 0:rows].astype(BF16), tile_matrix(states), TN)
    return jnp.where(spread_mask(rows, states), tiled, 0.0).astype(BF16)


def forward_kernel(kept, me_ref, pack_ref, act_ref, gate_ref, offset_ref, dw_ref, bias_ref, rate_ref, skip_ref, h_in, *rest):
    dt_ref, sp_ref, y_ref, gated_ref, hist_ref, h_s, dtm_s, u_s = rest[kept:]
    states, channels = rate_ref.shape
    chunk = act_ref.shape[0]

    @pl.when(pl.program_id(0) == 0)
    def _():
        h_s[...] = h_in[...]

    low, bt, ct = read_packed(pack_ref, states)
    wide = bt.shape[1]
    pre = mm(low, dw_ref[...]) + bias_ref[...]
    small = jnp.exp(-jnp.abs(pre))
    dt = jnp.maximum(pre, 0.0) + jnp.log1p(small)
    dt_ref[...] = dt
    sp_ref[...] = jnp.where(pre >= 0.0, 1.0, small) / (1.0 + small)
    act = act_ref[...].astype(F32)
    u_s[...] = dt * act
    dtm_s[...] = jnp.where(offset_ref[...] == 0, FAR, dt)
    rate = rate_ref[...]

    def group(g, h):
        base = pl.multiple_of(g * STEP, STEP)
        bg = pltpu.roll(bt, wide - base, 1)
        dtm = dtm_s[pl.ds(base, STEP), :]
        u = u_s[pl.ds(base, STEP), :]
        for j in range(STEP):
            a = jnp.exp(dtm[j:j + 1, :] * rate)
            h = a * h + u[j:j + 1, :] * bg[:, j:j + 1]
            at = pl.multiple_of((base + j) * states, states)
            hist_ref[pl.ds(at, states), :] = h.astype(BF16)
        return h

    h_s[...] = lax.fori_loop(0, chunk // STEP, group, h_s[...])
    spread = spread_columns(ct, chunk, states)
    width = SPAN * states
    for g in range(chunk // SPAN):
        rows = slice(g * SPAN, (g + 1) * SPAN)
        y_ref[rows, :] = mm(spread[rows, :], hist_ref[g * width:(g + 1) * width, :])
    y = y_ref[...] + skip_ref[...] * act
    y_ref[...] = y
    gate = gate_ref[...].astype(F32)
    gated_ref[...] = (y * gate * sigmoid(gate)).astype(BF16)


def scan_forward(me, pack, act, projected, offset, delta_w, bias, rate, skip, held, whole, first, steps):
    tokens, channels = act.shape
    states = rate.shape[0]
    chunk = ROWS[0]
    row = lambda i, me: (first + i, 0)
    fixed = lambda i, me: (0, 0)
    done = steps * chunk
    return pl.pallas_call(
        functools.partial(forward_kernel, len(whole)),
        name="scan_forward",
        grid_spec=pltpu.PrefetchScalarGridSpec(
            num_scalar_prefetch=1,
            grid=(steps,),
            in_specs=[
                pl.BlockSpec((1,) + pack.shape[1:], lambda i, me: ((first + i) ^ me[0], 0, 0)),
                pl.BlockSpec((chunk, channels), row),
                pl.BlockSpec((chunk, channels), lambda i, me: (first + i, 1)),
                pl.BlockSpec((chunk, 1), row),
                pl.BlockSpec(delta_w.shape, fixed),
                pl.BlockSpec(bias.shape, fixed),
                pl.BlockSpec(rate.shape, fixed),
                pl.BlockSpec(skip.shape, fixed),
                pl.BlockSpec(rate.shape, fixed),
            ] + [pl.BlockSpec(memory_space=pl.ANY)] * len(whole),
            out_specs=[
                pl.BlockSpec((chunk, channels), row),
                pl.BlockSpec((chunk, channels), row),
                pl.BlockSpec((chunk, channels), row),
                pl.BlockSpec((chunk, channels), row),
                pl.BlockSpec((chunk * states, channels), row),
                pl.BlockSpec(rate.shape, fixed),
            ],
            scratch_shapes=[
                pltpu.VMEM((chunk, channels), F32),
                pltpu.VMEM((chunk, channels), F32),
            ],
        ),
        out_shape=[
            pltpu.HBM((tokens, channels), F32),
            pltpu.HBM((tokens, channels), F32),
            pltpu.HBM((tokens, channels), F32),
            pltpu.HBM((tokens, channels), BF16),
            pltpu.HBM((tokens * states, channels), BF16),
            jax.ShapeDtypeStruct(rate.shape, F32),
        ],
        input_output_aliases={10 + i: i for i in range(len(whole))},
        compiler_params=pltpu.CompilerParams(dimension_semantics=("arbitrary",), vmem_limit_bytes=16 << 20),
        cost_estimate=SMALL,
    )(me, pack, in_hbm(act), in_hbm(projected), offset, delta_w, bias, rate, skip, held, *(in_hbm(v) for v in whole))


def backward_kernel(kept, me_ref, pack_ref, dt_ref, sp_ref, act_ref, gate_ref, gg_ref, y_ref, offset_ref,
                    hist_ref, prior_ref, dw_ref, rate_ref, skip_ref, carry_in, rgrad_in, dwgrad_in, rows_in, *rest):
    (ggate_ref, gact_ref, part_ref, carry_s, rgrad_ref, dwgrad_ref, rows_ref,
     dtm_s, u_s, gy_s, drive_s, decay_s, wide_s, adj_s, thr_s) = rest[kept:]
    states, channels = rate_ref.shape
    chunk = act_ref.shape[0]

    @pl.when(pl.program_id(0) == 0)
    def _():
        carry_s[...] = carry_in[...]
        rgrad_ref[...] = rgrad_in[...]
        dwgrad_ref[...] = dwgrad_in[...]
        rows_ref[...] = rows_in[...]

    low, bt, ct = read_packed(pack_ref, states)
    wide = bt.shape[1]
    dt = dt_ref[...]
    act = act_ref[...].astype(F32)
    u_s[...] = dt * act
    dtm_s[...] = jnp.where(offset_ref[...] == 0, FAR, dt)
    gate = gate_ref[...].astype(F32)
    sig = sigmoid(gate)
    gg = gg_ref[...].astype(F32) * sig
    gy = gg * gate
    gy_s[...] = gy
    ggate_ref[...] = (gg * y_ref[...] * (1.0 + gate * (1.0 - sig))).astype(BF16)
    rate = rate_ref[...]
    groups = chunk // STEP

    def group(k, held):
        carry, rgrad = held
        g = groups - 1 - k
        base = pl.multiple_of(g * STEP, STEP)
        cg = pltpu.roll(ct, wide - base, 1)
        dtm = dtm_s[pl.ds(base, STEP), :]
        dts = dt_ref[pl.ds(base, STEP), :]
        gys = gy_s[pl.ds(base, STEP), :]
        for j in reversed(range(STEP)):
            if j > 0:
                at = pl.multiple_of((base + j - 1) * states, states)
                prior = hist_ref[pl.ds(at, states), :].astype(F32)
            else:
                at = pl.multiple_of(jnp.maximum(base - 1, 0) * states, states)
                prior = jnp.where(base == 0, prior_ref[...], hist_ref[pl.ds(at, states), :]).astype(F32)
            a = jnp.exp(dtm[j:j + 1, :] * rate)
            adj = cg[:, j:j + 1] * gys[j:j + 1, :] + carry
            carry = a * adj
            through = carry * prior
            rgrad = rgrad + through * dts[j:j + 1, :]
            at = pl.multiple_of((base + j) * states, states)
            adj_s[pl.ds(at, states), :] = adj.astype(BF16)
            thr_s[pl.ds(at, states), :] = (through * rate).astype(BF16)
        return carry, rgrad

    carry, rgrad = lax.fori_loop(0, groups, group, (carry_s[...], rgrad_ref[...]))
    carry_s[...] = carry
    rgrad_ref[...] = rgrad
    spread = spread_columns(bt, chunk, states)
    ones = jnp.where(spread_mask(SPAN, states), 1.0, 0.0).astype(BF16)
    width = SPAN * states
    ub = u_s[...].astype(BF16)
    gyb = gy.astype(BF16)
    ahead = (lax.broadcasted_iota(jnp.int32, (width, chunk), 1)
             - lax.broadcasted_iota(jnp.int32, (width, chunk), 0) // states)
    gb_all = jnp.zeros((width, chunk), F32)
    gc_all = jnp.zeros((width, chunk), F32)
    for g in range(chunk // SPAN):
        rows = slice(g * SPAN, (g + 1) * SPAN)
        adj = adj_s[g * width:(g + 1) * width, :]
        drive_s[rows, :] = mm(spread[rows, :], adj)
        decay_s[rows, :] = mm(ones, thr_s[g * width:(g + 1) * width, :])
        gb_all = jnp.where(ahead == g * SPAN, mm(adj, ub, NT), gb_all)
        gc_all = jnp.where(ahead == g * SPAN, mm(hist_ref[g * width:(g + 1) * width, :], gyb, NT), gc_all)
    tiles = tile_matrix(states)
    wide_s[0:states, 0:chunk] = mm(tiles, gb_all.astype(BF16))
    wide_s[states:2 * states, 0:chunk] = mm(tiles, gc_all.astype(BF16))
    drive = drive_s[...]
    gact_ref[...] = drive * dt + gy * skip_ref[...]
    gpre = ((drive * act + decay_s[...]) * sp_ref[...]).astype(BF16)
    rows_ref[0:1, :] += jnp.sum(gy * act, axis=0, keepdims=True)
    rows_ref[1:2, :] += jnp.sum(gpre.astype(F32), axis=0, keepdims=True)
    dwgrad_ref[...] += mm(low, gpre, TN)
    write_packed(part_ref, mm(gpre, dw_ref[...], NT), wide_s)


def scan_backward(me, pack, dt, sp, act, projected, gg, y, offset, hist, delta_w, rate, skip, held, whole, last, steps):
    tokens, channels = act.shape
    states = rate.shape[0]
    chunk = ROWS[0]
    row = lambda i, me: (last - i, 0)
    second = lambda i, me: (last - i, 1)
    run = lambda i, me: ((last - i) ^ me[0], 0, 0)
    fixed = lambda i, me: (0, 0)
    blocks = [pl.BlockSpec((chunk, channels), second), pl.BlockSpec((chunk, channels), row), pl.BlockSpec((1,) + pack.shape[1:], run)]
    shapes = [
        pltpu.HBM((tokens, 2 * channels), BF16),
        pltpu.HBM((tokens, channels), F32),
        jax.ShapeDtypeStruct(pack.shape, BF16),
    ]
    sums = [pl.BlockSpec(v.shape, fixed) for v in held]
    done = steps * chunk
    return pl.pallas_call(
        functools.partial(backward_kernel, len(whole)),
        name="scan_backward",
        grid_spec=pltpu.PrefetchScalarGridSpec(
            num_scalar_prefetch=1,
            grid=(steps,),
            in_specs=[
                pl.BlockSpec((1,) + pack.shape[1:], run),
                pl.BlockSpec((chunk, channels), row),
                pl.BlockSpec((chunk, channels), row),
                pl.BlockSpec((chunk, channels), row),
                pl.BlockSpec((chunk, channels), second),
                pl.BlockSpec((chunk, channels), row),
                pl.BlockSpec((chunk, channels), row),
                pl.BlockSpec((chunk, 1), row),
                pl.BlockSpec((chunk * states, channels), row),
                pl.BlockSpec((states, channels), lambda i, me: (jnp.maximum((last - i) * chunk - 1, 0), 0)),
                pl.BlockSpec(delta_w.shape, fixed),
                pl.BlockSpec(rate.shape, fixed),
                pl.BlockSpec(skip.shape, fixed),
            ] + sums + [pl.BlockSpec(memory_space=pl.ANY)] * len(whole),
            out_specs=blocks + sums,
            scratch_shapes=[pltpu.VMEM((chunk, channels), F32)] * 5
            + [pltpu.VMEM((2 * states, 2 * LANES), F32)]
            + [pltpu.VMEM((chunk * states, channels), BF16)] * 2,
        ),
        out_shape=shapes + [jax.ShapeDtypeStruct(v.shape, F32) for v in held],
        input_output_aliases={18 + i: i for i in range(len(whole))},
        compiler_params=pltpu.CompilerParams(dimension_semantics=("arbitrary",), vmem_limit_bytes=24 << 20),
        cost_estimate=SMALL,
    )(me, pack, in_hbm(dt), in_hbm(sp), in_hbm(act), in_hbm(projected), in_hbm(gg), in_hbm(y), offset, in_hbm(hist), in_hbm(hist), delta_w, rate, skip, *held, *(in_hbm(v) if k == 1 else v for k, v in enumerate(whole)))


def end_kernel(me_ref, pack_ref, gact_ref, act_ref, inner_ref, prior_ref, offset_ref, taps_ref, shift_ref, low_ref, bc_ref, grad_ref,
               ginner_ref, tapg_ref, selow_ref, selbc_ref, ext_s, after_s, wide_s):
    rows, channels = inner_ref.shape
    taps = taps_ref.shape[0]
    states = bc_ref.shape[0] // 2

    @pl.when(pl.program_id(0) == 0)
    def _():
        after_s[...] = jnp.zeros_like(after_s)
        tapg_ref[...] = jnp.zeros_like(tapg_ref)
        selow_ref[...] = jnp.zeros_like(selow_ref)
        selbc_ref[...] = jnp.zeros_like(selbc_ref)

    low, gbt, gct = read_packed(pack_ref, states)
    wide_s[0:states, :] = gbt
    wide_s[states:2 * states, :] = gct
    gbc = wide_s[:, 0:rows].astype(BF16)
    act = act_ref[...]
    selow_ref[...] += mm(act, low, TN)
    selbc_ref[...] += mm(gbc, act)
    gact = gact_ref[...] + mm(low, low_ref[...], NT) + mm(gbc, bc_ref[...], TN)
    before = prior_ref.shape[0]
    ext_s[0:before, :] = prior_ref[...].astype(F32)
    ext_s[before:before + rows, :] = inner_ref[...].astype(F32)
    offset = offset_ref[...]
    conv = shift_ref[...] + taps_ref[0:1, :] * ext_s[before:before + rows, :]
    for k in range(1, taps):
        conv += jnp.where(offset >= k, taps_ref[k:k + 1, :], 0.0) * ext_s[pl.ds(before - k, rows), :]
    q = sigmoid(conv)
    gconv = gact * q * (1.0 + conv * (1.0 - q))
    tapg_ref[taps:taps + 1, :] += jnp.sum(gconv, axis=0, keepdims=True)
    tapg_ref[0:1, :] += jnp.sum(gconv * ext_s[before:before + rows, :], axis=0, keepdims=True)
    ginner = gconv * taps_ref[0:1, :]
    for k in range(1, taps):
        masked = jnp.where(offset >= k, gconv, 0.0)
        tapg_ref[k:k + 1, :] += jnp.sum(masked * ext_s[pl.ds(before - k, rows), :], axis=0, keepdims=True)
        after_s[k - 1, rows:rows + 8, :] = after_s[k - 1, 0:8, :]
        after_s[k - 1, 0:rows, :] = masked * taps_ref[k:k + 1, :]
        ginner += after_s[k - 1, pl.ds(k, rows), :]
    ginner_ref[...] = ginner.astype(BF16)


def end(me, pack, gact, act, projected, offset, taps, shift, low_w, bc_w, grad_projected):
    tokens, channels = act.shape
    rows = ROWS[0]
    steps = tokens // rows
    row = lambda i, me: (steps - 1 - i, 0)
    fixed = lambda i, me: (0, 0)
    return pl.pallas_call(
        end_kernel,
        name="end",
        grid_spec=pltpu.PrefetchScalarGridSpec(
            num_scalar_prefetch=1,
            grid=(steps,),
            in_specs=[
                pl.BlockSpec((1,) + pack.shape[1:], lambda i, me: ((steps - 1 - i) ^ me[0], 0, 0)),
                pl.BlockSpec((rows, channels), row),
                pl.BlockSpec((rows, channels), row),
                pl.BlockSpec((rows, channels), row),
                pl.BlockSpec((16, channels), lambda i, me: (jnp.maximum((steps - 1 - i) * (rows // 16) - 1, 0), 0)),
                pl.BlockSpec((rows, 1), row),
                pl.BlockSpec(taps.shape, fixed),
                pl.BlockSpec(shift.shape, fixed),
                pl.BlockSpec(low_w.shape, fixed),
                pl.BlockSpec(bc_w.shape, fixed),
                pl.BlockSpec(memory_space=pl.ANY),
            ],
            out_specs=[
                pl.BlockSpec((rows, channels), row),
                pl.BlockSpec((8, channels), fixed),
                pl.BlockSpec(low_w.shape, fixed),
                pl.BlockSpec(bc_w.shape, fixed),
            ],
            scratch_shapes=[
                pltpu.VMEM((rows + 16, channels), F32),
                pltpu.VMEM((3, rows + 8, channels), F32),
                pltpu.VMEM((bc_w.shape[0], 2 * LANES), F32),
            ],
        ),
        out_shape=[
            pltpu.HBM(grad_projected.shape, BF16),
            jax.ShapeDtypeStruct((8, channels), F32),
            jax.ShapeDtypeStruct(low_w.shape, F32),
            jax.ShapeDtypeStruct(bc_w.shape, F32),
        ],
        input_output_aliases={11: 0},
        compiler_params=pltpu.CompilerParams(dimension_semantics=("arbitrary",), vmem_limit_bytes=14 << 20),
        cost_estimate=SMALL,
    )(me, pack, in_hbm(gact), in_hbm(act), in_hbm(projected), in_hbm(projected), offset, taps, shift, low_w, bc_w, in_hbm(grad_projected))


def weight_grad_kernel(count, turned, table_ref, *refs):
    a_refs, b_refs = refs[:count], refs[count:2 * count]
    out_ref, a_s, b_s = refs[-3:]
    rows = a_refs[0].shape[0]
    for s in range(count):
        a_s[s * rows:(s + 1) * rows, :] = a_refs[s][...]

    @pl.when(pl.program_id(0) == 0)
    def _():
        for s in range(count):
            b_s[s * rows:(s + 1) * rows, :] = b_refs[s][...]

    first, second = (b_s, a_s) if turned else (a_s, b_s)
    out_ref[0] = mm(first[...], second[...], TN).astype(BF16)


def weight_grad(table, distances, shards, b, column, channels, size, turned, slots=1, slot=0, into=()):
    rows, width = shards[0].shape
    block = width // size
    count = len(shards)
    shape = (1, channels, block) if turned else (1, block, channels)
    if distances is None:
        b_specs = [pl.BlockSpec((rows, channels), lambda i, table: (0, column))]
    else:
        b_specs = [pl.BlockSpec((rows, channels), lambda i, table, d=d: (table[d], column)) for d in distances]
    return pl.pallas_call(
        functools.partial(weight_grad_kernel, count, turned),
        name="weight_grad",
        grid_spec=pltpu.PrefetchScalarGridSpec(
            num_scalar_prefetch=1,
            grid=(size,),
            in_specs=[pl.BlockSpec((rows, block), lambda i, table: (0, i))] * count
            + b_specs + [pl.BlockSpec(memory_space=pl.ANY)] * len(into),
            out_specs=pl.BlockSpec(shape, lambda i, table: (i, slot, 0)),
            scratch_shapes=[pltpu.VMEM((rows * count, block), BF16), pltpu.VMEM((rows * count, channels), BF16)],
        ),
        out_shape=pltpu.HBM((size, slots * shape[1], shape[2]), BF16),
        input_output_aliases={1 + 2 * count + k: k for k in range(len(into))},
        compiler_params=pltpu.CompilerParams(dimension_semantics=("arbitrary",), vmem_limit_bytes=16 << 20),
        cost_estimate=SMALL,
    )(table, *(in_hbm(v) for v in shards), *([in_hbm(b)] * count), *(in_hbm(v) for v in into))


def weight_block(weight, dims, blocks):
    if dims[0][1] == (0,):
        columns = weight.shape[1] // blocks
        return pl.BlockSpec((weight.shape[0], columns), lambda i, *rest: (0, i)), columns
    columns = weight.shape[0] // blocks
    return pl.BlockSpec((columns, weight.shape[1]), lambda i, *rest: (i, 0)), columns


def placed_kernel(dims, count, table_ref, *refs):
    w_ref, out_ref = refs[count], refs[-1]
    for s in range(count):
        @pl.when(pl.program_id(1) == s)
        def _(s=s):
            out_ref[...] = mm(refs[s][...], w_ref[...], dims).astype(out_ref.dtype)


def pick_entry(values, i):
    chosen = values[0]
    for k in range(1, len(values)):
        chosen = jnp.where(i == k, values[k], chosen)
    return chosen


def placed_product(table, distances, shards, weight, dims, out):
    rows, width = shards[0].shape
    count, blocks = len(shards), 2
    spec, columns = weight_block(weight, dims, blocks)
    return pl.pallas_call(
        functools.partial(placed_kernel, dims, count),
        name="placed_product",
        grid_spec=pltpu.PrefetchScalarGridSpec(
            num_scalar_prefetch=1,
            grid=(blocks, count),
            in_specs=[pl.BlockSpec((rows, width), lambda i, k, table: (0, 0))] * count
            + [spec, pl.BlockSpec(memory_space=pl.ANY)],
            out_specs=pl.BlockSpec((rows, columns), lambda i, k, table: (pick_entry([table[d] for d in distances], k), i)),
        ),
        out_shape=pltpu.HBM(out.shape, out.dtype),
        input_output_aliases={count + 2: 0},
        compiler_params=pltpu.CompilerParams(dimension_semantics=("arbitrary", "arbitrary"), vmem_limit_bytes=16 << 20),
        cost_estimate=SMALL,
    )(table, *(in_hbm(v) for v in shards), in_hbm(weight), in_hbm(out))


def placed_halves_kernel(cuts, table_ref, first_ref, second_ref, *refs):
    w_refs, out_ref = refs[:cuts], refs[-1]
    depth = w_refs[0].shape[0]
    each = first_ref.shape[1] // depth
    total = None
    for c in range(cuts):
        ref, at = (first_ref, c) if c < each else (second_ref, c - each)
        term = mm(ref[:, at * depth:(at + 1) * depth], w_refs[c][...])
        total = term if total is None else total + term
    out_ref[...] = total.astype(out_ref.dtype)


def placed_halves(table, distance, first, second, weight, out):
    rows, middle = first.shape
    cuts = 8
    depth, width = weight.shape[0] // cuts, weight.shape[1]
    return pl.pallas_call(
        functools.partial(placed_halves_kernel, cuts),
        name="placed_halves",
        grid_spec=pltpu.PrefetchScalarGridSpec(
            num_scalar_prefetch=1,
            grid=(1,),
            in_specs=[pl.BlockSpec((rows, middle), lambda i, table: (0, 0))] * 2
            + [pl.BlockSpec((depth, width), lambda i, table, c=c: (c, 0)) for c in range(cuts)]
            + [pl.BlockSpec(memory_space=pl.ANY)],
            out_specs=pl.BlockSpec((rows, width), lambda i, table: (table[distance], 0)),
        ),
        out_shape=pltpu.HBM(out.shape, out.dtype),
        input_output_aliases={3 + cuts: 0},
        compiler_params=pltpu.CompilerParams(dimension_semantics=("arbitrary",), vmem_limit_bytes=16 << 20),
        cost_estimate=SMALL,
    )(table, in_hbm(first), in_hbm(second), *([in_hbm(weight)] * cuts), in_hbm(out))


def in_hbm(value):
    return pltpu.with_memory_space_constraint(value, pltpu.HBM)


def far_kernel(cuts, table_ref, g_ref, t_ref, *refs):
    w_refs, (ahead_ref, behind_ref) = refs[:cuts], refs[cuts:]
    columns = w_refs[0].shape[0]
    for ref, first in ((ahead_ref, True), (behind_ref, False)):
        @pl.when((pl.program_id(0) == 0) == first)
        def _(ref=ref):
            for c in range(cuts):
                at = slice(c * columns, (c + 1) * columns)
                ref[:, at] = (mm(g_ref[...], w_refs[c][...], NT) + t_ref[:, at].astype(F32)).astype(BF16)


def pair_kernel(cuts, table_ref, ga_ref, gb_ref, ta_ref, tb_ref, *refs, halves=False):
    w_refs, (ra_ref, rb_ref, ahead_ref, behind_ref) = refs[:cuts], refs[cuts:]
    rows, columns = ga_ref.shape[0], w_refs[0].shape[0]
    both = jnp.concatenate([ga_ref[...], gb_ref[...]], axis=0)
    low = pl.program_id(0) == 0
    for c in range(cuts):
        at = slice(c * columns, (c + 1) * columns)
        total = mm(both, w_refs[c][...], NT)
        ra, rb = ra_ref[:, at].astype(F32), rb_ref[:, at].astype(F32)
        if halves:
            ra, rb = jnp.where(low, ra, 0.0), jnp.where(low, 0.0, rb)
        ahead_ref[:, at] = (total[:rows] + ta_ref[:, at].astype(F32) + ra).astype(BF16)
        behind_ref[:, at] = (total[rows:] + tb_ref[:, at].astype(F32) + rb).astype(BF16)


def own_kernel(cuts, table_ref, g_ref, t_ref, *refs):
    w_refs, (ra_ref, rb_ref, place_ref), outs = refs[:cuts], refs[cuts:cuts + 3], refs[cuts + 3:]
    columns = w_refs[0].shape[0]
    pair = outs[0].shape[0]
    for c in range(cuts):
        at = slice(c * columns, (c + 1) * columns)
        total = mm(g_ref[...], w_refs[c][...], NT) + t_ref[:, at].astype(F32)
        total = (total + ra_ref[:, at].astype(F32) + rb_ref[:, at].astype(F32)).astype(BF16)
        for d, out_ref in enumerate(outs):
            out_ref[:, at] = mm(place_ref[d * pair:(d + 1) * pair, :], total).astype(BF16)


def ring_step(kernel, table, distances, grads, terms, weight, arrived=(), place=None, pieces=1):
    rows, cuts = ROWS[0], 4
    width, channels = weight.shape[0], weight.shape[1] // 2
    half, columns = width // 2, width // (2 * cuts)
    fixed = lambda i, table: (0, 0)
    side = lambda i, table: (0, i)
    far = not arrived
    if far:
        outs, shape = [fixed, fixed], (rows, half)
    else:
        outs, shape = [side, side] if place is None else [side] * pieces, (rows // pieces, width)
    small = not far and arrived[0].shape[1] == half
    extra = [] if place is None else [place]
    return pl.pallas_call(
        functools.partial(kernel, cuts, halves=True) if small else functools.partial(kernel, cuts),
        name=kernel.__name__,
        grid_spec=pltpu.PrefetchScalarGridSpec(
            num_scalar_prefetch=1,
            grid=(2,),
            in_specs=[pl.BlockSpec((rows, channels), lambda i, table, d=d: (table[d], 0)) for d in distances]
            + [pl.BlockSpec((rows, half), lambda i, table, d=d: (table[d], i)) for d in distances]
            + [pl.BlockSpec((columns, channels), lambda i, table, c=c: (i * cuts + c, 0)) for c in range(cuts)]
            + [pl.BlockSpec((rows, half), fixed if small else side) for v in arrived]
            + [pl.BlockSpec(v.shape, fixed) for v in extra],
            out_specs=[pl.BlockSpec((shape[0], half), m) for m in outs],
        ),
        out_shape=[pltpu.HBM(shape, BF16) for m in outs],
        compiler_params=pltpu.CompilerParams(dimension_semantics=("arbitrary",), vmem_limit_bytes=24 << 20),
        cost_estimate=SMALL,
    )(table, *([in_hbm(grads)] * len(distances)), *([in_hbm(terms)] * len(distances)), *([in_hbm(weight)] * cuts),
      *(in_hbm(v) for v in arrived), *extra)


def blank(*shapes):
    hbm = pl.BlockSpec(memory_space=pl.ANY)
    return pl.pallas_call(
        lambda *refs: None, name="blank", out_specs=[hbm] * len(shapes),
        out_shape=[pltpu.HBM(*v) for v in shapes],
        cost_estimate=SMALL)()


def deal_kernel(x_ref, cot_ref, order_ref, gain_ref, me_ref, pick_ref, place_ref, *sends):
    rows = x_ref.shape[0]
    dp_size = order_ref.shape[0]
    me = me_ref[0]
    group_tokens = me_ref[1]
    pair = rows // dp_size
    order = order_ref[...].astype(jnp.int32)
    near = lax.broadcasted_iota(jnp.int32, (dp_size, rows), 0)
    other = near ^ me
    source = order // group_tokens
    local = order % rows
    before = (
        lax.broadcasted_iota(jnp.int32, (rows, rows), 0) < lax.broadcasted_iota(jnp.int32, (rows, rows), 1)
    ).astype(BF16)
    slots = lax.broadcasted_iota(jnp.int32, (rows, rows), 0)
    chosen = source == me
    rank = mm(chosen.astype(BF16), before).astype(jnp.int32)
    slot = jnp.where(chosen, near * pair + rank, -1)
    pick = jnp.zeros((rows, rows), F32)
    for d in range(dp_size):
        pick += mm((slots == slot[d:d + 1, :]).astype(BF16), (slots == local[d:d + 1, :]).astype(BF16), NT)
    pick = pick.astype(BF16)
    pick_ref[...] = pick
    mine = source[0:1, :]
    held = (mine == other).astype(BF16)
    ranks = mm(held, before).astype(jnp.int32)
    arrived = jnp.sum(jnp.where(mine == other, near * pair + ranks, 0), axis=0, keepdims=True)
    place_ref[...] = (slots == arrived).astype(BF16)
    x = x_ref[...].astype(F32)
    rinv = lax.rsqrt(jnp.mean(x * x, axis=1, keepdims=True) + EPSILON)
    normed = (x * rinv * gain_ref[...]).astype(BF16)
    for d in range(dp_size):
        at = slice(d * pair, (d + 1) * pair)
        sends[d][...] = mm(pick[at], normed).astype(BF16)
        sends[dp_size + d][...] = mm(pick[at], cot_ref[...]).astype(BF16)


def deal(x, cot, order, gain, me):
    rows, width = x.shape
    dp_size = order.shape[0]
    vm = pl.BlockSpec(memory_space=pltpu.VMEM)
    pick, place, *sends = pl.pallas_call(
        deal_kernel,
        name="deal",
        in_specs=[vm, vm, vm, vm, pl.BlockSpec(memory_space=pltpu.SMEM)],
        out_specs=[vm] * (2 + 2 * dp_size),
        out_shape=[jax.ShapeDtypeStruct((rows, rows), BF16)] * 2
        + [jax.ShapeDtypeStruct((rows // dp_size, width), BF16)] * (2 * dp_size),
        compiler_params=pltpu.CompilerParams(vmem_limit_bytes=32 << 20),
        cost_estimate=SMALL,
    )(x, cot, order, gain, me)
    return sends[:dp_size], sends[dp_size:], pick, place


def round_dot(a, b, dims=(((1,), (0,)), ((), ()))):
    return mm(a, b, dims).astype(BF16)


def after(value, *earlier):
    return lax.optimization_barrier((value,) + earlier)[0]


def flip(value, axis, bit):
    return lax.ppermute(value, axis, [(i, i ^ bit) for i in range(lax.axis_size(axis))])


def exchange(pieces, axis, stack=True):
    pieces = [pieces[0]] + [flip(pieces[d], axis, d) for d in range(1, lax.axis_size(axis))]
    return jnp.stack(pieces) if stack else pieces


def swap(values, axis):
    return lax.all_to_all(values, axis, split_axis=0, concat_axis=0, tiled=True)


def share(value, axis):
    return exchange([value] * lax.axis_size(axis), axis)


def in_order(pieces, axis):
    size, me, bit = lax.axis_size(axis), lax.axis_index(axis), 1
    while bit < size:
        split = pieces.reshape((size // (2 * bit), 2, bit) + pieces.shape[1:])
        turned = jnp.concatenate([split[:, 1:], split[:, :1]], axis=1)
        pieces = jnp.where((me // bit) % 2 == 1, turned, split).reshape(pieces.shape)
        bit *= 2
    return pieces


def cube_sum(value, axis, bit, end_bit):
    while bit < end_bit:
        value = value + flip(value, axis, bit)
        bit *= 2
    return value


class Bag(dict):
    def meet(self, values, *names):
        values, held = lax.optimization_barrier((values, {n: self[n] for n in names}))
        self.update(held)
        return values


def add_up(pieces):
    return jnp.sum(pieces.astype(F32), axis=0)


class Ring:
    def __init__(self, axis):
        self.axis = axis
        self.size = size = lax.axis_size(axis)
        columns = max(c for c in range(1, size) if size % c == 0 and c * c <= size)
        rows = size // columns
        cycle = [(0, c) for c in range(columns)]
        for r in range(1, rows):
            snake = range(1, columns)
            cycle += [(r, c) for c in (snake if r % 2 == 0 else reversed(snake))]
        cycle += [(r, 0) for r in reversed(range(1, rows))]
        order = [r * columns + c for r, c in cycle]
        place = {t: i for i, t in enumerate(order)}
        table = jnp.array([[order[(place[t] + d) % size] for d in range(size)] for t in range(size)], jnp.int32)
        self.at = lax.dynamic_index_in_dim(table, lax.axis_index(axis), 0, keepdims=False)
        self.forward = [(order[i], order[(i + 1) % size]) for i in range(size)]
        self.backward = [(b, a) for a, b in self.forward]

    def hop(self, value, ahead):
        return lax.ppermute(value, self.axis, self.forward if ahead else self.backward)


def ring_gather(ring, own, between):
    half, size = ring.size // 2, ring.size
    middle = own.shape[1] // 2
    distances, shards = [0], [own]
    ahead = behind = own
    for d in range(1, half):
        ahead, behind = between(d, ring.hop(ahead, True), ring.hop(behind, False))
        distances += [size - d, d]
        shards += [ahead, behind]
    halves = between(half, ring.hop(ahead[:, :middle], True), ring.hop(behind[:, middle:], False))
    return distances + [half], shards, halves


def ring_reduce(ring, grads, terms, weight, place, pieces, between):
    half, size = ring.size // 2, ring.size
    step = functools.partial(ring_step, table=ring.at, grads=grads, terms=terms, weight=weight)
    ahead, behind = step(far_kernel, distances=[half])
    for d in range(half, 0, -1):
        ahead, behind = between(half - d, ahead, ring.hop(ahead, True), ring.hop(behind, False))
        if d > 1:
            ahead, behind = step(pair_kernel, distances=[d - 1, size + 1 - d], arrived=[ahead, behind])
    return step(own_kernel, distances=[0], arrived=[ahead, behind], place=place, pieces=pieces)


def shards(
    block_input, norm_gain, in_weight, conv_weight, conv_bias, select_weight, delta_weight, delta_bias,
    decay_log, skip_weight, out_weight, out_cotangent, seq_lengths, deal_order,
):
    rows_dev, width = block_input.shape
    dp_size = lax.axis_size("dp")
    tensor_size = lax.axis_size("tensor")
    pair = rows_dev // dp_size
    group_tokens = rows_dev * tensor_size
    ring = Ring("tensor")
    here = jnp.zeros((1,), jnp.int32)
    me = jnp.stack([lax.axis_index("dp"), jnp.int32(group_tokens)]).astype(jnp.int32)
    head = share(jnp.concatenate([deal_order.astype(F32), norm_gain.astype(F32)]), "dp")
    gain_values = in_order(head[:, rows_dev:], "dp").reshape(1, -1)
    send_rows, send_cot, pick, place = deal(block_input, out_cotangent, head[:, :rows_dev], gain_values, me)
    in_cat = jnp.swapaxes(after(in_weight, send_rows[0]), 0, 1).reshape(in_weight.shape[1], -1)
    recv_rows = exchange(send_rows, "dp")
    recv_rows, in_cat = lax.optimization_barrier((recv_rows, in_cat))
    in_full = lax.all_gather(in_cat, "dp", axis=0, tiled=True)
    normed = round_dot(place, recv_rows.reshape(rows_dev, -1), TN)
    channels = in_full.shape[1] // 2
    taps = conv_weight.shape[0]
    lane_width = conv_bias.shape[1] * dp_size
    own_states = decay_log.shape[1]
    states, low_rank = own_states * dp_size, delta_weight.shape[0] * dp_size
    lengths_row = seq_lengths[0]
    seq_ends = jnp.cumsum(lengths_row)
    begins = seq_ends - lengths_row
    positions = jnp.arange(group_tokens, dtype=jnp.int32)
    inside = (positions[:, None] >= begins[None, :]) & (positions[:, None] < seq_ends[None, :])
    offset = (positions - jnp.sum(jnp.where(inside, begins[None, :], 0), axis=1))[:, None]
    (projected,) = blank(((group_tokens, 2 * channels), BF16))
    half = tensor_size // 2
    NN = (((1,), (0,)), ((), ()))
    lanes_own = jnp.concatenate([conv_weight, jnp.stack([conv_bias, delta_bias, skip_weight])])
    bag = Bag(
        cot=send_cot, select=jnp.concatenate([select_weight, jnp.moveaxis(lanes_own, 0, 2)], axis=2),
        thin=jnp.concatenate([decay_log.T, delta_weight]), projected=projected)
    waiting = {"shards": [normed], "distances": [0]}

    def during_normed(d, ahead, behind):
        if d == 1:
            ahead, behind = bag.meet((ahead, behind), "select")
            bag["select"] = share(bag["select"], "dp")
            bag["own"] = out_weight
        elif d < half - 1:
            ahead, behind = bag.meet((ahead, behind), "own", "select", "cot")
            if d == 2:
                bag["cot"] = exchange(bag["cot"], "dp")
        elif d >= half - 1:
            bag["projected"] = placed_product(
                ring.at, waiting["distances"], waiting["shards"], in_full, NN, bag["projected"])
            waiting["shards"], waiting["distances"] = [], []
            ahead, behind = bag.meet((ahead, behind), "projected", *(["cot"] if d == half else []))
        if d < half:
            waiting["distances"] += [tensor_size - d, d]
            waiting["shards"] += [ahead, behind]
        return ahead, behind

    distances, normed_shards, halves = ring_gather(ring, normed, during_normed)

    def rows_of(values, distance):
        return lax.dynamic_slice(values, (ring.at[distance] * rows_dev, 0), (rows_dev, values.shape[1]))

    projected = placed_halves(ring.at, distances[-1], *halves, in_full, bag["projected"])
    dealt_cot = round_dot(place, bag["cot"].reshape(rows_dev, -1), TN)
    select_matrix = jnp.moveaxis(in_order(bag["select"], "dp"), 0, 1).reshape(channels, -1)
    low_w, bc_w = select_matrix[:, :low_rank], select_matrix[:, low_rank:low_rank + 2 * states].T
    lanes_float = select_matrix[:, low_rank + 2 * states:].astype(F32).T
    conv_taps = lanes_float[:taps]
    conv_shift, delta_shift, skip_values = (lanes_float[taps + i:taps + i + 1] for i in range(3))
    activated, part = front(here, projected, offset, conv_taps, conv_shift, low_w, bc_w)
    out_full = lax.all_gather(bag["own"], "dp", axis=1, tiled=True)
    group_cot = lax.all_gather(after(dealt_cot, halves[0]), "tensor", axis=0, tiled=True)
    bag["thin"] = lax.all_gather(after(bag["thin"], part)[None], "dp", axis=0, tiled=True)
    bag["last"] = jnp.concatenate([after(v, part) for v in halves], axis=1)
    arrived = bag.meet(swap(part, "tensor"), "thin", "last")
    normed_shards = normed_shards + [bag["last"]]
    decay_full = bag["thin"][:, :own_states].reshape(states, channels)
    delta_full = bag["thin"][:, own_states:].reshape(low_rank, channels)
    decay_rate = -jnp.exp(decay_full.astype(F32))
    total = jnp.sum(arrived.astype(F32), axis=0).astype(BF16)
    pack_all = swap(jnp.broadcast_to(total[None], part.shape), "tensor")
    step_size, slope, y, gated, hist, unused_state = scan_forward(
        here, pack_all, activated, projected, offset, delta_full, delta_shift, decay_rate, skip_values,
        jnp.zeros((states, channels), F32), [], 0, tensor_size)
    gg = mm(group_cot, out_full, NT)
    held = [
        jnp.zeros((states, channels), F32),
        jnp.zeros((states, channels), F32),
        jnp.zeros((low_rank, channels), F32),
        jnp.zeros((8, channels), F32),
    ]
    mixed = lax.psum_scatter(round_dot(gated, out_full), "tensor", scatter_dimension=0, tiled=True)
    grad_projected, grad_act, grad_part, unused_carry, rate_grad, delta_weight_grad, row_grads = scan_backward(
        here, pack_all, step_size, slope, activated, projected, gg, y, offset, hist, delta_full, decay_rate, skip_values,
        held, [], tensor_size - 1, tensor_size)
    decay_grad = rate_grad * decay_rate
    def by_lane(values):
        lanes = values.reshape(-1, channels // lane_width, dp_size, lane_width // dp_size)
        return jnp.moveaxis(lanes, 2, 0).reshape(dp_size, -1)

    def pack_scan(row_grads, decay_grad, delta_weight_grad):
        parts = [by_lane(row_grads[:2]), decay_grad.reshape(dp_size, -1), delta_weight_grad.reshape(dp_size, -1)]
        return jnp.concatenate(parts, axis=1).astype(BF16), [part.shape[1] for part in parts]

    def pack_conv(packed, taps_sum, low_sum, bc_sum):
        select_grad = jnp.concatenate([low_sum, bc_sum.T], axis=1)
        parts = [
            packed,
            by_lane(taps_sum[:taps + 1]).astype(BF16),
            jnp.moveaxis(select_grad.reshape(channels // lane_width, dp_size, -1), 1, 0).reshape(dp_size, -1).astype(BF16),
        ]
        flat = jnp.concatenate(parts, axis=1)
        flat = jnp.pad(flat, ((0, 0), (0, -flat.shape[1] % 2048))).reshape(dp_size, -1, LANES)
        return flat, [part.shape[1] for part in parts[1:]]

    merged = channels == width // dp_size
    bag["out"] = weight_grad(
        ring.at, None, [group_cot], after(gated, grad_part), 0, channels, dp_size, True, 2 if merged else 1)
    arrived = bag.meet(swap(grad_part, "tensor"), "out")
    grad_total = jnp.sum(arrived.astype(F32), axis=0).astype(BF16)
    bag["gate"] = weight_grad(
        ring.at, distances, normed_shards, after(grad_projected, grad_total), 1, channels, dp_size, False,
        *((2, 1, [bag["out"]]) if merged else ()))
    bag["packed"], sizes = pack_scan(*(after(v, grad_total) for v in (row_grads, decay_grad, delta_weight_grad)))
    bag["terms"] = round_dot(after(grad_projected, grad_total)[:, channels:], in_full[:, channels:], NT)
    grad_pack = bag.meet(swap(jnp.broadcast_to(grad_total[None], grad_part.shape), "tensor"), "gate", "terms", "packed")
    gate_terms = bag["terms"]
    bag["gate"] = lax.psum_scatter(bag["gate"], "dp", scatter_dimension=0, tiled=True)
    if not merged:
        bag["out"] = lax.psum_scatter(bag["out"], "dp", scatter_dimension=0, tiled=True)
    grad_projected, *sums = end(
        here, grad_pack, grad_act, activated, projected, offset, conv_taps, conv_shift, low_w, bc_w, grad_projected)
    bag["sums"] = [bag["packed"], *sums]
    bag["mixed"] = mixed

    def during_grad(k, sent, ahead, behind):
        names = []
        if k == 0:
            bag["grads"] = grad_projected
            names = ["mixed", "sums", "grads"]
        if k == 1:
            bag["inner"] = weight_grad(
                ring.at, distances, normed_shards, after(bag["grads"], sent), 0, channels, dp_size, False)
            names = ["mixed", "sums", "inner"]
        if k == half - 2:
            flat, more = pack_conv(*after(tuple(bag["sums"]), sent))
            sizes.extend(more)
            bag["flat"] = swap(flat, "dp")
            names = ["mixed", "flat", "gate"] + ([] if merged else ["out"])
        ahead, behind = bag.meet((ahead, behind), *names)
        if k == half - 2:
            bag["mixed"] = exchange(round_dot(place, bag["mixed"]).reshape(dp_size, pair, -1), "dp")
        if k == 1:
            bag["inner"] = lax.psum_scatter(bag["inner"], "dp", scatter_dimension=0, tiled=True)
        return ahead, behind

    send_grad = ring_reduce(ring, grad_projected, gate_terms, in_full, place, dp_size, during_grad)
    home_grad = exchange(send_grad, "dp").reshape(rows_dev, -1)
    home_out = bag["mixed"].reshape(rows_dev, -1)
    out_grad = (bag["gate"][0, :channels] if merged else bag["out"][0]).astype(F32)
    gate_grad = bag["gate"][:, channels:] if merged else bag["gate"]
    inner_grad = after(bag["inner"], send_grad[0])
    bag["in"] = jnp.concatenate([inner_grad, gate_grad]).astype(F32)
    gain_part = jnp.sum(in_weight.astype(F32) * bag["in"], axis=(0, 2))
    in_weight_grad = bag["in"]
    gain_parts = swap(jnp.broadcast_to(gain_part.reshape(1, -1, LANES), (tensor_size, gain_part.size // LANES, LANES)), "tensor")
    gain_grad = add_up(gain_parts).reshape(-1) / norm_gain.astype(F32)
    flat = jnp.sum(bag["flat"].astype(F32), axis=0).reshape(-1)
    small, start = [], 0
    for size in sizes:
        small.append(flat[start:start + size])
        start += size
    scan_grads = small[0].reshape((2,) + conv_bias.shape)
    lane_grads = small[3].reshape((taps + 1,) + conv_bias.shape)
    rows_float = block_input.astype(F32)
    block_output = (rows_float + mm(pick, home_out, TN)).astype(BF16)
    inverse_rms = lax.rsqrt(jnp.mean(rows_float * rows_float, axis=1, keepdims=True) + EPSILON)
    unit_rows = rows_float * inverse_rms
    scaled = mm(pick, home_grad, TN) * gain_values
    input_grad = (
        out_cotangent.astype(F32)
        + inverse_rms * (scaled - unit_rows * jnp.mean(scaled * unit_rows, axis=1, keepdims=True))
    ).astype(BF16)
    return (
        block_output,
        input_grad,
        gain_grad,
        in_weight_grad,
        lane_grads[:taps],
        lane_grads[taps],
        small[4].reshape(select_weight.shape),
        small[2].reshape(delta_weight.shape),
        scan_grads[1],
        small[1].reshape(decay_log.shape[1], decay_log.shape[0]).T,
        scan_grads[0],
        out_grad,
    )


def solution(mesh):
    return jax.shard_map(
        shards,
        mesh=mesh,
        in_specs=(
            P(("dp", "tensor"), None),
            P("dp"),
            P(None, "dp", "tensor"),
            P(None, "tensor", "dp"),
            P("tensor", "dp"),
            P("tensor", "dp", None),
            P("dp", "tensor"),
            P("tensor", "dp"),
            P("tensor", "dp"),
            P("tensor", "dp"),
            P("tensor", "dp"),
            P(("dp", "tensor"), None),
            P("dp", None),
            P(("dp", "tensor")),
        ),
        out_specs=(
            P(("dp", "tensor"), None),
            P(("dp", "tensor"), None),
            P("dp"),
            P(None, "dp", "tensor"),
            P(None, "tensor", "dp"),
            P("tensor", "dp"),
            P("tensor", "dp", None),
            P("dp", "tensor"),
            P("tensor", "dp"),
            P("tensor", "dp"),
            P("tensor", "dp"),
            P("tensor", "dp"),
        ),
        check_vma=False,
    )
```

```python
import functools

import jax
import jax.numpy as jnp
from jax import lax
from jax.experimental import pallas as pl
from jax.experimental.pallas import tpu as pltpu
from jax.sharding import PartitionSpec as P

EPSILON = 1e-05
FAR = 1e30
LANES = 128
STEP = 96
SPAN = 16
SMALL = pl.CostEstimate(flops=1, transcendentals=0, bytes_accessed=1)
NT = (((1,), (1,)), ((), ()))
TN = (((0,), (0,)), ((), ()))
F32 = jnp.float32
BF16 = jnp.bfloat16


def softplus(v):
    return jnp.maximum(v, 0.0) + jnp.log1p(jnp.exp(-jnp.abs(v)))


def sigmoid(v):
    return 1.0 / (1.0 + jnp.exp(-v))


def mm(a, b, dims=(((1,), (0,)), ((), ()))):
    return lax.dot_general(a, b, dims, preferred_element_type=F32)


def column_at(states, tokens):
    return lax.broadcasted_iota(jnp.int32, (states, tokens), 1)


def write_packed(out_ref, low, wide_ref):
    rows, rank = low.shape
    states = wide_ref.shape[0] // 2
    rest = rows - LANES
    out_ref[0, 0:rows, :] = low.astype(out_ref.dtype)
    out_ref[0, rows:rows + 2 * states, :] = wide_ref[:, 0:LANES].astype(out_ref.dtype)
    tail = wide_ref[:, LANES:2 * LANES]
    lane = lax.broadcasted_iota(jnp.int32, (states, LANES), 1)
    both = jnp.where(lane < rest, tail[:states], pltpu.roll(tail[states:], rest, 1))
    out_ref[0, rows + 2 * states:rows + 3 * states, :] = both.astype(out_ref.dtype)


def read_packed(in_ref, states):
    rows = in_ref.shape[1] - 3 * states
    rest = rows - LANES
    low = in_ref[0, 0:rows, :]
    head = in_ref[0, rows:rows + 2 * states, :].astype(F32)
    both = in_ref[0, rows + 2 * states:rows + 3 * states, :].astype(F32)
    first = jnp.concatenate([head[:states], both], axis=1)
    second = jnp.concatenate([head[states:], pltpu.roll(both, LANES - rest, 1)], axis=1)
    return low, first, second


def front_kernel(me_ref, inner_ref, offset_ref, taps_ref, shift_ref, low_ref, bc_ref, act_ref, part_ref, ext_s, wide_s):
    rows = inner_ref.shape[0]
    taps = taps_ref.shape[0]

    @pl.when(pl.program_id(0) == 0)
    def _():
        ext_s[0:8, :] = jnp.zeros((8, ext_s.shape[1]), F32)

    ext_s[8:8 + rows, :] = inner_ref[...].astype(F32)
    offset = offset_ref[...]
    conv = shift_ref[...] + taps_ref[0:1, :] * ext_s[8:8 + rows, :]
    for k in range(1, taps):
        conv += jnp.where(offset >= k, taps_ref[k:k + 1, :], 0.0) * ext_s[pl.ds(8 - k, rows), :]
    act = (conv * sigmoid(conv)).astype(BF16)
    act_ref[...] = act
    ext_s[0:8, :] = ext_s[rows:rows + 8, :]
    wide_s[:, 0:rows] = mm(bc_ref[...], act, NT)
    write_packed(part_ref, mm(act, low_ref[...]), wide_s)


def front(me, projected, offset, taps, shift, low_w, bc_w):
    tokens, channels = projected.shape[0], taps.shape[1]
    runs, rows = tokens // ROWS[0], ROWS[0]
    packed = rows + 3 * bc_w.shape[0] // 2
    row = lambda i, me: (i, 0)
    fixed = lambda i, me: (0, 0)
    return pl.pallas_call(
        front_kernel,
        name="front",
        grid_spec=pltpu.PrefetchScalarGridSpec(
            num_scalar_prefetch=1,
            grid=(runs,),
            in_specs=[
                pl.BlockSpec((rows, channels), row),
                pl.BlockSpec((rows, 1), row),
                pl.BlockSpec(taps.shape, fixed),
                pl.BlockSpec(shift.shape, fixed),
                pl.BlockSpec(low_w.shape, fixed),
                pl.BlockSpec(bc_w.shape, fixed),
            ],
            out_specs=[pl.BlockSpec((rows, channels), row), pl.BlockSpec((1, packed, LANES), lambda i, me: (i ^ me[0], 0, 0))],
            scratch_shapes=[pltpu.VMEM((rows + 8, channels), F32), pltpu.VMEM((bc_w.shape[0], 2 * LANES), F32)],
        ),
        out_shape=[
            pltpu.HBM((tokens, channels), BF16),
            jax.ShapeDtypeStruct((runs, packed, LANES), BF16),
        ],
        compiler_params=pltpu.CompilerParams(dimension_semantics=("arbitrary",), vmem_limit_bytes=8 << 20),
        cost_estimate=SMALL,
    )(me, in_hbm(projected), offset, taps, shift, low_w, bc_w)


ROWS = [192]


def spread_mask(rows, states):
    width = SPAN * states
    row = lax.broadcasted_iota(jnp.int32, (rows, width), 0) % SPAN
    return row == lax.broadcasted_iota(jnp.int32, (rows, width), 1) // states


def tile_matrix(states):
    width = SPAN * states
    row = lax.broadcasted_iota(jnp.int32, (states, width), 0)
    return (row == lax.broadcasted_iota(jnp.int32, (states, width), 1) % states).astype(BF16)


def spread_columns(columns, rows, states):
    tiled = mm(columns[:, 0:rows].astype(BF16), tile_matrix(states), TN)
    return jnp.where(spread_mask(rows, states), tiled, 0.0).astype(BF16)


def forward_kernel(kept, me_ref, pack_ref, act_ref, gate_ref, offset_ref, dw_ref, bias_ref, rate_ref, skip_ref, h_in, *rest):
    dt_ref, sp_ref, y_ref, gated_ref, hist_ref, h_s, dtm_s, u_s = rest[kept:]
    states, channels = rate_ref.shape
    chunk = act_ref.shape[0]

    @pl.when(pl.program_id(0) == 0)
    def _():
        h_s[...] = h_in[...]

    low, bt, ct = read_packed(pack_ref, states)
    wide = bt.shape[1]
    pre = mm(low, dw_ref[...]) + bias_ref[...]
    small = jnp.exp(-jnp.abs(pre))
    dt = jnp.maximum(pre, 0.0) + jnp.log1p(small)
    dt_ref[...] = dt
    sp_ref[...] = jnp.where(pre >= 0.0, 1.0, small) / (1.0 + small)
    act = act_ref[...].astype(F32)
    u_s[...] = dt * act
    dtm_s[...] = jnp.where(offset_ref[...] == 0, FAR, dt)
    rate = rate_ref[...]

    def group(g, h):
        base = pl.multiple_of(g * STEP, STEP)
        bg = pltpu.roll(bt, wide - base, 1)
        dtm = dtm_s[pl.ds(base, STEP), :]
        u = u_s[pl.ds(base, STEP), :]
        for j in range(STEP):
            a = jnp.exp(dtm[j:j + 1, :] * rate)
            h = a * h + u[j:j + 1, :] * bg[:, j:j + 1]
            at = pl.multiple_of((base + j) * states, states)
            hist_ref[pl.ds(at, states), :] = h.astype(BF16)
        return h

    h_s[...] = lax.fori_loop(0, chunk // STEP, group, h_s[...])
    spread = spread_columns(ct, chunk, states)
    width = SPAN * states
    for g in range(chunk // SPAN):
        rows = slice(g * SPAN, (g + 1) * SPAN)
        y_ref[rows, :] = mm(spread[rows, :], hist_ref[g * width:(g + 1) * width, :])
    y = y_ref[...] + skip_ref[...] * act
    y_ref[...] = y
    gate = gate_ref[...].astype(F32)
    gated_ref[...] = (y * gate * sigmoid(gate)).astype(BF16)


def scan_forward(me, pack, act, projected, offset, delta_w, bias, rate, skip, held, whole, first, steps):
    tokens, channels = act.shape
    states = rate.shape[0]
    chunk = ROWS[0]
    row = lambda i, me: (first + i, 0)
    fixed = lambda i, me: (0, 0)
    done = steps * chunk
    return pl.pallas_call(
        functools.partial(forward_kernel, len(whole)),
        name="scan_forward",
        grid_spec=pltpu.PrefetchScalarGridSpec(
            num_scalar_prefetch=1,
            grid=(steps,),
            in_specs=[
                pl.BlockSpec((1,) + pack.shape[1:], lambda i, me: ((first + i) ^ me[0], 0, 0)),
                pl.BlockSpec((chunk, channels), row),
                pl.BlockSpec((chunk, channels), lambda i, me: (first + i, 1)),
                pl.BlockSpec((chunk, 1), row),
                pl.BlockSpec(delta_w.shape, fixed),
                pl.BlockSpec(bias.shape, fixed),
                pl.BlockSpec(rate.shape, fixed),
                pl.BlockSpec(skip.shape, fixed),
                pl.BlockSpec(rate.shape, fixed),
            ] + [pl.BlockSpec(memory_space=pl.ANY)] * len(whole),
            out_specs=[
                pl.BlockSpec((chunk, channels), row),
                pl.BlockSpec((chunk, channels), row),
                pl.BlockSpec((chunk, channels), row),
                pl.BlockSpec((chunk, channels), row),
                pl.BlockSpec((chunk * states, channels), row),
                pl.BlockSpec(rate.shape, fixed),
            ],
            scratch_shapes=[
                pltpu.VMEM((chunk, channels), F32),
                pltpu.VMEM((chunk, channels), F32),
            ],
        ),
        out_shape=[
            pltpu.HBM((tokens, channels), F32),
            pltpu.HBM((tokens, channels), F32),
            pltpu.HBM((tokens, channels), F32),
            pltpu.HBM((tokens, channels), BF16),
            pltpu.HBM((tokens * states, channels), BF16),
            jax.ShapeDtypeStruct(rate.shape, F32),
        ],
        input_output_aliases={10 + i: i for i in range(len(whole))},
        compiler_params=pltpu.CompilerParams(dimension_semantics=("arbitrary",), vmem_limit_bytes=16 << 20),
        cost_estimate=SMALL,
    )(me, pack, in_hbm(act), in_hbm(projected), offset, delta_w, bias, rate, skip, held, *(in_hbm(v) for v in whole))


def backward_kernel(kept, me_ref, pack_ref, dt_ref, sp_ref, act_ref, gate_ref, gg_ref, y_ref, offset_ref,
                    hist_ref, prior_ref, dw_ref, rate_ref, skip_ref, carry_in, rgrad_in, dwgrad_in, rows_in, *rest):
    (ggate_ref, gact_ref, part_ref, carry_s, rgrad_ref, dwgrad_ref, rows_ref,
     dtm_s, u_s, gy_s, drive_s, decay_s, wide_s, adj_s, thr_s) = rest[kept:]
    states, channels = rate_ref.shape
    chunk = act_ref.shape[0]

    @pl.when(pl.program_id(0) == 0)
    def _():
        carry_s[...] = carry_in[...]
        rgrad_ref[...] = rgrad_in[...]
        dwgrad_ref[...] = dwgrad_in[...]
        rows_ref[...] = rows_in[...]

    low, bt, ct = read_packed(pack_ref, states)
    wide = bt.shape[1]
    dt = dt_ref[...]
    act = act_ref[...].astype(F32)
    u_s[...] = dt * act
    dtm_s[...] = jnp.where(offset_ref[...] == 0, FAR, dt)
    gate = gate_ref[...].astype(F32)
    sig = sigmoid(gate)
    gg = gg_ref[...].astype(F32) * sig
    gy = gg * gate
    gy_s[...] = gy
    ggate_ref[...] = (gg * y_ref[...] * (1.0 + gate * (1.0 - sig))).astype(BF16)
    rate = rate_ref[...]
    groups = chunk // STEP

    def group(k, held):
        carry, rgrad = held
        g = groups - 1 - k
        base = pl.multiple_of(g * STEP, STEP)
        cg = pltpu.roll(ct, wide - base, 1)
        dtm = dtm_s[pl.ds(base, STEP), :]
        dts = dt_ref[pl.ds(base, STEP), :]
        gys = gy_s[pl.ds(base, STEP), :]
        for j in reversed(range(STEP)):
            if j > 0:
                at = pl.multiple_of((base + j - 1) * states, states)
                prior = hist_ref[pl.ds(at, states), :].astype(F32)
            else:
                at = pl.multiple_of(jnp.maximum(base - 1, 0) * states, states)
                prior = jnp.where(base == 0, prior_ref[...], hist_ref[pl.ds(at, states), :]).astype(F32)
            a = jnp.exp(dtm[j:j + 1, :] * rate)
            adj = cg[:, j:j + 1] * gys[j:j + 1, :] + carry
            carry = a * adj
            through = carry * prior
            rgrad = rgrad + through * dts[j:j + 1, :]
            at = pl.multiple_of((base + j) * states, states)
            adj_s[pl.ds(at, states), :] = adj.astype(BF16)
            scaled = through * rate
            scaled = scaled[:states // 2] + scaled[states // 2:]
            if j % 2:
                later = scaled
            else:
                at = pl.multiple_of((base + j) * (states // 2), states)
                thr_s[pl.ds(at, states), :] = jnp.concatenate([scaled, later], axis=0).astype(BF16)
        return carry, rgrad

    carry, rgrad = lax.fori_loop(0, groups, group, (carry_s[...], rgrad_ref[...]))
    carry_s[...] = carry
    rgrad_ref[...] = rgrad
    spread = spread_columns(bt, chunk, states)
    width = SPAN * states
    ones = (
        lax.broadcasted_iota(jnp.int32, (2 * SPAN, width), 0)
        == lax.broadcasted_iota(jnp.int32, (2 * SPAN, width), 1) // (states // 2)
    ).astype(BF16)
    ub = u_s[...].astype(BF16)
    gyb = gy.astype(BF16)
    ahead = (lax.broadcasted_iota(jnp.int32, (width, chunk), 1)
             - lax.broadcasted_iota(jnp.int32, (width, chunk), 0) // states)
    gb_wide = mm(adj_s[...], ub, NT)
    gc_wide = mm(hist_ref[...], gyb, NT)
    gb_all = jnp.zeros((width, chunk), F32)
    gc_all = jnp.zeros((width, chunk), F32)
    for g in range(chunk // SPAN):
        rows = slice(g * SPAN, (g + 1) * SPAN)
        adj = adj_s[g * width:(g + 1) * width, :]
        drive_s[rows, :] = mm(spread[rows, :], adj)
        if g % 2 == 0:
            pair = slice(g * SPAN, (g + 2) * SPAN)
            decay_s[pair, :] = mm(ones, thr_s[g * width // 2:(g + 2) * width // 2, :])
        gb_all = jnp.where(ahead == g * SPAN, gb_wide[g * width:(g + 1) * width], gb_all)
        gc_all = jnp.where(ahead == g * SPAN, gc_wide[g * width:(g + 1) * width], gc_all)
    tiles = tile_matrix(states)
    wide_s[0:states, 0:chunk] = mm(tiles, gb_all.astype(BF16))
    wide_s[states:2 * states, 0:chunk] = mm(tiles, gc_all.astype(BF16))
    drive = drive_s[...]
    gact_ref[...] = drive * dt + gy * skip_ref[...]
    gpre = ((drive * act + decay_s[...]) * sp_ref[...]).astype(BF16)
    rows_ref[0:1, :] += jnp.sum(gy * act, axis=0, keepdims=True)
    rows_ref[1:2, :] += jnp.sum(gpre.astype(F32), axis=0, keepdims=True)
    dwgrad_ref[...] += mm(low, gpre, TN)
    write_packed(part_ref, mm(gpre, dw_ref[...], NT), wide_s)


def scan_backward(me, pack, dt, sp, act, projected, gg, y, offset, hist, delta_w, rate, skip, held, whole, last, steps):
    tokens, channels = act.shape
    states = rate.shape[0]
    chunk = ROWS[0]
    row = lambda i, me: (last - i, 0)
    second = lambda i, me: (last - i, 1)
    run = lambda i, me: ((last - i) ^ me[0], 0, 0)
    fixed = lambda i, me: (0, 0)
    blocks = [pl.BlockSpec((chunk, channels), second), pl.BlockSpec((chunk, channels), row), pl.BlockSpec((1,) + pack.shape[1:], run)]
    shapes = [
        pltpu.HBM((tokens, 2 * channels), BF16),
        pltpu.HBM((tokens, channels), F32),
        jax.ShapeDtypeStruct(pack.shape, BF16),
    ]
    sums = [pl.BlockSpec(v.shape, fixed) for v in held]
    done = steps * chunk
    return pl.pallas_call(
        functools.partial(backward_kernel, len(whole)),
        name="scan_backward",
        grid_spec=pltpu.PrefetchScalarGridSpec(
            num_scalar_prefetch=1,
            grid=(steps,),
            in_specs=[
                pl.BlockSpec((1,) + pack.shape[1:], run),
                pl.BlockSpec((chunk, channels), row),
                pl.BlockSpec((chunk, channels), row),
                pl.BlockSpec((chunk, channels), row),
                pl.BlockSpec((chunk, channels), second),
                pl.BlockSpec((chunk, channels), row),
                pl.BlockSpec((chunk, channels), row),
                pl.BlockSpec((chunk, 1), row),
                pl.BlockSpec((chunk * states, channels), row),
                pl.BlockSpec((states, channels), lambda i, me: (jnp.maximum((last - i) * chunk - 1, 0), 0)),
                pl.BlockSpec(delta_w.shape, fixed),
                pl.BlockSpec(rate.shape, fixed),
                pl.BlockSpec(skip.shape, fixed),
            ] + sums + [pl.BlockSpec(memory_space=pl.ANY)] * len(whole),
            out_specs=blocks + sums,
            scratch_shapes=[pltpu.VMEM((chunk, channels), F32)] * 5
            + [pltpu.VMEM((2 * states, 2 * LANES), F32)]
            + [pltpu.VMEM((chunk * states, channels), BF16), pltpu.VMEM((chunk * states // 2, channels), BF16)],
        ),
        out_shape=shapes + [jax.ShapeDtypeStruct(v.shape, F32) for v in held],
        input_output_aliases={18 + i: i for i in range(len(whole))},
        compiler_params=pltpu.CompilerParams(dimension_semantics=("arbitrary",), vmem_limit_bytes=40 << 20),
        cost_estimate=SMALL,
    )(me, pack, in_hbm(dt), in_hbm(sp), in_hbm(act), in_hbm(projected), in_hbm(gg), in_hbm(y), offset, in_hbm(hist), in_hbm(hist), delta_w, rate, skip, *held, *(in_hbm(v) if k == 1 else v for k, v in enumerate(whole)))


def end_kernel(me_ref, pack_ref, gact_ref, act_ref, inner_ref, prior_ref, offset_ref, taps_ref, shift_ref, low_ref, bc_ref, grad_ref,
               ginner_ref, tapg_ref, selow_ref, selbc_ref, ext_s, after_s, wide_s):
    rows, channels = inner_ref.shape
    taps = taps_ref.shape[0]
    states = bc_ref.shape[0] // 2

    @pl.when(pl.program_id(0) == 0)
    def _():
        after_s[...] = jnp.zeros_like(after_s)
        tapg_ref[...] = jnp.zeros_like(tapg_ref)
        selow_ref[...] = jnp.zeros_like(selow_ref)
        selbc_ref[...] = jnp.zeros_like(selbc_ref)

    low, gbt, gct = read_packed(pack_ref, states)
    wide_s[0:states, :] = gbt
    wide_s[states:2 * states, :] = gct
    gbc = wide_s[:, 0:rows].astype(BF16)
    act = act_ref[...]
    selow_ref[...] += mm(act, low, TN)
    selbc_ref[...] += mm(gbc, act)
    gact = gact_ref[...] + mm(low, low_ref[...], NT) + mm(gbc, bc_ref[...], TN)
    before = prior_ref.shape[0]
    ext_s[0:before, :] = prior_ref[...].astype(F32)
    ext_s[before:before + rows, :] = inner_ref[...].astype(F32)
    offset = offset_ref[...]
    conv = shift_ref[...] + taps_ref[0:1, :] * ext_s[before:before + rows, :]
    for k in range(1, taps):
        conv += jnp.where(offset >= k, taps_ref[k:k + 1, :], 0.0) * ext_s[pl.ds(before - k, rows), :]
    q = sigmoid(conv)
    gconv = gact * q * (1.0 + conv * (1.0 - q))
    tapg_ref[taps:taps + 1, :] += jnp.sum(gconv, axis=0, keepdims=True)
    tapg_ref[0:1, :] += jnp.sum(gconv * ext_s[before:before + rows, :], axis=0, keepdims=True)
    ginner = gconv * taps_ref[0:1, :]
    for k in range(1, taps):
        masked = jnp.where(offset >= k, gconv, 0.0)
        tapg_ref[k:k + 1, :] += jnp.sum(masked * ext_s[pl.ds(before - k, rows), :], axis=0, keepdims=True)
        after_s[k - 1, rows:rows + 8, :] = after_s[k - 1, 0:8, :]
        after_s[k - 1, 0:rows, :] = masked * taps_ref[k:k + 1, :]
        ginner += after_s[k - 1, pl.ds(k, rows), :]
    ginner_ref[...] = ginner.astype(BF16)


def end(me, pack, gact, act, projected, offset, taps, shift, low_w, bc_w, grad_projected):
    tokens, channels = act.shape
    rows = ROWS[0]
    steps = tokens // rows
    row = lambda i, me: (steps - 1 - i, 0)
    fixed = lambda i, me: (0, 0)
    return pl.pallas_call(
        end_kernel,
        name="end",
        grid_spec=pltpu.PrefetchScalarGridSpec(
            num_scalar_prefetch=1,
            grid=(steps,),
            in_specs=[
                pl.BlockSpec((1,) + pack.shape[1:], lambda i, me: ((steps - 1 - i) ^ me[0], 0, 0)),
                pl.BlockSpec((rows, channels), row),
                pl.BlockSpec((rows, channels), row),
                pl.BlockSpec((rows, channels), row),
                pl.BlockSpec((16, channels), lambda i, me: (jnp.maximum((steps - 1 - i) * (rows // 16) - 1, 0), 0)),
                pl.BlockSpec((rows, 1), row),
                pl.BlockSpec(taps.shape, fixed),
                pl.BlockSpec(shift.shape, fixed),
                pl.BlockSpec(low_w.shape, fixed),
                pl.BlockSpec(bc_w.shape, fixed),
                pl.BlockSpec(memory_space=pl.ANY),
            ],
            out_specs=[
                pl.BlockSpec((rows, channels), row),
                pl.BlockSpec((8, channels), fixed),
                pl.BlockSpec(low_w.shape, fixed),
                pl.BlockSpec(bc_w.shape, fixed),
            ],
            scratch_shapes=[
                pltpu.VMEM((rows + 16, channels), F32),
                pltpu.VMEM((3, rows + 8, channels), F32),
                pltpu.VMEM((bc_w.shape[0], 2 * LANES), F32),
            ],
        ),
        out_shape=[
            pltpu.HBM(grad_projected.shape, BF16),
            jax.ShapeDtypeStruct((8, channels), F32),
            jax.ShapeDtypeStruct(low_w.shape, F32),
            jax.ShapeDtypeStruct(bc_w.shape, F32),
        ],
        input_output_aliases={11: 0},
        compiler_params=pltpu.CompilerParams(dimension_semantics=("arbitrary",), vmem_limit_bytes=14 << 20),
        cost_estimate=SMALL,
    )(me, pack, in_hbm(gact), in_hbm(act), in_hbm(projected), in_hbm(projected), offset, taps, shift, low_w, bc_w, in_hbm(grad_projected))


def weight_grad_kernel(count, turned, table_ref, *refs):
    a_refs, b_refs = refs[:count], refs[count:2 * count]
    out_ref, a_s, b_s = refs[-3:]
    rows = a_refs[0].shape[0]
    for s in range(count):
        a_s[s * rows:(s + 1) * rows, :] = a_refs[s][...]

    @pl.when(pl.program_id(0) == 0)
    def _():
        for s in range(count):
            b_s[s * rows:(s + 1) * rows, :] = b_refs[s][...]

    first, second = (b_s, a_s) if turned else (a_s, b_s)
    out_ref[0] = mm(first[...], second[...], TN).astype(BF16)


def weight_grad(table, distances, shards, b, column, channels, size, turned, slots=1, slot=0, into=()):
    rows, width = shards[0].shape
    block = width // size
    count = len(shards)
    shape = (1, channels, block) if turned else (1, block, channels)
    if distances is None:
        b_specs = [pl.BlockSpec((rows, channels), lambda i, table: (0, column))]
    else:
        b_specs = [pl.BlockSpec((rows, channels), lambda i, table, d=d: (table[d], column)) for d in distances]
    return pl.pallas_call(
        functools.partial(weight_grad_kernel, count, turned),
        name="weight_grad",
        grid_spec=pltpu.PrefetchScalarGridSpec(
            num_scalar_prefetch=1,
            grid=(size,),
            in_specs=[pl.BlockSpec((rows, block), lambda i, table: (0, i))] * count
            + b_specs + [pl.BlockSpec(memory_space=pl.ANY)] * len(into),
            out_specs=pl.BlockSpec(shape, lambda i, table: (i, slot, 0)),
            scratch_shapes=[pltpu.VMEM((rows * count, block), BF16), pltpu.VMEM((rows * count, channels), BF16)],
        ),
        out_shape=pltpu.HBM((size, slots * shape[1], shape[2]), BF16),
        input_output_aliases={1 + 2 * count + k: k for k in range(len(into))},
        compiler_params=pltpu.CompilerParams(dimension_semantics=("arbitrary",), vmem_limit_bytes=16 << 20),
        cost_estimate=SMALL,
    )(table, *(in_hbm(v) for v in shards), *([in_hbm(b)] * count), *(in_hbm(v) for v in into))


def weight_block(weight, dims, blocks):
    if dims[0][1] == (0,):
        columns = weight.shape[1] // blocks
        return pl.BlockSpec((weight.shape[0], columns), lambda i, *rest: (0, i)), columns
    columns = weight.shape[0] // blocks
    return pl.BlockSpec((columns, weight.shape[1]), lambda i, *rest: (i, 0)), columns


def placed_kernel(dims, count, table_ref, *refs):
    w_ref, out_ref = refs[count], refs[-1]
    for s in range(count):
        @pl.when(pl.program_id(1) == s)
        def _(s=s):
            out_ref[...] = mm(refs[s][...], w_ref[...], dims).astype(out_ref.dtype)


def pick_entry(values, i):
    chosen = values[0]
    for k in range(1, len(values)):
        chosen = jnp.where(i == k, values[k], chosen)
    return chosen


def placed_product(table, distances, shards, weight, dims, out):
    rows, width = shards[0].shape
    count, blocks = len(shards), 2
    spec, columns = weight_block(weight, dims, blocks)
    return pl.pallas_call(
        functools.partial(placed_kernel, dims, count),
        name="placed_product",
        grid_spec=pltpu.PrefetchScalarGridSpec(
            num_scalar_prefetch=1,
            grid=(blocks, count),
            in_specs=[pl.BlockSpec((rows, width), lambda i, k, table: (0, 0))] * count
            + [spec, pl.BlockSpec(memory_space=pl.ANY)],
            out_specs=pl.BlockSpec((rows, columns), lambda i, k, table: (pick_entry([table[d] for d in distances], k), i)),
        ),
        out_shape=pltpu.HBM(out.shape, out.dtype),
        input_output_aliases={count + 2: 0},
        compiler_params=pltpu.CompilerParams(dimension_semantics=("arbitrary", "arbitrary"), vmem_limit_bytes=16 << 20),
        cost_estimate=SMALL,
    )(table, *(in_hbm(v) for v in shards), in_hbm(weight), in_hbm(out))


def placed_halves_kernel(cuts, table_ref, first_ref, second_ref, *refs):
    w_refs, out_ref = refs[:cuts], refs[-1]
    depth = w_refs[0].shape[0]
    each = first_ref.shape[1] // depth
    total = None
    for c in range(cuts):
        ref, at = (first_ref, c) if c < each else (second_ref, c - each)
        term = mm(ref[:, at * depth:(at + 1) * depth], w_refs[c][...])
        total = term if total is None else total + term
    out_ref[...] = total.astype(out_ref.dtype)


def placed_halves(table, distance, first, second, weight, out):
    rows, middle = first.shape
    cuts = 8
    depth, width = weight.shape[0] // cuts, weight.shape[1]
    return pl.pallas_call(
        functools.partial(placed_halves_kernel, cuts),
        name="placed_halves",
        grid_spec=pltpu.PrefetchScalarGridSpec(
            num_scalar_prefetch=1,
            grid=(1,),
            in_specs=[pl.BlockSpec((rows, middle), lambda i, table: (0, 0))] * 2
            + [pl.BlockSpec((depth, width), lambda i, table, c=c: (c, 0)) for c in range(cuts)]
            + [pl.BlockSpec(memory_space=pl.ANY)],
            out_specs=pl.BlockSpec((rows, width), lambda i, table: (table[distance], 0)),
        ),
        out_shape=pltpu.HBM(out.shape, out.dtype),
        input_output_aliases={3 + cuts: 0},
        compiler_params=pltpu.CompilerParams(dimension_semantics=("arbitrary",), vmem_limit_bytes=16 << 20),
        cost_estimate=SMALL,
    )(table, in_hbm(first), in_hbm(second), *([in_hbm(weight)] * cuts), in_hbm(out))


def in_hbm(value):
    return pltpu.with_memory_space_constraint(value, pltpu.HBM)


def far_kernel(cuts, table_ref, g_ref, t_ref, *refs):
    w_refs, (ahead_ref, behind_ref) = refs[:cuts], refs[cuts:]
    columns = w_refs[0].shape[0]
    for ref, first in ((ahead_ref, True), (behind_ref, False)):
        @pl.when((pl.program_id(0) == 0) == first)
        def _(ref=ref):
            for c in range(cuts):
                at = slice(c * columns, (c + 1) * columns)
                ref[:, at] = (mm(g_ref[...], w_refs[c][...], NT) + t_ref[:, at].astype(F32)).astype(BF16)


def pair_kernel(cuts, table_ref, ga_ref, gb_ref, ta_ref, tb_ref, *refs, halves=False):
    w_refs, (ra_ref, rb_ref, ahead_ref, behind_ref) = refs[:cuts], refs[cuts:]
    rows, columns = ga_ref.shape[0], w_refs[0].shape[0]
    both = jnp.concatenate([ga_ref[...], gb_ref[...]], axis=0)
    low = pl.program_id(0) == 0
    for c in range(cuts):
        at = slice(c * columns, (c + 1) * columns)
        total = mm(both, w_refs[c][...], NT)
        ra, rb = ra_ref[:, at].astype(F32), rb_ref[:, at].astype(F32)
        if halves:
            ra, rb = jnp.where(low, ra, 0.0), jnp.where(low, 0.0, rb)
        ahead_ref[:, at] = (total[:rows] + ta_ref[:, at].astype(F32) + ra).astype(BF16)
        behind_ref[:, at] = (total[rows:] + tb_ref[:, at].astype(F32) + rb).astype(BF16)


def own_kernel(cuts, table_ref, g_ref, t_ref, *refs):
    w_refs, (ra_ref, rb_ref, place_ref), outs = refs[:cuts], refs[cuts:cuts + 3], refs[cuts + 3:]
    columns = w_refs[0].shape[0]
    pair = outs[0].shape[0]
    for c in range(cuts):
        at = slice(c * columns, (c + 1) * columns)
        total = mm(g_ref[...], w_refs[c][...], NT) + t_ref[:, at].astype(F32)
        total = (total + ra_ref[:, at].astype(F32) + rb_ref[:, at].astype(F32)).astype(BF16)
        for d, out_ref in enumerate(outs):
            out_ref[:, at] = mm(place_ref[d * pair:(d + 1) * pair, :], total).astype(BF16)


def ring_step(kernel, table, distances, grads, terms, weight, arrived=(), place=None, pieces=1):
    rows, cuts = ROWS[0], 4
    width, channels = weight.shape[0], weight.shape[1] // 2
    half, columns = width // 2, width // (2 * cuts)
    fixed = lambda i, table: (0, 0)
    side = lambda i, table: (0, i)
    far = not arrived
    if far:
        outs, shape = [fixed, fixed], (rows, half)
    else:
        outs, shape = [side, side] if place is None else [side] * pieces, (rows // pieces, width)
    small = not far and arrived[0].shape[1] == half
    extra = [] if place is None else [place]
    return pl.pallas_call(
        functools.partial(kernel, cuts, halves=True) if small else functools.partial(kernel, cuts),
        name=kernel.__name__,
        grid_spec=pltpu.PrefetchScalarGridSpec(
            num_scalar_prefetch=1,
            grid=(2,),
            in_specs=[pl.BlockSpec((rows, channels), lambda i, table, d=d: (table[d], 0)) for d in distances]
            + [pl.BlockSpec((rows, half), lambda i, table, d=d: (table[d], i)) for d in distances]
            + [pl.BlockSpec((columns, channels), lambda i, table, c=c: (i * cuts + c, 0)) for c in range(cuts)]
            + [pl.BlockSpec((rows, half), fixed if small else side) for v in arrived]
            + [pl.BlockSpec(v.shape, fixed) for v in extra],
            out_specs=[pl.BlockSpec((shape[0], half), m) for m in outs],
        ),
        out_shape=[pltpu.HBM(shape, BF16) for m in outs],
        compiler_params=pltpu.CompilerParams(dimension_semantics=("arbitrary",), vmem_limit_bytes=24 << 20),
        cost_estimate=SMALL,
    )(table, *([in_hbm(grads)] * len(distances)), *([in_hbm(terms)] * len(distances)), *([in_hbm(weight)] * cuts),
      *(in_hbm(v) for v in arrived), *extra)


def blank(*shapes):
    hbm = pl.BlockSpec(memory_space=pl.ANY)
    return pl.pallas_call(
        lambda *refs: None, name="blank", out_specs=[hbm] * len(shapes),
        out_shape=[pltpu.HBM(*v) for v in shapes],
        cost_estimate=SMALL)()


def deal_kernel(x_ref, cot_ref, order_ref, gain_ref, me_ref, pick_ref, place_ref, *sends):
    rows = x_ref.shape[0]
    dp_size = order_ref.shape[0]
    me = me_ref[0]
    group_tokens = me_ref[1]
    pair = rows // dp_size
    order = order_ref[...].astype(jnp.int32)
    near = lax.broadcasted_iota(jnp.int32, (dp_size, rows), 0)
    other = near ^ me
    source = order // group_tokens
    local = order % rows
    before = (
        lax.broadcasted_iota(jnp.int32, (rows, rows), 0) < lax.broadcasted_iota(jnp.int32, (rows, rows), 1)
    ).astype(BF16)
    slots = lax.broadcasted_iota(jnp.int32, (rows, rows), 0)
    chosen = source == me
    rank = mm(chosen.astype(BF16), before).astype(jnp.int32)
    slot = jnp.where(chosen, near * pair + rank, -1)
    pick = jnp.zeros((rows, rows), F32)
    for d in range(dp_size):
        pick += mm((slots == slot[d:d + 1, :]).astype(BF16), (slots == local[d:d + 1, :]).astype(BF16), NT)
    pick = pick.astype(BF16)
    pick_ref[...] = pick
    mine = source[0:1, :]
    held = (mine == other).astype(BF16)
    ranks = mm(held, before).astype(jnp.int32)
    arrived = jnp.sum(jnp.where(mine == other, near * pair + ranks, 0), axis=0, keepdims=True)
    place_ref[...] = (slots == arrived).astype(BF16)
    x = x_ref[...].astype(F32)
    rinv = lax.rsqrt(jnp.mean(x * x, axis=1, keepdims=True) + EPSILON)
    normed = (x * rinv * gain_ref[...]).astype(BF16)
    for d in range(dp_size):
        at = slice(d * pair, (d + 1) * pair)
        sends[d][...] = mm(pick[at], normed).astype(BF16)
        sends[dp_size + d][...] = mm(pick[at], cot_ref[...]).astype(BF16)


def deal(x, cot, order, gain, me):
    rows, width = x.shape
    dp_size = order.shape[0]
    vm = pl.BlockSpec(memory_space=pltpu.VMEM)
    pick, place, *sends = pl.pallas_call(
        deal_kernel,
        name="deal",
        in_specs=[vm, vm, vm, vm, pl.BlockSpec(memory_space=pltpu.SMEM)],
        out_specs=[vm] * (2 + 2 * dp_size),
        out_shape=[jax.ShapeDtypeStruct((rows, rows), BF16)] * 2
        + [jax.ShapeDtypeStruct((rows // dp_size, width), BF16)] * (2 * dp_size),
        compiler_params=pltpu.CompilerParams(vmem_limit_bytes=32 << 20),
        cost_estimate=SMALL,
    )(x, cot, order, gain, me)
    return sends[:dp_size], sends[dp_size:], pick, place


def round_dot(a, b, dims=(((1,), (0,)), ((), ()))):
    return mm(a, b, dims).astype(BF16)


def after(value, *earlier):
    return lax.optimization_barrier((value,) + earlier)[0]


def flip(value, axis, bit):
    return lax.ppermute(value, axis, [(i, i ^ bit) for i in range(lax.axis_size(axis))])


def exchange(pieces, axis, stack=True):
    pieces = [pieces[0]] + [flip(pieces[d], axis, d) for d in range(1, lax.axis_size(axis))]
    return jnp.stack(pieces) if stack else pieces


def swap(values, axis):
    return lax.all_to_all(values, axis, split_axis=0, concat_axis=0, tiled=True)


def share(value, axis):
    return exchange([value] * lax.axis_size(axis), axis)


def in_order(pieces, axis):
    size, me, bit = lax.axis_size(axis), lax.axis_index(axis), 1
    while bit < size:
        split = pieces.reshape((size // (2 * bit), 2, bit) + pieces.shape[1:])
        turned = jnp.concatenate([split[:, 1:], split[:, :1]], axis=1)
        pieces = jnp.where((me // bit) % 2 == 1, turned, split).reshape(pieces.shape)
        bit *= 2
    return pieces


def cube_sum(value, axis, bit, end_bit):
    while bit < end_bit:
        value = value + flip(value, axis, bit)
        bit *= 2
    return value


class Bag(dict):
    def meet(self, values, *names):
        values, held = lax.optimization_barrier((values, {n: self[n] for n in names}))
        self.update(held)
        return values


def add_up(pieces):
    return jnp.sum(pieces.astype(F32), axis=0)


class Ring:
    def __init__(self, axis):
        self.axis = axis
        self.size = size = lax.axis_size(axis)
        columns = max(c for c in range(1, size) if size % c == 0 and c * c <= size)
        rows = size // columns
        cycle = [(0, c) for c in range(columns)]
        for r in range(1, rows):
            snake = range(1, columns)
            cycle += [(r, c) for c in (snake if r % 2 == 0 else reversed(snake))]
        cycle += [(r, 0) for r in reversed(range(1, rows))]
        order = [r * columns + c for r, c in cycle]
        place = {t: i for i, t in enumerate(order)}
        table = jnp.array([[order[(place[t] + d) % size] for d in range(size)] for t in range(size)], jnp.int32)
        self.at = lax.dynamic_index_in_dim(table, lax.axis_index(axis), 0, keepdims=False)
        self.forward = [(order[i], order[(i + 1) % size]) for i in range(size)]
        self.backward = [(b, a) for a, b in self.forward]

    def hop(self, value, ahead):
        return lax.ppermute(value, self.axis, self.forward if ahead else self.backward)


def ring_gather(ring, own, between):
    half, size = ring.size // 2, ring.size
    middle = own.shape[1] // 2
    distances, shards = [0], [own]
    ahead = behind = own
    for d in range(1, half):
        ahead, behind = between(d, ring.hop(ahead, True), ring.hop(behind, False))
        distances += [size - d, d]
        shards += [ahead, behind]
    halves = between(half, ring.hop(ahead[:, :middle], True), ring.hop(behind[:, middle:], False))
    return distances + [half], shards, halves


def ring_reduce(ring, grads, terms, weight, place, pieces, between):
    half, size = ring.size // 2, ring.size
    step = functools.partial(ring_step, table=ring.at, grads=grads, terms=terms, weight=weight)
    ahead, behind = step(far_kernel, distances=[half])
    for d in range(half, 0, -1):
        ahead, behind = between(half - d, ahead, ring.hop(ahead, True), ring.hop(behind, False))
        if d > 1:
            ahead, behind = step(pair_kernel, distances=[d - 1, size + 1 - d], arrived=[ahead, behind])
    return step(own_kernel, distances=[0], arrived=[ahead, behind], place=place, pieces=pieces)


def shards(
    block_input, norm_gain, in_weight, conv_weight, conv_bias, select_weight, delta_weight, delta_bias,
    decay_log, skip_weight, out_weight, out_cotangent, seq_lengths, deal_order,
):
    rows_dev, width = block_input.shape
    dp_size = lax.axis_size("dp")
    tensor_size = lax.axis_size("tensor")
    pair = rows_dev // dp_size
    group_tokens = rows_dev * tensor_size
    ring = Ring("tensor")
    here = jnp.zeros((1,), jnp.int32)
    me = jnp.stack([lax.axis_index("dp"), jnp.int32(group_tokens)]).astype(jnp.int32)
    head = share(jnp.concatenate([deal_order.astype(F32), norm_gain.astype(F32)]), "dp")
    gain_values = in_order(head[:, rows_dev:], "dp").reshape(1, -1)
    send_rows, send_cot, pick, place = deal(block_input, out_cotangent, head[:, :rows_dev], gain_values, me)
    in_cat = jnp.swapaxes(after(in_weight, send_rows[0]), 0, 1).reshape(in_weight.shape[1], -1)
    recv_rows = exchange(send_rows, "dp")
    recv_rows, in_cat = lax.optimization_barrier((recv_rows, in_cat))
    in_full = lax.all_gather(in_cat, "dp", axis=0, tiled=True)
    normed = round_dot(place, recv_rows.reshape(rows_dev, -1), TN)
    channels = in_full.shape[1] // 2
    taps = conv_weight.shape[0]
    lane_width = conv_bias.shape[1] * dp_size
    own_states = decay_log.shape[1]
    states, low_rank = own_states * dp_size, delta_weight.shape[0] * dp_size
    lengths_row = seq_lengths[0]
    seq_ends = jnp.cumsum(lengths_row)
    begins = seq_ends - lengths_row
    positions = jnp.arange(group_tokens, dtype=jnp.int32)
    inside = (positions[:, None] >= begins[None, :]) & (positions[:, None] < seq_ends[None, :])
    offset = (positions - jnp.sum(jnp.where(inside, begins[None, :], 0), axis=1))[:, None]
    (projected,) = blank(((group_tokens, 2 * channels), BF16))
    half = tensor_size // 2
    NN = (((1,), (0,)), ((), ()))
    lanes_own = jnp.concatenate([conv_weight, jnp.stack([conv_bias, delta_bias, skip_weight])])
    bag = Bag(
        cot=send_cot, select=jnp.concatenate([select_weight, jnp.moveaxis(lanes_own, 0, 2)], axis=2),
        thin=jnp.concatenate([decay_log.T, delta_weight]), projected=projected)
    waiting = {"shards": [normed], "distances": [0]}

    def during_normed(d, ahead, behind):
        if d == 1:
            ahead, behind = bag.meet((ahead, behind), "select")
            bag["select"] = share(bag["select"], "dp")
            bag["own"] = out_weight
        elif d < half - 1:
            ahead, behind = bag.meet((ahead, behind), "own", "select", "cot")
            if d == 2:
                bag["cot"] = exchange(bag["cot"], "dp")
        elif d >= half - 1:
            bag["projected"] = placed_product(
                ring.at, waiting["distances"], waiting["shards"], in_full, NN, bag["projected"])
            waiting["shards"], waiting["distances"] = [], []
            ahead, behind = bag.meet((ahead, behind), "projected", *(["cot"] if d == half else []))
        if d < half:
            waiting["distances"] += [tensor_size - d, d]
            waiting["shards"] += [ahead, behind]
        return ahead, behind

    distances, normed_shards, halves = ring_gather(ring, normed, during_normed)

    def rows_of(values, distance):
        return lax.dynamic_slice(values, (ring.at[distance] * rows_dev, 0), (rows_dev, values.shape[1]))

    projected = placed_halves(ring.at, distances[-1], *halves, in_full, bag["projected"])
    dealt_cot = round_dot(place, bag["cot"].reshape(rows_dev, -1), TN)
    select_matrix = jnp.moveaxis(in_order(bag["select"], "dp"), 0, 1).reshape(channels, -1)
    low_w, bc_w = select_matrix[:, :low_rank], select_matrix[:, low_rank:low_rank + 2 * states].T
    lanes_float = select_matrix[:, low_rank + 2 * states:].astype(F32).T
    conv_taps = lanes_float[:taps]
    conv_shift, delta_shift, skip_values = (lanes_float[taps + i:taps + i + 1] for i in range(3))
    activated, part = front(here, projected, offset, conv_taps, conv_shift, low_w, bc_w)
    out_full = lax.all_gather(bag["own"], "dp", axis=1, tiled=True)
    group_cot = lax.all_gather(after(dealt_cot, halves[0]), "tensor", axis=0, tiled=True)
    bag["thin"] = lax.all_gather(after(bag["thin"], part)[None], "dp", axis=0, tiled=True)
    bag["last"] = jnp.concatenate([after(v, part) for v in halves], axis=1)
    arrived = bag.meet(swap(part, "tensor"), "thin", "last")
    normed_shards = normed_shards + [bag["last"]]
    decay_full = bag["thin"][:, :own_states].reshape(states, channels)
    delta_full = bag["thin"][:, own_states:].reshape(low_rank, channels)
    decay_rate = -jnp.exp(decay_full.astype(F32))
    total = jnp.sum(arrived.astype(F32), axis=0).astype(BF16)
    pack_all = swap(jnp.broadcast_to(total[None], part.shape), "tensor")
    step_size, slope, y, gated, hist, unused_state = scan_forward(
        here, pack_all, activated, projected, offset, delta_full, delta_shift, decay_rate, skip_values,
        jnp.zeros((states, channels), F32), [], 0, tensor_size)
    gg = mm(group_cot, out_full, NT)
    held = [
        jnp.zeros((states, channels), F32),
        jnp.zeros((states, channels), F32),
        jnp.zeros((low_rank, channels), F32),
        jnp.zeros((8, channels), F32),
    ]
    mixed = lax.psum_scatter(round_dot(gated, out_full), "tensor", scatter_dimension=0, tiled=True)
    grad_projected, grad_act, grad_part, unused_carry, rate_grad, delta_weight_grad, row_grads = scan_backward(
        here, pack_all, step_size, slope, activated, projected, gg, y, offset, hist, delta_full, decay_rate, skip_values,
        held, [], tensor_size - 1, tensor_size)
    decay_grad = rate_grad * decay_rate
    def by_lane(values):
        lanes = values.reshape(-1, channels // lane_width, dp_size, lane_width // dp_size)
        return jnp.moveaxis(lanes, 2, 0).reshape(dp_size, -1)

    def pack_scan(row_grads, decay_grad, delta_weight_grad):
        parts = [by_lane(row_grads[:2]), decay_grad.reshape(dp_size, -1), delta_weight_grad.reshape(dp_size, -1)]
        return jnp.concatenate(parts, axis=1).astype(BF16), [part.shape[1] for part in parts]

    def pack_conv(packed, taps_sum, low_sum, bc_sum):
        select_grad = jnp.concatenate([low_sum, bc_sum.T], axis=1)
        parts = [
            packed,
            by_lane(taps_sum[:taps + 1]).astype(BF16),
            jnp.moveaxis(select_grad.reshape(channels // lane_width, dp_size, -1), 1, 0).reshape(dp_size, -1).astype(BF16),
        ]
        flat = jnp.concatenate(parts, axis=1)
        flat = jnp.pad(flat, ((0, 0), (0, -flat.shape[1] % 2048))).reshape(dp_size, -1, LANES)
        return flat, [part.shape[1] for part in parts[1:]]

    merged = channels == width // dp_size
    bag["out"] = weight_grad(
        ring.at, None, [group_cot], after(gated, grad_part), 0, channels, dp_size, True, 2 if merged else 1)
    arrived = bag.meet(swap(grad_part, "tensor"), "out")
    grad_total = jnp.sum(arrived.astype(F32), axis=0).astype(BF16)
    bag["gate"] = weight_grad(
        ring.at, distances, normed_shards, after(grad_projected, grad_total), 1, channels, dp_size, False,
        *((2, 1, [bag["out"]]) if merged else ()))
    bag["packed"], sizes = pack_scan(*(after(v, grad_total) for v in (row_grads, decay_grad, delta_weight_grad)))
    bag["terms"] = round_dot(after(grad_projected, grad_total)[:, channels:], in_full[:, channels:], NT)
    grad_pack = bag.meet(swap(jnp.broadcast_to(grad_total[None], grad_part.shape), "tensor"), "gate", "terms", "packed")
    gate_terms = bag["terms"]
    bag["gate"] = lax.psum_scatter(bag["gate"], "dp", scatter_dimension=0, tiled=True)
    if not merged:
        bag["out"] = lax.psum_scatter(bag["out"], "dp", scatter_dimension=0, tiled=True)
    grad_projected, *sums = end(
        here, grad_pack, grad_act, activated, projected, offset, conv_taps, conv_shift, low_w, bc_w, grad_projected)
    bag["sums"] = [bag["packed"], *sums]
    bag["mixed"] = mixed

    def during_grad(k, sent, ahead, behind):
        names = []
        if k == 0:
            bag["grads"] = grad_projected
            names = ["mixed", "sums", "grads"]
        if k == 1:
            bag["inner"] = weight_grad(
                ring.at, distances, normed_shards, after(bag["grads"], sent), 0, channels, dp_size, False)
            names = ["mixed", "sums", "inner"]
        if k == half - 2:
            flat, more = pack_conv(*after(tuple(bag["sums"]), sent))
            sizes.extend(more)
            bag["flat"] = swap(flat, "dp")
            names = ["mixed", "flat", "gate"] + ([] if merged else ["out"])
        ahead, behind = bag.meet((ahead, behind), *names)
        if k == half - 2:
            bag["mixed"] = exchange(round_dot(place, bag["mixed"]).reshape(dp_size, pair, -1), "dp")
        if k == 1:
            bag["inner"] = lax.psum_scatter(bag["inner"], "dp", scatter_dimension=0, tiled=True)
        return ahead, behind

    send_grad = ring_reduce(ring, grad_projected, gate_terms, in_full, place, dp_size, during_grad)
    home_grad = exchange(send_grad, "dp").reshape(rows_dev, -1)
    home_out = bag["mixed"].reshape(rows_dev, -1)
    out_grad = (bag["gate"][0, :channels] if merged else bag["out"][0]).astype(F32)
    gate_grad = bag["gate"][:, channels:] if merged else bag["gate"]
    inner_grad = after(bag["inner"], send_grad[0])
    bag["in"] = jnp.concatenate([inner_grad, gate_grad]).astype(F32)
    gain_part = jnp.sum(in_weight.astype(F32) * bag["in"], axis=(0, 2))
    in_weight_grad = bag["in"]
    gain_parts = swap(jnp.broadcast_to(gain_part.reshape(1, -1, LANES), (tensor_size, gain_part.size // LANES, LANES)), "tensor")
    gain_grad = add_up(gain_parts).reshape(-1) / norm_gain.astype(F32)
    flat = jnp.sum(bag["flat"].astype(F32), axis=0).reshape(-1)
    small, start = [], 0
    for size in sizes:
        small.append(flat[start:start + size])
        start += size
    scan_grads = small[0].reshape((2,) + conv_bias.shape)
    lane_grads = small[3].reshape((taps + 1,) + conv_bias.shape)
    rows_float = block_input.astype(F32)
    block_output = (rows_float + mm(pick, home_out, TN)).astype(BF16)
    inverse_rms = lax.rsqrt(jnp.mean(rows_float * rows_float, axis=1, keepdims=True) + EPSILON)
    unit_rows = rows_float * inverse_rms
    scaled = mm(pick, home_grad, TN) * gain_values
    input_grad = (
        out_cotangent.astype(F32)
        + inverse_rms * (scaled - unit_rows * jnp.mean(scaled * unit_rows, axis=1, keepdims=True))
    ).astype(BF16)
    return (
        block_output,
        input_grad,
        gain_grad,
        in_weight_grad,
        lane_grads[:taps],
        lane_grads[taps],
        small[4].reshape(select_weight.shape),
        small[2].reshape(delta_weight.shape),
        scan_grads[1],
        small[1].reshape(decay_log.shape[1], decay_log.shape[0]).T,
        scan_grads[0],
        out_grad,
    )


def solution(mesh):
    return jax.shard_map(
        shards,
        mesh=mesh,
        in_specs=(
            P(("dp", "tensor"), None),
            P("dp"),
            P(None, "dp", "tensor"),
            P(None, "tensor", "dp"),
            P("tensor", "dp"),
            P("tensor", "dp", None),
            P("dp", "tensor"),
            P("tensor", "dp"),
            P("tensor", "dp"),
            P("tensor", "dp"),
            P("tensor", "dp"),
            P(("dp", "tensor"), None),
            P("dp", None),
            P(("dp", "tensor")),
        ),
        out_specs=(
            P(("dp", "tensor"), None),
            P(("dp", "tensor"), None),
            P("dp"),
            P(None, "dp", "tensor"),
            P(None, "tensor", "dp"),
            P("tensor", "dp"),
            P("tensor", "dp", None),
            P("dp", "tensor"),
            P("tensor", "dp"),
            P("tensor", "dp"),
            P("tensor", "dp"),
            P("tensor", "dp"),
        ),
        check_vma=False,
    )
```

```python
import functools

import jax
import jax.numpy as jnp
from jax import lax
from jax.experimental import pallas as pl
from jax.experimental.pallas import tpu as pltpu
from jax.sharding import PartitionSpec as P

EPSILON = 1e-05
FAR = 1e30
LANES = 128
STEP = 96
SPAN = 16
SMALL = pl.CostEstimate(flops=1, transcendentals=0, bytes_accessed=1)
NT = (((1,), (1,)), ((), ()))
TN = (((0,), (0,)), ((), ()))
F32 = jnp.float32
BF16 = jnp.bfloat16


def softplus(v):
    return jnp.maximum(v, 0.0) + jnp.log1p(jnp.exp(-jnp.abs(v)))


def sigmoid(v):
    return 1.0 / (1.0 + jnp.exp(-v))


def mm(a, b, dims=(((1,), (0,)), ((), ()))):
    return lax.dot_general(a, b, dims, preferred_element_type=F32)


def column_at(states, tokens):
    return lax.broadcasted_iota(jnp.int32, (states, tokens), 1)


def write_packed(out_ref, low, wide_ref):
    rows, rank = low.shape
    states = wide_ref.shape[0] // 2
    rest = rows - LANES
    out_ref[0, 0:rows, :] = low.astype(out_ref.dtype)
    out_ref[0, rows:rows + 2 * states, :] = wide_ref[:, 0:LANES].astype(out_ref.dtype)
    tail = wide_ref[:, LANES:2 * LANES]
    lane = lax.broadcasted_iota(jnp.int32, (states, LANES), 1)
    both = jnp.where(lane < rest, tail[:states], pltpu.roll(tail[states:], rest, 1))
    out_ref[0, rows + 2 * states:rows + 3 * states, :] = both.astype(out_ref.dtype)


def read_packed(in_ref, states):
    rows = in_ref.shape[1] - 3 * states
    rest = rows - LANES
    low = in_ref[0, 0:rows, :]
    head = in_ref[0, rows:rows + 2 * states, :].astype(F32)
    both = in_ref[0, rows + 2 * states:rows + 3 * states, :].astype(F32)
    first = jnp.concatenate([head[:states], both], axis=1)
    second = jnp.concatenate([head[states:], pltpu.roll(both, LANES - rest, 1)], axis=1)
    return low, first, second


def front_kernel(me_ref, inner_ref, offset_ref, taps_ref, shift_ref, low_ref, bc_ref, act_ref, part_ref, ext_s, wide_s):
    rows = inner_ref.shape[0]
    taps = taps_ref.shape[0]

    @pl.when(pl.program_id(0) == 0)
    def _():
        ext_s[0:8, :] = jnp.zeros((8, ext_s.shape[1]), F32)

    ext_s[8:8 + rows, :] = inner_ref[...].astype(F32)
    offset = offset_ref[...]
    conv = shift_ref[...] + taps_ref[0:1, :] * ext_s[8:8 + rows, :]
    for k in range(1, taps):
        conv += jnp.where(offset >= k, taps_ref[k:k + 1, :], 0.0) * ext_s[pl.ds(8 - k, rows), :]
    act = (conv * sigmoid(conv)).astype(BF16)
    act_ref[...] = act
    ext_s[0:8, :] = ext_s[rows:rows + 8, :]
    wide_s[:, 0:rows] = mm(bc_ref[...], act, NT)
    write_packed(part_ref, mm(act, low_ref[...]), wide_s)


def front(me, projected, offset, taps, shift, low_w, bc_w):
    tokens, channels = projected.shape[0], taps.shape[1]
    runs, rows = tokens // ROWS[0], ROWS[0]
    packed = rows + 3 * bc_w.shape[0] // 2
    row = lambda i, me: (i, 0)
    fixed = lambda i, me: (0, 0)
    return pl.pallas_call(
        front_kernel,
        name="front",
        grid_spec=pltpu.PrefetchScalarGridSpec(
            num_scalar_prefetch=1,
            grid=(runs,),
            in_specs=[
                pl.BlockSpec((rows, channels), row),
                pl.BlockSpec((rows, 1), row),
                pl.BlockSpec(taps.shape, fixed),
                pl.BlockSpec(shift.shape, fixed),
                pl.BlockSpec(low_w.shape, fixed),
                pl.BlockSpec(bc_w.shape, fixed),
            ],
            out_specs=[pl.BlockSpec((rows, channels), row), pl.BlockSpec((1, packed, LANES), lambda i, me: (i ^ me[0], 0, 0))],
            scratch_shapes=[pltpu.VMEM((rows + 8, channels), F32), pltpu.VMEM((bc_w.shape[0], 2 * LANES), F32)],
        ),
        out_shape=[
            pltpu.HBM((tokens, channels), BF16),
            jax.ShapeDtypeStruct((runs, packed, LANES), BF16),
        ],
        compiler_params=pltpu.CompilerParams(dimension_semantics=("arbitrary",), vmem_limit_bytes=8 << 20),
        cost_estimate=SMALL,
    )(me, in_hbm(projected), offset, taps, shift, low_w, bc_w)


ROWS = [192]


def spread_mask(rows, states):
    width = SPAN * states
    row = lax.broadcasted_iota(jnp.int32, (rows, width), 0) % SPAN
    return row == lax.broadcasted_iota(jnp.int32, (rows, width), 1) // states


def tile_matrix(states):
    width = SPAN * states
    row = lax.broadcasted_iota(jnp.int32, (states, width), 0)
    return (row == lax.broadcasted_iota(jnp.int32, (states, width), 1) % states).astype(BF16)


def spread_columns(columns, rows, states):
    tiled = mm(columns[:, 0:rows].astype(BF16), tile_matrix(states), TN)
    return jnp.where(spread_mask(rows, states), tiled, 0.0).astype(BF16)


def forward_kernel(kept, me_ref, pack_ref, act_ref, gate_ref, offset_ref, dw_ref, bias_ref, rate_ref, skip_ref, h_in, *rest):
    dt_ref, sp_ref, y_ref, gated_ref, hist_ref, h_s, dtm_s, u_s = rest[kept:]
    states, channels = rate_ref.shape
    chunk = act_ref.shape[0]

    @pl.when(pl.program_id(0) == 0)
    def _():
        h_s[...] = h_in[...]

    low, bt, ct = read_packed(pack_ref, states)
    wide = bt.shape[1]
    pre = mm(low, dw_ref[...]) + bias_ref[...]
    small = jnp.exp(-jnp.abs(pre))
    dt = jnp.maximum(pre, 0.0) + jnp.log1p(small)
    dt_ref[...] = dt
    sp_ref[...] = jnp.where(pre >= 0.0, 1.0, small) / (1.0 + small)
    act = act_ref[...].astype(F32)
    u_s[...] = dt * act
    dtm_s[...] = jnp.where(offset_ref[...] == 0, FAR, dt)
    rate = rate_ref[...]

    def group(g, h):
        base = pl.multiple_of(g * STEP, STEP)
        bg = pltpu.roll(bt, wide - base, 1)
        dtm = dtm_s[pl.ds(base, STEP), :]
        u = u_s[pl.ds(base, STEP), :]
        for j in range(STEP):
            a = jnp.exp(dtm[j:j + 1, :] * rate)
            h = a * h + u[j:j + 1, :] * bg[:, j:j + 1]
            at = pl.multiple_of((base + j) * states, states)
            hist_ref[pl.ds(at, states), :] = h.astype(BF16)
        return h

    h_s[...] = lax.fori_loop(0, chunk // STEP, group, h_s[...])
    spread = spread_columns(ct, chunk, states)
    width = SPAN * states
    for g in range(chunk // SPAN):
        rows = slice(g * SPAN, (g + 1) * SPAN)
        y_ref[rows, :] = mm(spread[rows, :], hist_ref[g * width:(g + 1) * width, :])
    y = y_ref[...] + skip_ref[...] * act
    y_ref[...] = y
    gate = gate_ref[...].astype(F32)
    gated_ref[...] = (y * gate * sigmoid(gate)).astype(BF16)


def scan_forward(me, pack, act, projected, offset, delta_w, bias, rate, skip, held, whole, first, steps):
    tokens, channels = act.shape
    states = rate.shape[0]
    chunk = ROWS[0]
    row = lambda i, me: (first + i, 0)
    fixed = lambda i, me: (0, 0)
    done = steps * chunk
    return pl.pallas_call(
        functools.partial(forward_kernel, len(whole)),
        name="scan_forward",
        grid_spec=pltpu.PrefetchScalarGridSpec(
            num_scalar_prefetch=1,
            grid=(steps,),
            in_specs=[
                pl.BlockSpec((1,) + pack.shape[1:], lambda i, me: ((first + i) ^ me[0], 0, 0)),
                pl.BlockSpec((chunk, channels), row),
                pl.BlockSpec((chunk, channels), lambda i, me: (first + i, 1)),
                pl.BlockSpec((chunk, 1), row),
                pl.BlockSpec(delta_w.shape, fixed),
                pl.BlockSpec(bias.shape, fixed),
                pl.BlockSpec(rate.shape, fixed),
                pl.BlockSpec(skip.shape, fixed),
                pl.BlockSpec(rate.shape, fixed),
            ] + [pl.BlockSpec(memory_space=pl.ANY)] * len(whole),
            out_specs=[
                pl.BlockSpec((chunk, channels), row),
                pl.BlockSpec((chunk, channels), row),
                pl.BlockSpec((chunk, channels), row),
                pl.BlockSpec((chunk, channels), row),
                pl.BlockSpec((chunk * states, channels), row),
                pl.BlockSpec(rate.shape, fixed),
            ],
            scratch_shapes=[
                pltpu.VMEM((chunk, channels), F32),
                pltpu.VMEM((chunk, channels), F32),
            ],
        ),
        out_shape=[
            pltpu.HBM((tokens, channels), F32),
            pltpu.HBM((tokens, channels), F32),
            pltpu.HBM((tokens, channels), F32),
            pltpu.HBM((tokens, channels), BF16),
            pltpu.HBM((tokens * states, channels), BF16),
            jax.ShapeDtypeStruct(rate.shape, F32),
        ],
        input_output_aliases={10 + i: i for i in range(len(whole))},
        compiler_params=pltpu.CompilerParams(dimension_semantics=("arbitrary",), vmem_limit_bytes=16 << 20),
        cost_estimate=SMALL,
    )(me, pack, in_hbm(act), in_hbm(projected), offset, delta_w, bias, rate, skip, held, *(in_hbm(v) for v in whole))


def backward_kernel(kept, me_ref, pack_ref, dt_ref, sp_ref, act_ref, gate_ref, gg_ref, y_ref, offset_ref,
                    hist_ref, prior_ref, dw_ref, rate_ref, skip_ref, carry_in, rgrad_in, dwgrad_in, rows_in, *rest):
    (ggate_ref, gact_ref, part_ref, carry_s, rgrad_ref, dwgrad_ref, rows_ref,
     dtm_s, u_s, gy_s, drive_s, decay_s, wide_s, adj_s, thr_s) = rest[kept:]
    states, channels = rate_ref.shape
    chunk = act_ref.shape[0]

    @pl.when(pl.program_id(0) == 0)
    def _():
        carry_s[...] = carry_in[...]
        rgrad_ref[...] = rgrad_in[...]
        dwgrad_ref[...] = dwgrad_in[...]
        rows_ref[...] = rows_in[...]

    low, bt, ct = read_packed(pack_ref, states)
    wide = bt.shape[1]
    dt = dt_ref[...]
    act = act_ref[...].astype(F32)
    u_s[...] = dt * act
    dtm_s[...] = jnp.where(offset_ref[...] == 0, FAR, dt)
    gate = gate_ref[...].astype(F32)
    sig = sigmoid(gate)
    gg = gg_ref[...].astype(F32) * sig
    gy = gg * gate
    gy_s[...] = gy
    ggate_ref[...] = (gg * y_ref[...] * (1.0 + gate * (1.0 - sig))).astype(BF16)
    rate = rate_ref[...]
    groups = chunk // STEP

    def group(k, held):
        carry, rgrad = held
        g = groups - 1 - k
        base = pl.multiple_of(g * STEP, STEP)
        cg = pltpu.roll(ct, wide - base, 1)
        dtm = dtm_s[pl.ds(base, STEP), :]
        dts = dt_ref[pl.ds(base, STEP), :]
        gys = gy_s[pl.ds(base, STEP), :]
        for j in reversed(range(STEP)):
            if j > 0:
                at = pl.multiple_of((base + j - 1) * states, states)
                prior = hist_ref[pl.ds(at, states), :].astype(F32)
            else:
                at = pl.multiple_of(jnp.maximum(base - 1, 0) * states, states)
                prior = jnp.where(base == 0, prior_ref[...], hist_ref[pl.ds(at, states), :]).astype(F32)
            a = jnp.exp(dtm[j:j + 1, :] * rate)
            adj = cg[:, j:j + 1] * gys[j:j + 1, :] + carry
            carry = a * adj
            through = carry * prior
            rgrad = rgrad + through * dts[j:j + 1, :]
            at = pl.multiple_of((base + j) * states, states)
            adj_s[pl.ds(at, states), :] = adj.astype(BF16)
            scaled = through * rate
            scaled = scaled[:states // 2] + scaled[states // 2:]
            if j % 2:
                later = scaled
            else:
                at = pl.multiple_of((base + j) * (states // 2), states)
                thr_s[pl.ds(at, states), :] = jnp.concatenate([scaled, later], axis=0).astype(BF16)
        return carry, rgrad

    carry, rgrad = lax.fori_loop(0, groups, group, (carry_s[...], rgrad_ref[...]))
    carry_s[...] = carry
    rgrad_ref[...] = rgrad
    spread = spread_columns(bt, chunk, states)
    width = SPAN * states
    ones = (
        lax.broadcasted_iota(jnp.int32, (2 * SPAN, width), 0)
        == lax.broadcasted_iota(jnp.int32, (2 * SPAN, width), 1) // (states // 2)
    ).astype(BF16)
    ub = u_s[...].astype(BF16)
    gyb = gy.astype(BF16)
    ahead = (lax.broadcasted_iota(jnp.int32, (width, chunk), 1)
             - lax.broadcasted_iota(jnp.int32, (width, chunk), 0) // states)
    gb_wide = mm(adj_s[...], ub, NT)
    gc_wide = mm(hist_ref[...], gyb, NT)
    gb_all = jnp.zeros((width, chunk), F32)
    gc_all = jnp.zeros((width, chunk), F32)
    for g in range(chunk // SPAN):
        rows = slice(g * SPAN, (g + 1) * SPAN)
        adj = adj_s[g * width:(g + 1) * width, :]
        drive_s[rows, :] = mm(spread[rows, :], adj)
        if g % 2 == 0:
            pair = slice(g * SPAN, (g + 2) * SPAN)
            decay_s[pair, :] = mm(ones, thr_s[g * width // 2:(g + 2) * width // 2, :])
        gb_all = jnp.where(ahead == g * SPAN, gb_wide[g * width:(g + 1) * width], gb_all)
        gc_all = jnp.where(ahead == g * SPAN, gc_wide[g * width:(g + 1) * width], gc_all)
    tiles = tile_matrix(states)
    wide_s[0:states, 0:chunk] = mm(tiles, gb_all.astype(BF16))
    wide_s[states:2 * states, 0:chunk] = mm(tiles, gc_all.astype(BF16))
    drive = drive_s[...]
    gact_ref[...] = drive * dt + gy * skip_ref[...]
    gpre = ((drive * act + decay_s[...]) * sp_ref[...]).astype(BF16)
    rows_ref[0:1, :] += jnp.sum(gy * act, axis=0, keepdims=True)
    rows_ref[1:2, :] += jnp.sum(gpre.astype(F32), axis=0, keepdims=True)
    dwgrad_ref[...] += mm(low, gpre, TN)
    write_packed(part_ref, mm(gpre, dw_ref[...], NT), wide_s)


def scan_backward(me, pack, dt, sp, act, projected, gg, y, offset, hist, delta_w, rate, skip, held, whole, last, steps):
    tokens, channels = act.shape
    states = rate.shape[0]
    chunk = ROWS[0]
    row = lambda i, me: (last - i, 0)
    second = lambda i, me: (last - i, 1)
    run = lambda i, me: ((last - i) ^ me[0], 0, 0)
    fixed = lambda i, me: (0, 0)
    blocks = [pl.BlockSpec((chunk, channels), second), pl.BlockSpec((chunk, channels), row), pl.BlockSpec((1,) + pack.shape[1:], run)]
    shapes = [
        pltpu.HBM((tokens, 2 * channels), BF16),
        pltpu.HBM((tokens, channels), F32),
        jax.ShapeDtypeStruct(pack.shape, BF16),
    ]
    sums = [pl.BlockSpec(v.shape, fixed) for v in held]
    done = steps * chunk
    return pl.pallas_call(
        functools.partial(backward_kernel, len(whole)),
        name="scan_backward",
        grid_spec=pltpu.PrefetchScalarGridSpec(
            num_scalar_prefetch=1,
            grid=(steps,),
            in_specs=[
                pl.BlockSpec((1,) + pack.shape[1:], run),
                pl.BlockSpec((chunk, channels), row),
                pl.BlockSpec((chunk, channels), row),
                pl.BlockSpec((chunk, channels), row),
                pl.BlockSpec((chunk, channels), second),
                pl.BlockSpec((chunk, channels), row),
                pl.BlockSpec((chunk, channels), row),
                pl.BlockSpec((chunk, 1), row),
                pl.BlockSpec((chunk * states, channels), row),
                pl.BlockSpec((states, channels), lambda i, me: (jnp.maximum((last - i) * chunk - 1, 0), 0)),
                pl.BlockSpec(delta_w.shape, fixed),
                pl.BlockSpec(rate.shape, fixed),
                pl.BlockSpec(skip.shape, fixed),
            ] + sums + [pl.BlockSpec(memory_space=pl.ANY)] * len(whole),
            out_specs=blocks + sums,
            scratch_shapes=[pltpu.VMEM((chunk, channels), F32)] * 5
            + [pltpu.VMEM((2 * states, 2 * LANES), F32)]
            + [pltpu.VMEM((chunk * states, channels), BF16), pltpu.VMEM((chunk * states // 2, channels), BF16)],
        ),
        out_shape=shapes + [jax.ShapeDtypeStruct(v.shape, F32) for v in held],
        input_output_aliases={18 + i: i for i in range(len(whole))},
        compiler_params=pltpu.CompilerParams(dimension_semantics=("arbitrary",), vmem_limit_bytes=40 << 20),
        cost_estimate=SMALL,
    )(me, pack, in_hbm(dt), in_hbm(sp), in_hbm(act), in_hbm(projected), in_hbm(gg), in_hbm(y), offset, in_hbm(hist), in_hbm(hist), delta_w, rate, skip, *held, *(in_hbm(v) if k == 1 else v for k, v in enumerate(whole)))


def end_kernel(me_ref, pack_ref, gact_ref, act_ref, inner_ref, prior_ref, offset_ref, taps_ref, shift_ref, low_ref, bc_ref, grad_ref,
               ginner_ref, tapg_ref, selow_ref, selbc_ref, ext_s, after_s, wide_s):
    rows, channels = inner_ref.shape
    taps = taps_ref.shape[0]
    states = bc_ref.shape[0] // 2

    @pl.when(pl.program_id(0) == 0)
    def _():
        after_s[...] = jnp.zeros_like(after_s)
        tapg_ref[...] = jnp.zeros_like(tapg_ref)
        selow_ref[...] = jnp.zeros_like(selow_ref)
        selbc_ref[...] = jnp.zeros_like(selbc_ref)

    low, gbt, gct = read_packed(pack_ref, states)
    wide_s[0:states, :] = gbt
    wide_s[states:2 * states, :] = gct
    gbc = wide_s[:, 0:rows].astype(BF16)
    act = act_ref[...]
    selow_ref[...] += mm(act, low, TN)
    selbc_ref[...] += mm(gbc, act)
    gact = gact_ref[...] + mm(low, low_ref[...], NT) + mm(gbc, bc_ref[...], TN)
    before = prior_ref.shape[0]
    ext_s[0:before, :] = prior_ref[...].astype(F32)
    ext_s[before:before + rows, :] = inner_ref[...].astype(F32)
    offset = offset_ref[...]
    conv = shift_ref[...] + taps_ref[0:1, :] * ext_s[before:before + rows, :]
    for k in range(1, taps):
        conv += jnp.where(offset >= k, taps_ref[k:k + 1, :], 0.0) * ext_s[pl.ds(before - k, rows), :]
    q = sigmoid(conv)
    gconv = gact * q * (1.0 + conv * (1.0 - q))
    tapg_ref[taps:taps + 1, :] += jnp.sum(gconv, axis=0, keepdims=True)
    tapg_ref[0:1, :] += jnp.sum(gconv * ext_s[before:before + rows, :], axis=0, keepdims=True)
    ginner = gconv * taps_ref[0:1, :]
    for k in range(1, taps):
        masked = jnp.where(offset >= k, gconv, 0.0)
        tapg_ref[k:k + 1, :] += jnp.sum(masked * ext_s[pl.ds(before - k, rows), :], axis=0, keepdims=True)
        after_s[k - 1, rows:rows + 8, :] = after_s[k - 1, 0:8, :]
        after_s[k - 1, 0:rows, :] = masked * taps_ref[k:k + 1, :]
        ginner += after_s[k - 1, pl.ds(k, rows), :]
    ginner_ref[...] = ginner.astype(BF16)


def end(me, pack, gact, act, projected, offset, taps, shift, low_w, bc_w, grad_projected):
    tokens, channels = act.shape
    rows = ROWS[0]
    steps = tokens // rows
    row = lambda i, me: (steps - 1 - i, 0)
    fixed = lambda i, me: (0, 0)
    return pl.pallas_call(
        end_kernel,
        name="end",
        grid_spec=pltpu.PrefetchScalarGridSpec(
            num_scalar_prefetch=1,
            grid=(steps,),
            in_specs=[
                pl.BlockSpec((1,) + pack.shape[1:], lambda i, me: ((steps - 1 - i) ^ me[0], 0, 0)),
                pl.BlockSpec((rows, channels), row),
                pl.BlockSpec((rows, channels), row),
                pl.BlockSpec((rows, channels), row),
                pl.BlockSpec((16, channels), lambda i, me: (jnp.maximum((steps - 1 - i) * (rows // 16) - 1, 0), 0)),
                pl.BlockSpec((rows, 1), row),
                pl.BlockSpec(taps.shape, fixed),
                pl.BlockSpec(shift.shape, fixed),
                pl.BlockSpec(low_w.shape, fixed),
                pl.BlockSpec(bc_w.shape, fixed),
                pl.BlockSpec(memory_space=pl.ANY),
            ],
            out_specs=[
                pl.BlockSpec((rows, channels), row),
                pl.BlockSpec((8, channels), fixed),
                pl.BlockSpec(low_w.shape, fixed),
                pl.BlockSpec(bc_w.shape, fixed),
            ],
            scratch_shapes=[
                pltpu.VMEM((rows + 16, channels), F32),
                pltpu.VMEM((3, rows + 8, channels), F32),
                pltpu.VMEM((bc_w.shape[0], 2 * LANES), F32),
            ],
        ),
        out_shape=[
            pltpu.HBM(grad_projected.shape, BF16),
            jax.ShapeDtypeStruct((8, channels), F32),
            jax.ShapeDtypeStruct(low_w.shape, F32),
            jax.ShapeDtypeStruct(bc_w.shape, F32),
        ],
        input_output_aliases={11: 0},
        compiler_params=pltpu.CompilerParams(dimension_semantics=("arbitrary",), vmem_limit_bytes=14 << 20),
        cost_estimate=SMALL,
    )(me, pack, in_hbm(gact), in_hbm(act), in_hbm(projected), in_hbm(projected), offset, taps, shift, low_w, bc_w, in_hbm(grad_projected))


def weight_grad_kernel(count, turned, table_ref, *refs):
    a_refs, b_refs = refs[:count], refs[count:2 * count]
    out_ref, a_s, b_s = refs[-3:]
    rows = a_refs[0].shape[0]
    for s in range(count):
        a_s[s * rows:(s + 1) * rows, :] = a_refs[s][...]

    @pl.when(pl.program_id(0) == 0)
    def _():
        for s in range(count):
            b_s[s * rows:(s + 1) * rows, :] = b_refs[s][...]

    first, second = (b_s, a_s) if turned else (a_s, b_s)
    out_ref[0] = mm(first[...], second[...], TN).astype(BF16)


def weight_grad(table, distances, shards, b, column, channels, size, turned, slots=1, slot=0, into=()):
    rows, width = shards[0].shape
    block = width // size
    count = len(shards)
    shape = (1, channels, block) if turned else (1, block, channels)
    if distances is None:
        b_specs = [pl.BlockSpec((rows, channels), lambda i, table: (0, column))]
    else:
        b_specs = [pl.BlockSpec((rows, channels), lambda i, table, d=d: (table[d], column)) for d in distances]
    return pl.pallas_call(
        functools.partial(weight_grad_kernel, count, turned),
        name="weight_grad",
        grid_spec=pltpu.PrefetchScalarGridSpec(
            num_scalar_prefetch=1,
            grid=(size,),
            in_specs=[pl.BlockSpec((rows, block), lambda i, table: (0, i))] * count
            + b_specs + [pl.BlockSpec(memory_space=pl.ANY)] * len(into),
            out_specs=pl.BlockSpec(shape, lambda i, table: (i, slot, 0)),
            scratch_shapes=[pltpu.VMEM((rows * count, block), BF16), pltpu.VMEM((rows * count, channels), BF16)],
        ),
        out_shape=pltpu.HBM((size, slots * shape[1], shape[2]), BF16),
        input_output_aliases={1 + 2 * count + k: k for k in range(len(into))},
        compiler_params=pltpu.CompilerParams(dimension_semantics=("arbitrary",), vmem_limit_bytes=16 << 20),
        cost_estimate=SMALL,
    )(table, *(in_hbm(v) for v in shards), *([in_hbm(b)] * count), *(in_hbm(v) for v in into))


def weight_block(weight, dims, blocks):
    if dims[0][1] == (0,):
        columns = weight.shape[1] // blocks
        return pl.BlockSpec((weight.shape[0], columns), lambda i, *rest: (0, i)), columns
    columns = weight.shape[0] // blocks
    return pl.BlockSpec((columns, weight.shape[1]), lambda i, *rest: (i, 0)), columns


def placed_kernel(dims, count, table_ref, *refs):
    w_ref, out_ref = refs[count], refs[-1]
    for s in range(count):
        @pl.when(pl.program_id(1) == s)
        def _(s=s):
            out_ref[...] = mm(refs[s][...], w_ref[...], dims).astype(out_ref.dtype)


def pick_entry(values, i):
    chosen = values[0]
    for k in range(1, len(values)):
        chosen = jnp.where(i == k, values[k], chosen)
    return chosen


def placed_product(table, distances, shards, weight, dims, out):
    rows, width = shards[0].shape
    count, blocks = len(shards), 2
    spec, columns = weight_block(weight, dims, blocks)
    return pl.pallas_call(
        functools.partial(placed_kernel, dims, count),
        name="placed_product",
        grid_spec=pltpu.PrefetchScalarGridSpec(
            num_scalar_prefetch=1,
            grid=(blocks, count),
            in_specs=[pl.BlockSpec((rows, width), lambda i, k, table: (0, 0))] * count
            + [spec, pl.BlockSpec(memory_space=pl.ANY)],
            out_specs=pl.BlockSpec((rows, columns), lambda i, k, table: (pick_entry([table[d] for d in distances], k), i)),
        ),
        out_shape=pltpu.HBM(out.shape, out.dtype),
        input_output_aliases={count + 2: 0},
        compiler_params=pltpu.CompilerParams(dimension_semantics=("arbitrary", "arbitrary"), vmem_limit_bytes=16 << 20),
        cost_estimate=SMALL,
    )(table, *(in_hbm(v) for v in shards), in_hbm(weight), in_hbm(out))


def placed_halves_kernel(cuts, table_ref, first_ref, second_ref, *refs):
    w_refs, out_ref = refs[:cuts], refs[-1]
    depth = w_refs[0].shape[0]
    each = first_ref.shape[1] // depth
    total = None
    for c in range(cuts):
        ref, at = (first_ref, c) if c < each else (second_ref, c - each)
        term = mm(ref[:, at * depth:(at + 1) * depth], w_refs[c][...])
        total = term if total is None else total + term
    out_ref[...] = total.astype(out_ref.dtype)


def placed_halves(table, distance, first, second, weight, out):
    rows, middle = first.shape
    cuts = 8
    depth, width = weight.shape[0] // cuts, weight.shape[1]
    return pl.pallas_call(
        functools.partial(placed_halves_kernel, cuts),
        name="placed_halves",
        grid_spec=pltpu.PrefetchScalarGridSpec(
            num_scalar_prefetch=1,
            grid=(1,),
            in_specs=[pl.BlockSpec((rows, middle), lambda i, table: (0, 0))] * 2
            + [pl.BlockSpec((depth, width), lambda i, table, c=c: (c, 0)) for c in range(cuts)]
            + [pl.BlockSpec(memory_space=pl.ANY)],
            out_specs=pl.BlockSpec((rows, width), lambda i, table: (table[distance], 0)),
        ),
        out_shape=pltpu.HBM(out.shape, out.dtype),
        input_output_aliases={3 + cuts: 0},
        compiler_params=pltpu.CompilerParams(dimension_semantics=("arbitrary",), vmem_limit_bytes=16 << 20),
        cost_estimate=SMALL,
    )(table, in_hbm(first), in_hbm(second), *([in_hbm(weight)] * cuts), in_hbm(out))


def in_hbm(value):
    return pltpu.with_memory_space_constraint(value, pltpu.HBM)


def far_kernel(cuts, table_ref, g_ref, t_ref, *refs):
    w_refs, (ahead_ref, behind_ref) = refs[:cuts], refs[cuts:]
    columns = w_refs[0].shape[0]
    for ref, first in ((ahead_ref, True), (behind_ref, False)):
        @pl.when((pl.program_id(0) == 0) == first)
        def _(ref=ref):
            for c in range(cuts):
                at = slice(c * columns, (c + 1) * columns)
                ref[:, at] = (mm(g_ref[...], w_refs[c][...], NT) + t_ref[:, at].astype(F32)).astype(BF16)


def pair_kernel(cuts, table_ref, ga_ref, gb_ref, ta_ref, tb_ref, *refs, halves=False):
    w_refs, (ra_ref, rb_ref, ahead_ref, behind_ref) = refs[:cuts], refs[cuts:]
    rows, columns = ga_ref.shape[0], w_refs[0].shape[0]
    both = jnp.concatenate([ga_ref[...], gb_ref[...]], axis=0)
    low = pl.program_id(0) == 0
    for c in range(cuts):
        at = slice(c * columns, (c + 1) * columns)
        total = mm(both, w_refs[c][...], NT)
        ra, rb = ra_ref[:, at].astype(F32), rb_ref[:, at].astype(F32)
        if halves:
            ra, rb = jnp.where(low, ra, 0.0), jnp.where(low, 0.0, rb)
        ahead_ref[:, at] = (total[:rows] + ta_ref[:, at].astype(F32) + ra).astype(BF16)
        behind_ref[:, at] = (total[rows:] + tb_ref[:, at].astype(F32) + rb).astype(BF16)


def own_kernel(cuts, table_ref, g_ref, t_ref, *refs):
    w_refs, (ra_ref, rb_ref, place_ref), outs = refs[:cuts], refs[cuts:cuts + 3], refs[cuts + 3:]
    columns = w_refs[0].shape[0]
    pair = outs[0].shape[0]
    for c in range(cuts):
        at = slice(c * columns, (c + 1) * columns)
        total = mm(g_ref[...], w_refs[c][...], NT) + t_ref[:, at].astype(F32)
        total = (total + ra_ref[:, at].astype(F32) + rb_ref[:, at].astype(F32)).astype(BF16)
        for d, out_ref in enumerate(outs):
            out_ref[:, at] = mm(place_ref[d * pair:(d + 1) * pair, :], total).astype(BF16)


def ring_step(kernel, table, distances, grads, terms, weight, arrived=(), place=None, pieces=1):
    rows, cuts = ROWS[0], 4
    width, channels = weight.shape[0], weight.shape[1] // 2
    half, columns = width // 2, width // (2 * cuts)
    fixed = lambda i, table: (0, 0)
    side = lambda i, table: (0, i)
    far = not arrived
    if far:
        outs, shape = [fixed, fixed], (rows, half)
    else:
        outs, shape = [side, side] if place is None else [side] * pieces, (rows // pieces, width)
    small = not far and arrived[0].shape[1] == half
    extra = [] if place is None else [place]
    return pl.pallas_call(
        functools.partial(kernel, cuts, halves=True) if small else functools.partial(kernel, cuts),
        name=kernel.__name__,
        grid_spec=pltpu.PrefetchScalarGridSpec(
            num_scalar_prefetch=1,
            grid=(2,),
            in_specs=[pl.BlockSpec((rows, channels), lambda i, table, d=d: (table[d], 0)) for d in distances]
            + [pl.BlockSpec((rows, half), lambda i, table, d=d: (table[d], i)) for d in distances]
            + [pl.BlockSpec((columns, channels), lambda i, table, c=c: (i * cuts + c, 0)) for c in range(cuts)]
            + [pl.BlockSpec((rows, half), fixed if small else side) for v in arrived]
            + [pl.BlockSpec(v.shape, fixed) for v in extra],
            out_specs=[pl.BlockSpec((shape[0], half), m) for m in outs],
        ),
        out_shape=[pltpu.HBM(shape, BF16) for m in outs],
        compiler_params=pltpu.CompilerParams(dimension_semantics=("arbitrary",), vmem_limit_bytes=24 << 20),
        cost_estimate=SMALL,
    )(table, *([in_hbm(grads)] * len(distances)), *([in_hbm(terms)] * len(distances)), *([in_hbm(weight)] * cuts),
      *(in_hbm(v) for v in arrived), *extra)


def blank(*shapes):
    hbm = pl.BlockSpec(memory_space=pl.ANY)
    return pl.pallas_call(
        lambda *refs: None, name="blank", out_specs=[hbm] * len(shapes),
        out_shape=[pltpu.HBM(*v) for v in shapes],
        cost_estimate=SMALL)()


def deal_kernel(x_ref, cot_ref, order_ref, gain_ref, me_ref, pick_ref, place_ref, *sends):
    rows = x_ref.shape[0]
    dp_size = order_ref.shape[0]
    me = me_ref[0]
    group_tokens = me_ref[1]
    pair = rows // dp_size
    order = order_ref[...].astype(jnp.int32)
    near = lax.broadcasted_iota(jnp.int32, (dp_size, rows), 0)
    other = near ^ me
    source = order // group_tokens
    local = order % rows
    before = (
        lax.broadcasted_iota(jnp.int32, (rows, rows), 0) < lax.broadcasted_iota(jnp.int32, (rows, rows), 1)
    ).astype(BF16)
    slots = lax.broadcasted_iota(jnp.int32, (rows, rows), 0)
    chosen = source == me
    rank = mm(chosen.astype(BF16), before).astype(jnp.int32)
    slot = jnp.where(chosen, near * pair + rank, -1)
    pick = jnp.zeros((rows, rows), F32)
    for d in range(dp_size):
        pick += mm((slots == slot[d:d + 1, :]).astype(BF16), (slots == local[d:d + 1, :]).astype(BF16), NT)
    pick = pick.astype(BF16)
    pick_ref[...] = pick
    mine = source[0:1, :]
    held = (mine == other).astype(BF16)
    ranks = mm(held, before).astype(jnp.int32)
    arrived = jnp.sum(jnp.where(mine == other, near * pair + ranks, 0), axis=0, keepdims=True)
    place_ref[...] = (slots == arrived).astype(BF16)
    x = x_ref[...].astype(F32)
    rinv = lax.rsqrt(jnp.mean(x * x, axis=1, keepdims=True) + EPSILON)
    normed = (x * rinv * gain_ref[...]).astype(BF16)
    for d in range(dp_size):
        at = slice(d * pair, (d + 1) * pair)
        sends[d][...] = mm(pick[at], normed).astype(BF16)
        sends[dp_size + d][...] = mm(pick[at], cot_ref[...]).astype(BF16)


def deal(x, cot, order, gain, me):
    rows, width = x.shape
    dp_size = order.shape[0]
    vm = pl.BlockSpec(memory_space=pltpu.VMEM)
    pick, place, *sends = pl.pallas_call(
        deal_kernel,
        name="deal",
        in_specs=[vm, vm, vm, vm, pl.BlockSpec(memory_space=pltpu.SMEM)],
        out_specs=[vm] * (2 + 2 * dp_size),
        out_shape=[jax.ShapeDtypeStruct((rows, rows), BF16)] * 2
        + [jax.ShapeDtypeStruct((rows // dp_size, width), BF16)] * (2 * dp_size),
        compiler_params=pltpu.CompilerParams(vmem_limit_bytes=32 << 20),
        cost_estimate=SMALL,
    )(x, cot, order, gain, me)
    return sends[:dp_size], sends[dp_size:], pick, place


def round_dot(a, b, dims=(((1,), (0,)), ((), ()))):
    return mm(a, b, dims).astype(BF16)


def after(value, *earlier):
    return lax.optimization_barrier((value,) + earlier)[0]


def flip(value, axis, bit):
    return lax.ppermute(value, axis, [(i, i ^ bit) for i in range(lax.axis_size(axis))])


def exchange(pieces, axis, stack=True):
    pieces = [pieces[0]] + [flip(pieces[d], axis, d) for d in range(1, lax.axis_size(axis))]
    return jnp.stack(pieces) if stack else pieces


def swap(values, axis):
    return lax.all_to_all(values, axis, split_axis=0, concat_axis=0, tiled=True)


def share(value, axis):
    return exchange([value] * lax.axis_size(axis), axis)


def in_order(pieces, axis):
    size, me, bit = lax.axis_size(axis), lax.axis_index(axis), 1
    while bit < size:
        split = pieces.reshape((size // (2 * bit), 2, bit) + pieces.shape[1:])
        turned = jnp.concatenate([split[:, 1:], split[:, :1]], axis=1)
        pieces = jnp.where((me // bit) % 2 == 1, turned, split).reshape(pieces.shape)
        bit *= 2
    return pieces


def cube_sum(value, axis, bit, end_bit):
    while bit < end_bit:
        value = value + flip(value, axis, bit)
        bit *= 2
    return value


class Bag(dict):
    def meet(self, values, *names):
        values, held = lax.optimization_barrier((values, {n: self[n] for n in names}))
        self.update(held)
        return values


def add_up(pieces):
    return jnp.sum(pieces.astype(F32), axis=0)


class Ring:
    def __init__(self, axis):
        self.axis = axis
        self.size = size = lax.axis_size(axis)
        columns = max(c for c in range(1, size) if size % c == 0 and c * c <= size)
        rows = size // columns
        cycle = [(0, c) for c in range(columns)]
        for r in range(1, rows):
            snake = range(1, columns)
            cycle += [(r, c) for c in (snake if r % 2 == 0 else reversed(snake))]
        cycle += [(r, 0) for r in reversed(range(1, rows))]
        order = [r * columns + c for r, c in cycle]
        place = {t: i for i, t in enumerate(order)}
        table = jnp.array([[order[(place[t] + d) % size] for d in range(size)] for t in range(size)], jnp.int32)
        self.at = lax.dynamic_index_in_dim(table, lax.axis_index(axis), 0, keepdims=False)
        self.forward = [(order[i], order[(i + 1) % size]) for i in range(size)]
        self.backward = [(b, a) for a, b in self.forward]

    def hop(self, value, ahead):
        return lax.ppermute(value, self.axis, self.forward if ahead else self.backward)


def ring_gather(ring, own, between):
    half, size = ring.size // 2, ring.size
    middle = own.shape[1] // 2
    distances, shards = [0], [own]
    ahead = behind = own
    for d in range(1, half):
        ahead, behind = between(d, ring.hop(ahead, True), ring.hop(behind, False))
        distances += [size - d, d]
        shards += [ahead, behind]
    halves = between(half, ring.hop(ahead[:, :middle], True), ring.hop(behind[:, middle:], False))
    return distances + [half], shards, halves


def ring_reduce(ring, grads, terms, weight, place, pieces, between):
    half, size = ring.size // 2, ring.size
    step = functools.partial(ring_step, table=ring.at, grads=grads, terms=terms, weight=weight)
    ahead, behind = step(far_kernel, distances=[half])
    for d in range(half, 0, -1):
        ahead, behind = between(half - d, ahead, ring.hop(ahead, True), ring.hop(behind, False))
        if d > 1:
            ahead, behind = step(pair_kernel, distances=[d - 1, size + 1 - d], arrived=[ahead, behind])
    return step(own_kernel, distances=[0], arrived=[ahead, behind], place=place, pieces=pieces)


def shards(
    block_input, norm_gain, in_weight, conv_weight, conv_bias, select_weight, delta_weight, delta_bias,
    decay_log, skip_weight, out_weight, out_cotangent, seq_lengths, deal_order,
):
    rows_dev, width = block_input.shape
    dp_size = lax.axis_size("dp")
    tensor_size = lax.axis_size("tensor")
    pair = rows_dev // dp_size
    group_tokens = rows_dev * tensor_size
    ring = Ring("tensor")
    here = jnp.zeros((1,), jnp.int32)
    me = jnp.stack([lax.axis_index("dp"), jnp.int32(group_tokens)]).astype(jnp.int32)
    head = share(jnp.concatenate([deal_order.astype(F32), norm_gain.astype(F32)]), "dp")
    gain_values = in_order(head[:, rows_dev:], "dp").reshape(1, -1)
    send_rows, send_cot, pick, place = deal(block_input, out_cotangent, head[:, :rows_dev], gain_values, me)
    in_cat = jnp.swapaxes(after(in_weight, send_rows[0]), 0, 1).reshape(in_weight.shape[1], -1)
    recv_rows = exchange(send_rows, "dp")
    recv_rows, in_cat = lax.optimization_barrier((recv_rows, in_cat))
    in_full = lax.all_gather(in_cat, "dp", axis=0, tiled=True)
    normed = round_dot(place, recv_rows.reshape(rows_dev, -1), TN)
    channels = in_full.shape[1] // 2
    taps = conv_weight.shape[0]
    lane_width = conv_bias.shape[1] * dp_size
    own_states = decay_log.shape[1]
    states, low_rank = own_states * dp_size, delta_weight.shape[0] * dp_size
    lengths_row = seq_lengths[0]
    seq_ends = jnp.cumsum(lengths_row)
    begins = seq_ends - lengths_row
    positions = jnp.arange(group_tokens, dtype=jnp.int32)
    inside = (positions[:, None] >= begins[None, :]) & (positions[:, None] < seq_ends[None, :])
    offset = (positions - jnp.sum(jnp.where(inside, begins[None, :], 0), axis=1))[:, None]
    (projected,) = blank(((group_tokens, 2 * channels), BF16))
    half = tensor_size // 2
    NN = (((1,), (0,)), ((), ()))
    lanes_own = jnp.concatenate([conv_weight, jnp.stack([conv_bias, delta_bias, skip_weight])])
    bag = Bag(
        cot=send_cot, select=jnp.concatenate([select_weight, jnp.moveaxis(lanes_own, 0, 2)], axis=2),
        thin=jnp.concatenate([decay_log.T, delta_weight]), projected=projected)
    waiting = {"shards": [normed], "distances": [0]}

    def during_normed(d, ahead, behind):
        if d == 1:
            ahead, behind = bag.meet((ahead, behind), "select")
            bag["select"] = share(bag["select"], "dp")
            bag["own"] = out_weight
        elif d < half - 1:
            ahead, behind = bag.meet((ahead, behind), "own", "select", "cot")
            if d == 2:
                bag["cot"] = exchange(bag["cot"], "dp")
        elif d >= half - 1:
            bag["projected"] = placed_product(
                ring.at, waiting["distances"], waiting["shards"], in_full, NN, bag["projected"])
            waiting["shards"], waiting["distances"] = [], []
            ahead, behind = bag.meet((ahead, behind), "projected", *(["cot"] if d == half else []))
        if d < half:
            waiting["distances"] += [tensor_size - d, d]
            waiting["shards"] += [ahead, behind]
        return ahead, behind

    distances, normed_shards, halves = ring_gather(ring, normed, during_normed)

    def rows_of(values, distance):
        return lax.dynamic_slice(values, (ring.at[distance] * rows_dev, 0), (rows_dev, values.shape[1]))

    projected = placed_halves(ring.at, distances[-1], *halves, in_full, bag["projected"])
    dealt_cot = round_dot(place, bag["cot"].reshape(rows_dev, -1), TN)
    select_matrix = jnp.moveaxis(in_order(bag["select"], "dp"), 0, 1).reshape(channels, -1)
    low_w, bc_w = select_matrix[:, :low_rank], select_matrix[:, low_rank:low_rank + 2 * states].T
    lanes_float = select_matrix[:, low_rank + 2 * states:].astype(F32).T
    conv_taps = lanes_float[:taps]
    conv_shift, delta_shift, skip_values = (lanes_float[taps + i:taps + i + 1] for i in range(3))
    activated, part = front(here, projected, offset, conv_taps, conv_shift, low_w, bc_w)
    out_full = lax.all_gather(bag["own"], "dp", axis=1, tiled=True)
    group_cot = lax.all_gather(after(dealt_cot, halves[0]), "tensor", axis=0, tiled=True)
    bag["thin"] = lax.all_gather(after(bag["thin"], part)[None], "dp", axis=0, tiled=True)
    bag["last"] = jnp.concatenate([after(v, part) for v in halves], axis=1)
    arrived = bag.meet(swap(part, "tensor"), "thin", "last")
    normed_shards = normed_shards + [bag["last"]]
    decay_full = bag["thin"][:, :own_states].reshape(states, channels)
    delta_full = bag["thin"][:, own_states:].reshape(low_rank, channels)
    decay_rate = -jnp.exp(decay_full.astype(F32))
    total = jnp.sum(arrived.astype(F32), axis=0).astype(BF16)
    pack_all = swap(jnp.broadcast_to(total[None], part.shape), "tensor")
    step_size, slope, y, gated, hist, unused_state = scan_forward(
        here, pack_all, activated, projected, offset, delta_full, delta_shift, decay_rate, skip_values,
        jnp.zeros((states, channels), F32), [], 0, tensor_size)
    gg = mm(group_cot, out_full, NT)
    held = [
        jnp.zeros((states, channels), F32),
        jnp.zeros((states, channels), F32),
        jnp.zeros((low_rank, channels), F32),
        jnp.zeros((8, channels), F32),
    ]
    mixed = lax.psum_scatter(round_dot(gated, out_full), "tensor", scatter_dimension=0, tiled=True)
    grad_projected, grad_act, grad_part, unused_carry, rate_grad, delta_weight_grad, row_grads = scan_backward(
        here, pack_all, step_size, slope, activated, projected, gg, y, offset, hist, delta_full, decay_rate, skip_values,
        held, [], tensor_size - 1, tensor_size)
    decay_grad = rate_grad * decay_rate
    def by_lane(values):
        lanes = values.reshape(-1, channels // lane_width, dp_size, lane_width // dp_size)
        return jnp.moveaxis(lanes, 2, 0).reshape(dp_size, -1)

    def pack_scan(row_grads, decay_grad, delta_weight_grad):
        parts = [by_lane(row_grads[:2]), decay_grad.reshape(dp_size, -1), delta_weight_grad.reshape(dp_size, -1)]
        return jnp.concatenate(parts, axis=1).astype(BF16), [part.shape[1] for part in parts]

    def pack_conv(packed, taps_sum, low_sum, bc_sum):
        select_grad = jnp.concatenate([low_sum, bc_sum.T], axis=1)
        parts = [
            packed,
            by_lane(taps_sum[:taps + 1]).astype(BF16),
            jnp.moveaxis(select_grad.reshape(channels // lane_width, dp_size, -1), 1, 0).reshape(dp_size, -1).astype(BF16),
        ]
        flat = jnp.concatenate(parts, axis=1)
        flat = jnp.pad(flat, ((0, 0), (0, -flat.shape[1] % 2048))).reshape(dp_size, -1, LANES)
        return flat, [part.shape[1] for part in parts[1:]]

    merged = channels == width // dp_size
    bag["out"] = weight_grad(
        ring.at, None, [group_cot], after(gated, grad_part), 0, channels, dp_size, True, 2 if merged else 1)
    arrived = bag.meet(swap(grad_part, "tensor"), "out")
    grad_total = jnp.sum(arrived.astype(F32), axis=0).astype(BF16)
    bag["gate"] = weight_grad(
        ring.at, distances, normed_shards, after(grad_projected, grad_total), 1, channels, dp_size, False,
        *((2, 1, [bag["out"]]) if merged else ()))
    bag["packed"], sizes = pack_scan(*(after(v, grad_total) for v in (row_grads, decay_grad, delta_weight_grad)))
    bag["terms"] = round_dot(after(grad_projected, grad_total)[:, channels:], in_full[:, channels:], NT)
    grad_pack = bag.meet(swap(jnp.broadcast_to(grad_total[None], grad_part.shape), "tensor"), "gate", "terms", "packed")
    gate_terms = bag["terms"]
    bag["gate"] = lax.psum_scatter(bag["gate"], "dp", scatter_dimension=0, tiled=True)
    if not merged:
        bag["out"] = lax.psum_scatter(bag["out"], "dp", scatter_dimension=0, tiled=True)
    grad_projected, *sums = end(
        here, grad_pack, grad_act, activated, projected, offset, conv_taps, conv_shift, low_w, bc_w, grad_projected)
    bag["sums"] = [bag["packed"], *sums]
    bag["mixed"] = mixed

    def during_grad(k, sent, ahead, behind):
        names = []
        if k == 0:
            bag["grads"] = grad_projected
            names = ["sums", "grads"]
        if k == 1:
            bag["inner"] = weight_grad(
                ring.at, distances, normed_shards, after(bag["grads"], sent), 0, channels, dp_size, False)
            names = ["sums", "inner"]
        if k == half - 2:
            flat, more = pack_conv(*after(tuple(bag["sums"]), sent))
            sizes.extend(more)
            bag["flat"] = swap(flat, "dp")
            names = ["mixed", "flat", "gate"] + ([] if merged else ["out"])
        ahead, behind = bag.meet((ahead, behind), *names)
        if k == half - 2:
            bag["mixed"] = exchange(round_dot(place, bag["mixed"]).reshape(dp_size, pair, -1), "dp")
        if k == 1:
            bag["inner"] = lax.psum_scatter(bag["inner"], "dp", scatter_dimension=0, tiled=True)
        return ahead, behind

    send_grad = ring_reduce(ring, grad_projected, gate_terms, in_full, place, dp_size, during_grad)
    home_grad = exchange(send_grad, "dp").reshape(rows_dev, -1)
    home_out = bag["mixed"].reshape(rows_dev, -1)
    out_grad = (bag["gate"][0, :channels] if merged else bag["out"][0]).astype(F32)
    gate_grad = bag["gate"][:, channels:] if merged else bag["gate"]
    inner_grad = after(bag["inner"], send_grad[0])
    bag["in"] = jnp.concatenate([inner_grad, gate_grad]).astype(F32)
    gain_part = jnp.sum(in_weight.astype(F32) * bag["in"], axis=(0, 2))
    in_weight_grad = bag["in"]
    gain_parts = swap(jnp.broadcast_to(gain_part.reshape(1, -1, LANES), (tensor_size, gain_part.size // LANES, LANES)), "tensor")
    gain_grad = add_up(gain_parts).reshape(-1) / norm_gain.astype(F32)
    flat = jnp.sum(bag["flat"].astype(F32), axis=0).reshape(-1)
    small, start = [], 0
    for size in sizes:
        small.append(flat[start:start + size])
        start += size
    scan_grads = small[0].reshape((2,) + conv_bias.shape)
    lane_grads = small[3].reshape((taps + 1,) + conv_bias.shape)
    rows_float = block_input.astype(F32)
    block_output = (rows_float + mm(pick, home_out, TN)).astype(BF16)
    inverse_rms = lax.rsqrt(jnp.mean(rows_float * rows_float, axis=1, keepdims=True) + EPSILON)
    unit_rows = rows_float * inverse_rms
    scaled = mm(pick, home_grad, TN) * gain_values
    input_grad = (
        out_cotangent.astype(F32)
        + inverse_rms * (scaled - unit_rows * jnp.mean(scaled * unit_rows, axis=1, keepdims=True))
    ).astype(BF16)
    return (
        block_output,
        input_grad,
        gain_grad,
        in_weight_grad,
        lane_grads[:taps],
        lane_grads[taps],
        small[4].reshape(select_weight.shape),
        small[2].reshape(delta_weight.shape),
        scan_grads[1],
        small[1].reshape(decay_log.shape[1], decay_log.shape[0]).T,
        scan_grads[0],
        out_grad,
    )


def solution(mesh):
    return jax.shard_map(
        shards,
        mesh=mesh,
        in_specs=(
            P(("dp", "tensor"), None),
            P("dp"),
            P(None, "dp", "tensor"),
            P(None, "tensor", "dp"),
            P("tensor", "dp"),
            P("tensor", "dp", None),
            P("dp", "tensor"),
            P("tensor", "dp"),
            P("tensor", "dp"),
            P("tensor", "dp"),
            P("tensor", "dp"),
            P(("dp", "tensor"), None),
            P("dp", None),
            P(("dp", "tensor")),
        ),
        out_specs=(
            P(("dp", "tensor"), None),
            P(("dp", "tensor"), None),
            P("dp"),
            P(None, "dp", "tensor"),
            P(None, "tensor", "dp"),
            P("tensor", "dp"),
            P("tensor", "dp", None),
            P("dp", "tensor"),
            P("tensor", "dp"),
            P("tensor", "dp"),
            P("tensor", "dp"),
            P("tensor", "dp"),
        ),
        check_vma=False,
    )
```
